32 devices in a mesh: dom: 16 (over z, y, x), blk: 2 (over core).
Axes of the slice: x: 2, y: 2, z: 4, core: 2. Of those that a mesh axis runs over, the one named last changes fastest.
Arguments:
- self_block: float32 [96, 96, 4096], P(None, None, ('dom', 'blk')), may hold values from -1 to 8
- couple: float32 [64, 96, 4096], P(None, None, ('dom', 'blk')), may hold values from -0.625 to 0.625
- inverse: float32 [64, 64, 4096], P(None, None, ('dom', 'blk')), may hold values from -1 to 8
- body_force: float32 [3, 64, 4096], P(None, None, ('dom', 'blk')), may hold values from -6 to 6
- face_mortar: int32 [24576], P(('dom', 'blk')), may hold values from 0 to 8191, as said below
- face_kind: int32 [24576], P(('dom', 'blk')), may hold values from 0 to 4
Outputs:
- trace_field: float32 [48, 8192], P(None, ('dom', 'blk'))
- interior: float32 [3, 64, 4096], P(None, None, ('dom', 'blk'))
The draws below stay inside these ranges and needn't reach their ends.
Inputs may be any that keep to these rules, and one draw needn't show every extreme that they name: `face_mortar`: mortar m is owned by device m // 256 along the curve. The 768 slots of device r come in five runs in this order: mortars owned by r - 2, r - 1, r, r + 1, r + 32 // 2 (modulo 32); each of the four other runs holds 1 to 32 slots and one of them holds exactly 32; the first 256 slots of the run owned by r name each of r's mortars once.
All inputs are finite; a program needn't handle non-finite values.
Results may differ from the reference program's by a relative error of at most 0.0003.
Values sent between devices are 32-bit elements; how exact they have to be, the bound alone decides.
No kernel may reach another device: no remote copies, remote signals or barrier semaphores. Data moves between devices by JAX's collectives and lax.ppermute only.
A program may use at most 128 MiB of HBM per device.

```python
import jax
import jax.numpy as jnp
import numpy as np
from jax import lax

INNER = 64
COMP = 3
TRACE = 96
E_DEV = 128
CAP = 32
M_DEV = 256
ITERS = 3
RANKS = 32
ELEMS = 4096
MORTARS = 8192
SLOTS = 24576


def dominant(key, dimension):
    key_entries, key_diagonal, key_scale = jax.random.split(key, 3)
    entries = jax.random.uniform(key_entries, (dimension, dimension, ELEMS), jnp.float32, -1.0, 1.0)
    symmetric = (entries + jnp.transpose(entries, (1, 0, 2))) * (0.5 / dimension)
    identity = jnp.eye(dimension, dtype=jnp.float32)[:, :, None]
    diagonal = jax.random.uniform(key_diagonal, (dimension, 1, ELEMS), jnp.float32, 1.2, 2.0)
    spread_log = jax.random.uniform(key_scale, (ELEMS,), jnp.float32, jnp.log(0.5), jnp.log(2.0))
    block = symmetric * (1.0 - identity) + identity * diagonal
    return block * jnp.exp(spread_log)[None, None, :]


def draw_self_block(key, part):
    return dominant(key, TRACE)


def draw_inverse(key, part):
    return dominant(key, INNER)


def draw_face_mortar(key, part):
    key_counts, key_full, key_local, key_cover = jax.random.split(key, 4)
    slot_count = 6 * E_DEV
    lowest = max(1, CAP // 2)
    counts = jax.random.randint(key_counts, (RANKS, 4), lowest, CAP + 1)
    chosen = jax.random.randint(key_full, (RANKS, 1), 0, 4)
    counts = jnp.where(jnp.arange(4)[None, :] == chosen, CAP, counts)
    places = jnp.arange(slot_count)[None, :]
    first_end = counts[:, 0:1]
    second_end = first_end + counts[:, 1:2]
    fourth_end = slot_count - counts[:, 3:4]
    third_end = fourth_end - counts[:, 2:3]
    offsets = jnp.where(places < first_end, -2, jnp.where(places < second_end, -1, jnp.where(places < third_end, 0, jnp.where(places < fourth_end, 1, RANKS // 2))))
    owners = (jnp.arange(RANKS)[:, None] + offsets) % RANKS
    scattered = jax.random.randint(key_local, (RANKS, slot_count), 0, M_DEV)
    covering = jax.vmap(lambda single: jax.random.permutation(single, M_DEV))(jax.random.split(key_cover, RANKS))
    self_place = places - second_end
    covered = jnp.take_along_axis(covering, jnp.clip(self_place, 0, M_DEV - 1), axis=1)
    local_part = jnp.where((offsets == 0) & (self_place < M_DEV), covered, scattered)
    return (owners * M_DEV + local_part).reshape(-1).astype(jnp.int32)


def with_ends(result, own_key, least, high):
    spot = [jax.random.randint(jax.random.fold_in(own_key, axis), (), 0, length) for axis, length in enumerate(result.shape)]
    longest = result.shape.index(max(result.shape))
    beside = spot[:longest] + [(spot[longest] + 1) % result.shape[longest]] + spot[longest + 1:]
    return result.at[tuple(spot)].set(least).at[tuple(beside)].set(high)


def levels(own_key, extent, pieces, low, largest):
    def one(position, blocks):
        heights = jax.random.uniform(jax.random.fold_in(jax.random.fold_in(own_key, 6), position), (blocks,), jnp.float32, low / len(pieces), largest / len(pieces))
        return jnp.repeat(jnp.exp(heights), extent[position] // blocks).reshape((-1,) + (1,) * (len(extent) - position - 1))

    loudness = one(*pieces[0])
    for cut in pieces[1:]:
        loudness = loudness * one(*cut)
    return loudness


def centred(rng, extent, width, most, cuts=(), kind=jnp.bfloat16):
    values = jax.random.normal(rng, extent, jnp.float32) * width
    if len(cuts) > 0:
        values = levels(rng, extent, cuts, -0.22, 0.18) * values
    return jnp.clip(values, min=-most, max=most).astype(kind)


def setup_inputs(seed: int = 0) -> dict:
    splits = jax.random.split(jax.random.key(seed), 7)
    self_block = draw_self_block(jax.random.fold_in(splits[6], 71), 0)
    couple = centred(splits[1], (INNER, TRACE, ELEMS), TRACE ** -0.5, 0.625, ((2, 32),), jnp.float32)
    inverse = draw_inverse(jax.random.fold_in(splits[6], 71), 0)
    body_force = centred(splits[3], (COMP, INNER, ELEMS), 1.0, 6.0, ((2, 32),), jnp.float32)
    face_mortar = draw_face_mortar(jax.random.fold_in(splits[6], 71), 0)
    face_kind = with_ends(jax.random.randint(splits[5], (SLOTS,), 0, 5), jax.random.fold_in(splits[5], 1), 0, 4).astype(jnp.int32)
    return {"self_block": self_block, "couple": couple, "inverse": inverse, "body_force": body_force, "face_mortar": face_mortar, "face_kind": face_kind}


PRECISE = lax.Precision.HIGHEST


def interp_tables():
    abscissae = -np.cos(np.pi * np.arange(4) / 3.0)

    def lagrange(points):
        columns = [np.prod([(points - abscissae[other_node]) / (abscissae[basis_node] - abscissae[other_node]) for other_node in range(4) if other_node != basis_node], axis=0) for basis_node in range(4)]
        return np.stack(columns, axis=1)

    lower_map = lagrange((abscissae - 1.0) / 2.0)
    upper_map = lagrange((abscissae + 1.0) / 2.0)
    identity = np.eye(4)
    return np.stack([np.kron(identity, identity), np.kron(lower_map, lower_map), np.kron(lower_map, upper_map), np.kron(upper_map, lower_map), np.kron(upper_map, upper_map)])


def to_faces(values, kind_ids, tables):
    node_count = tables.shape[1]
    by_comp = values.reshape(values.shape[0] // node_count, node_count, values.shape[1])
    mapped = jnp.einsum('kab,cbi->kcai', tables, by_comp, precision=PRECISE)
    selector = (kind_ids[None, :] == jnp.arange(5, dtype=jnp.int32)[:, None]).astype(values.dtype)
    return jnp.einsum('kcai,ki->cai', mapped, selector, precision=PRECISE).reshape(values.shape)


def to_mortar(values, kind_ids, tables):
    node_count = tables.shape[1]
    by_comp = values.reshape(values.shape[0] // node_count, node_count, values.shape[1])
    mapped = jnp.einsum('kab,cai->kcbi', tables, by_comp, precision=PRECISE)
    selector = (kind_ids[None, :] == jnp.arange(5, dtype=jnp.int32)[:, None]).astype(values.dtype)
    return jnp.einsum('kcbi,ki->cbi', mapped, selector, precision=PRECISE).reshape(values.shape)


def slot_to_element(values, elements, node_count):
    comp_count = values.shape[0] // node_count
    arranged = values.reshape(comp_count, node_count, elements, 6)
    return jnp.transpose(arranged, (0, 3, 1, 2)).reshape(comp_count, 6 * node_count, elements)


def element_to_slot(values, elements, node_count):
    comp_count = values.shape[0]
    arranged = values.reshape(comp_count, 6, node_count, elements)
    return jnp.transpose(arranged, (0, 2, 3, 1)).reshape(comp_count * node_count, elements * 6)


def reference(self_block, couple, inverse, body_force, face_mortar, face_kind):
    elements = self_block.shape[2]
    tables = jnp.asarray(interp_tables(), dtype=jnp.float32)
    node_count = tables.shape[1]
    weighted = jnp.einsum('ike,kbe->ibe', inverse, couple, precision=PRECISE)
    condensed = self_block + jnp.einsum('iae,ibe->abe', couple, weighted, precision=PRECISE)
    solved_load = jnp.einsum('ike,cke->cie', inverse, body_force, precision=PRECISE)
    local_rhs = jnp.einsum('iae,cie->cae', couple, solved_load, precision=PRECISE)

    def assemble(per_element):
        slot_values = element_to_slot(per_element, elements, node_count)
        mortar_values = to_mortar(slot_values, face_kind, tables)
        return jnp.zeros((mortar_values.shape[0], MORTARS), jnp.float32).at[:, face_mortar].add(mortar_values)

    def spread(field_values):
        return slot_to_element(to_faces(field_values[:, face_mortar], face_kind, tables), elements, node_count)

    def operate(field_values):
        return assemble(jnp.einsum('abe,cbe->cae', condensed, spread(field_values), precision=PRECISE))

    residual = assemble(local_rhs)
    trace_field = jnp.zeros_like(residual)
    direction = residual
    current = jnp.sum(residual * residual)
    for iteration in range(ITERS):
        image_field = operate(direction)
        step_length = current / jnp.sum(direction * image_field)
        trace_field = trace_field + step_length * direction
        if iteration + 1 < ITERS:
            residual = residual - step_length * image_field
            following = jnp.sum(residual * residual)
            direction = residual + (following / current) * direction
            current = following
    faces_elem = spread(trace_field)
    difference = body_force - jnp.einsum('ibe,cbe->cie', couple, faces_elem, precision=PRECISE)
    interior = jnp.einsum('ike,cke->cie', inverse, difference, precision=PRECISE)
    return trace_field, interior
```

```python
import functools

import jax
import jax.numpy as jnp
import numpy as np
from jax import lax
from jax.experimental import pallas as pl
from jax.experimental.pallas import tpu as pltpu
from jax.sharding import PartitionSpec as P

AXES = ("dom", "blk")
COMP = 3
NODES = 16
FACES = 6
RUNS = 4
F32 = jnp.float32
BF16 = jnp.bfloat16


def interp_tables():
    abscissae = -np.cos(np.pi * np.arange(4) / 3.0)

    def lagrange(points):
        columns = [
            np.prod(
                [
                    (points - abscissae[other_node])
                    / (abscissae[basis_node] - abscissae[other_node])
                    for other_node in range(4)
                    if other_node != basis_node
                ],
                axis=0,
            )
            for basis_node in range(4)
        ]
        return np.stack(columns, axis=1)

    lower_map = lagrange((abscissae - 1.0) / 2.0)
    upper_map = lagrange((abscissae + 1.0) / 2.0)
    return np.stack(
        [
            np.kron(lower_map, lower_map),
            np.kron(lower_map, upper_map),
            np.kron(upper_map, lower_map),
            np.kron(upper_map, upper_map),
        ]
    ).astype(np.float32)


def block_tables():
    tables = interp_tables()
    eye = np.eye(COMP, dtype=np.float32)
    forward = np.concatenate([np.kron(eye, t) for t in tables])
    backward = np.concatenate([np.kron(eye, t.T) for t in tables])
    return forward, backward


def split(x):
    hi = x.astype(BF16)
    return hi, (x - hi.astype(F32)).astype(BF16)


def dot(a, b, rhs_dim=0):
    return lax.dot_general(a, b, (((1,), (rhs_dim,)), ((), ())), preferred_element_type=F32)


def exact_dot(x, onehot, rhs_dim=0):
    hi, lo = split(x)
    both = dot(jnp.concatenate([hi, lo], axis=0), onehot, rhs_dim)
    return both[: x.shape[0]] + both[x.shape[0] :]


def by_kind(x, table_ref, kind):
    rows = x.shape[0]
    t_hi, t_lo = split(table_ref[...])
    x_hi, x_lo = split(x)
    mapped = dot(
        jnp.concatenate([t_hi, t_hi, t_lo], axis=1), jnp.concatenate([x_hi, x_lo, x_hi], axis=0)
    )
    for number in range(4):
        x = jnp.where(kind == number + 1, mapped[number * rows : (number + 1) * rows], x)
    return x


def lanes(rows_ref, start, count=FACES):
    return jnp.concatenate([rows_ref[start + f : start + f + 1, :] for f in range(count)], axis=1)


def contract(acc, mat_ref, vec_ref, outs, terms, across, unroll=8):
    blocks = outs // 8

    def body(t, acc):
        acc = [list(a) for a in acc]
        vecs = [
            jnp.broadcast_to(vec_ref[pl.ds(c * terms + t, 1), :], (8, vec_ref.shape[1]))
            for c in range(COMP)
        ]
        for j in range(blocks):
            if across:
                tile = mat_ref[pl.ds(j * 8 * terms + t, 8, stride=terms), :]
            else:
                tile = mat_ref[pl.ds(pl.multiple_of(t * outs + j * 8, 8), 8), :]
            for c in range(COMP):
                acc[c][j] = acc[c][j] + tile * vecs[c]
        return acc

    return lax.fori_loop(0, terms, body, acc, unroll=unroll)


def zeros(outs, width):
    return [[jnp.zeros((8, width), F32) for _ in range(outs // 8)] for _ in range(COMP)]


def put(ref, acc):
    outs = 8 * len(acc[0])
    for c in range(COMP):
        for j, tile in enumerate(acc[c]):
            ref[c * outs + 8 * j : c * outs + 8 * j + 8, :] = tile


def face_columns(acc):
    half = NODES // 8
    return jnp.concatenate(
        [
            jnp.concatenate(
                [acc[c][f * half + h] for c in range(COMP) for h in range(half)], axis=0
            )
            for f in range(FACES)
        ],
        axis=1,
    )


def start_kernel(
    ranks, inner, trace, owned, cap,
    mortar_ref, kind_ref, inverse_ref, couple_ref, force_ref, back_ref,
    own_ref, out_ref, onehot_ref, meta_ref, load_ref,
):
    width = mortar_ref.shape[1]
    mortar = mortar_ref[...]
    owner = lax.div(mortar, owned)
    index = lax.rem(mortar, owned)
    me = lax.rem(owner[0:1, 0:1] + 2, ranks)
    distance = lax.rem(owner - me + ranks, ranks)
    slot = lax.broadcasted_iota(jnp.int32, mortar.shape, 1) * FACES + lax.broadcasted_iota(
        jnp.int32, mortar.shape, 0
    )
    column = index
    begin = jnp.zeros((1, 1), jnp.int32)
    for number, away in enumerate((ranks - 2, ranks - 1, 0, 1, ranks // 2)):
        inside = distance == away
        count = jnp.sum(inside.astype(F32), keepdims=True).astype(jnp.int32)
        if away:
            run = number - (number > 2)
            column = jnp.where(inside, owned + run * cap + slot - begin, column)
        begin = begin + count
    meta_ref[0:FACES, :] = kind_ref[...]
    meta_ref[FACES : FACES + 1, :] = jnp.broadcast_to(lax.rem(me, 2), (1, width))
    meta_ref[FACES + 1 : FACES + 2, :] = jnp.zeros((1, width), jnp.int32)
    rows = owned + RUNS * cap
    for f in range(FACES):
        onehot_ref[:, f * width : (f + 1) * width] = jnp.where(
            lax.broadcasted_iota(jnp.int32, (rows, width), 0) == column[f : f + 1, :], 1.0, 0.0
        ).astype(BF16)
    load = contract(zeros(inner, width), inverse_ref, force_ref, inner, inner, True)
    put(load_ref, load)
    y = contract(zeros(trace, width), couple_ref, load_ref, trace, inner, False)
    z = by_kind(face_columns(y), back_ref, lanes(kind_ref, 0))
    label = jnp.concatenate([index[f : f + 1, :] for f in range(FACES)], axis=1) + 1
    label = jnp.where(
        lax.broadcasted_iota(jnp.int32, (8, z.shape[1]), 0) == 0, label, 0
    ).astype(F32)
    sums = exact_dot(jnp.concatenate([z, label], axis=0), onehot_ref[...], 1)
    own_ref[...] = sums[: COMP * NODES, :owned]
    out_ref[...] = sums[:, owned:]


def merged(meta_ref, first, second, third, fourth, cap, to_owner):
    lane = lax.broadcasted_iota(jnp.int32, (1, RUNS * cap), 1)
    odd = meta_ref[FACES : FACES + 1, :] == 1
    low = lane < 2 * cap
    take_first = (low != odd) if to_owner else (low == odd)
    middle = jnp.where(take_first, first, second)
    return jnp.where(lane < cap, fourth, jnp.where(lane < 3 * cap, middle, third))


def owner_kernel(owned, cap, initial, meta_ref, label_ref, own_ref, a_ref, b_ref, c_ref, d_ref, *outs):
    received = merged(meta_ref, a_ref[...], b_ref[...], c_ref[...], d_ref[...], cap, True)
    rows = COMP * NODES
    if initial:
        field_ref, out_ref, label_out_ref = outs
        label = received[rows : rows + 8]
        label_out_ref[...] = label
    else:
        field_ref, out_ref = outs
        label = label_ref[...]
    wanted = (
        lax.broadcasted_iota(jnp.int32, (owned, RUNS * cap), 0)
        == label[0:1, :].astype(jnp.int32) - 1
    )
    wanted = jnp.where(wanted, 1.0, 0.0).astype(BF16)
    field = own_ref[...] + exact_dot(received[:rows], wanted, 1)
    field_ref[...] = field
    out_ref[...] = exact_dot(field, wanted)


def element_values(cap, meta_ref, onehot_ref, forth_ref, field_ref, blocks, spread_ref):
    received = merged(meta_ref, *[b[...] for b in blocks], cap, False)
    source = jnp.concatenate([field_ref[...], received], axis=1)
    kind = lanes(meta_ref, 0)
    faces = by_kind(exact_dot(source, onehot_ref[...]), forth_ref, kind)
    width = spread_ref.shape[1]
    for c in range(COMP):
        for f in range(FACES):
            spread_ref[(c * FACES + f) * NODES : (c * FACES + f + 1) * NODES, :] = faces[
                c * NODES : (c + 1) * NODES, f * width : (f + 1) * width
            ]
    return kind


def apply_kernel(
    inner, trace, owned, cap,
    meta_ref, onehot_ref, forth_ref, back_ref, inverse_ref, couple_ref, self_ref,
    field_ref, a_ref, b_ref, c_ref, d_ref,
    own_ref, out_ref, spread_ref, mid_ref, weight_ref,
):
    width = spread_ref.shape[1]
    kind = element_values(
        cap, meta_ref, onehot_ref, forth_ref, field_ref, (a_ref, b_ref, c_ref, d_ref), spread_ref
    )
    put(mid_ref, contract(zeros(inner, width), couple_ref, spread_ref, inner, trace, True))
    put(weight_ref, contract(zeros(inner, width), inverse_ref, mid_ref, inner, inner, True))
    y = contract(zeros(trace, width), self_ref, spread_ref, trace, trace, True)
    y = contract(y, couple_ref, weight_ref, trace, inner, False)
    z = by_kind(face_columns(y), back_ref, kind)
    sums = exact_dot(z, onehot_ref[...], 1)
    own_ref[...] = sums[:, :owned]
    out_ref[...] = sums[:, owned:]


def total(x):
    return jnp.sum(jnp.sum(x, axis=0, keepdims=True), axis=1, keepdims=True)


def last_kernel(
    inner, trace, cap,
    meta_ref, onehot_ref, forth_ref, inverse_ref, couple_ref, self_ref,
    k0_ref, k1_ref, k2_ref, a_ref, b_ref, c_ref, d_ref, s0_ref, s1_ref, u0_ref, u1_ref,
    weight_ref, moment_ref, spread_ref, mid_ref, image_ref,
):
    width = spread_ref.shape[1]
    element_values(
        cap, meta_ref, onehot_ref, forth_ref, k2_ref, (a_ref, b_ref, c_ref, d_ref), spread_ref
    )
    put(mid_ref, contract(zeros(inner, width), couple_ref, spread_ref, inner, trace, True))
    put(weight_ref, contract(zeros(inner, width), inverse_ref, mid_ref, inner, inner, True))
    put(image_ref, contract(zeros(trace, width), self_ref, spread_ref, trace, trace, True))
    image, weight = image_ref[...], weight_ref[...]
    ks = (k0_ref[...], k1_ref[...], k2_ref[...])
    values = [total(ks[i] * ks[j]) for i in range(3) for j in range(i, 3)]
    for s_ref, u_ref in ((s0_ref, u0_ref), (s1_ref, u1_ref), (spread_ref, mid_ref)):
        values.append(total(s_ref[...] * image) + total(u_ref[...] * weight))
    lane = lax.broadcasted_iota(jnp.int32, (1, width), 1)
    row = jnp.zeros((1, width), F32)
    for number, value in enumerate(values):
        row = jnp.where(lane == number, value, row)
    moment_ref[...] = jnp.broadcast_to(row[None], moment_ref.shape)


def finish_kernel(
    moment_ref, k0_ref, k1_ref, k2_ref, w0_ref, w1_ref, w2_ref, load_ref, field_ref, interior_ref
):
    sums = jnp.sum(moment_ref[...], axis=0)
    m = [sums[:, n : n + 1] for n in range(9)]
    gram = [[m[0], m[1], m[2]], [m[1], m[3], m[4]], [m[2], m[4], m[5]]]
    energy = [[gram[i][1], gram[i][2], m[6 + i]] for i in range(3)]

    def form(x, matrix):
        return sum(x[i] * sum(matrix[i][j] * x[j] for j in range(3)) for i in range(3))

    zero, one = jnp.zeros((1, 1), F32), jnp.ones((1, 1), F32)
    x = [zero, zero, zero]
    r = [one, zero, zero]
    d = [one, zero, zero]
    current = gram[0][0]
    for iteration in range(3):
        step = current / form(d, energy)
        x = [x[i] + step * d[i] for i in range(3)]
        if iteration < 2:
            r = [r[0], r[1] - step * d[0], r[2] - step * d[1]]
            following = form(r, gram)
            d = [r[i] + following / current * d[i] for i in range(3)]
            current = following
    field_ref[...] = x[0] * k0_ref[...] + x[1] * k1_ref[...] + x[2] * k2_ref[...]
    interior_ref[...] = load_ref[...] - (
        x[0] * w0_ref[...] + x[1] * w1_ref[...] + x[2] * w2_ref[...]
    )


def call(kernel, outs, *args):
    return pl.pallas_call(
        kernel,
        out_shape=[jax.ShapeDtypeStruct(shape, dtype) for shape, dtype in outs],
        in_specs=[pl.BlockSpec(memory_space=pltpu.VMEM)] * len(args),
        out_specs=[pl.BlockSpec(memory_space=pltpu.VMEM)] * len(outs),
        compiler_params=pltpu.CompilerParams(vmem_limit_bytes=40 * 1024 * 1024),
    )(*args)


def call_scratch(kernel, outs, scratch, *args):
    return pl.pallas_call(
        kernel,
        out_shape=[jax.ShapeDtypeStruct(shape, dtype) for shape, dtype in outs],
        in_specs=[pl.BlockSpec(memory_space=pltpu.VMEM)] * len(args),
        out_specs=[pl.BlockSpec(memory_space=pltpu.VMEM)] * len(outs),
        scratch_shapes=[pltpu.VMEM(shape, F32) for shape in scratch],
        compiler_params=pltpu.CompilerParams(vmem_limit_bytes=40 * 1024 * 1024),
    )(*args)


def exchange(block, ranks, to_owner):
    away = ranks - 2 if to_owner else 2
    pairs = [
        [(r, r ^ 1) for r in range(ranks)],
        [(r, (r + (1 if r % 2 else ranks - 1)) % ranks) for r in range(ranks)],
        [(r, (r + ranks // 2) % ranks) for r in range(ranks)],
        [(r, (r + away) % ranks) for r in range(ranks)],
    ]
    return [lax.ppermute(block, AXES, p) for p in pairs]


def local(self_block, couple, inverse, body_force, face_mortar, face_kind, *, ranks):
    trace, _, elements = self_block.shape
    inner = inverse.shape[0]
    owned = 2 * elements
    cap = max(2, elements // 4)
    width = elements
    rows = COMP * NODES
    forward, backward = block_tables()
    mortar = face_mortar.reshape(elements, FACES).T
    kind = face_kind.reshape(elements, FACES).T
    self_block = self_block.reshape(trace * trace, width)
    couple = couple.reshape(inner * trace, width)
    inverse = inverse.reshape(inner * inner, width)
    force = body_force.reshape(COMP * inner, width)

    own, out, onehot, meta, load = call(
        functools.partial(start_kernel, ranks, inner, trace, owned, cap),
        [
            ((rows, owned), F32),
            ((rows + 8, RUNS * cap), F32),
            ((owned + RUNS * cap, FACES * width), BF16),
            ((8, width), jnp.int32),
            ((COMP * inner, width), F32),
        ],
        mortar, kind, inverse, couple, force, backward,
    )
    blocks = exchange(out, ranks, True)
    field, out, label = call(
        functools.partial(owner_kernel, owned, cap, True),
        [((rows, owned), F32), ((rows, RUNS * cap), F32), ((8, RUNS * cap), F32)],
        meta, meta, own, *blocks,
    )
    fields, spreads, mids, weights = [field], [], [], []
    for _ in range(2):
        blocks = exchange(out, ranks, False)
        own, out, spread, mid, weight = call(
            functools.partial(apply_kernel, inner, trace, owned, cap),
            [
                ((rows, owned), F32),
                ((rows, RUNS * cap), F32),
                ((COMP * trace, width), F32),
                ((COMP * inner, width), F32),
                ((COMP * inner, width), F32),
            ],
            meta, onehot, forward, backward, inverse, couple, self_block, field, *blocks,
        )
        spreads.append(spread)
        mids.append(mid)
        weights.append(weight)
        blocks = exchange(out, ranks, True)
        field, out = call(
            functools.partial(owner_kernel, owned, cap, False),
            [((rows, owned), F32), ((rows, RUNS * cap), F32)],
            meta, label, own, *blocks,
        )
        fields.append(field)
    blocks = exchange(out, ranks, False)
    weight, moments = call_scratch(
        functools.partial(last_kernel, inner, trace, cap),
        [((COMP * inner, width), F32), ((ranks, 1, width), F32)],
        [(COMP * trace, width), (COMP * inner, width), (COMP * trace, width)],
        meta, onehot, forward, inverse, couple, self_block, *fields, *blocks, *spreads, *mids,
    )
    weights.append(weight)
    moments = lax.all_to_all(moments, AXES, split_axis=0, concat_axis=0, tiled=True)
    trace_field, interior = call(
        finish_kernel,
        [((rows, owned), F32), ((COMP * inner, width), F32)],
        moments, *fields, *weights, load,
    )
    return trace_field, interior.reshape(COMP, inner, elements)


def solution(mesh):
    placed = (
        P(None, None, AXES),
        P(None, None, AXES),
        P(None, None, AXES),
        P(None, None, AXES),
        P(AXES),
        P(AXES),
    )
    ranks = int(np.prod([mesh.shape[a] for a in AXES]))
    return jax.shard_map(
        functools.partial(local, ranks=ranks),
        mesh=mesh,
        in_specs=placed,
        out_specs=(P(None, AXES), P(None, None, AXES)),
        check_vma=False,
    )
```

```python
import functools

import jax
import jax.numpy as jnp
import numpy as np
from jax import lax
from jax.experimental import pallas as pl
from jax.experimental.pallas import tpu as pltpu
from jax.sharding import PartitionSpec as P

AXES = ("dom", "blk")
COMP = 3
NODES = 16
FACES = 6
RUNS = 4
F32 = jnp.float32
BF16 = jnp.bfloat16


def interp_tables():
    abscissae = -np.cos(np.pi * np.arange(4) / 3.0)

    def lagrange(points):
        columns = [
            np.prod(
                [
                    (points - abscissae[other_node])
                    / (abscissae[basis_node] - abscissae[other_node])
                    for other_node in range(4)
                    if other_node != basis_node
                ],
                axis=0,
            )
            for basis_node in range(4)
        ]
        return np.stack(columns, axis=1)

    lower_map = lagrange((abscissae - 1.0) / 2.0)
    upper_map = lagrange((abscissae + 1.0) / 2.0)
    return np.stack(
        [
            np.kron(lower_map, lower_map),
            np.kron(lower_map, upper_map),
            np.kron(upper_map, lower_map),
            np.kron(upper_map, upper_map),
        ]
    ).astype(np.float32)


def block_tables():
    tables = interp_tables()
    eye = np.eye(COMP, dtype=np.float32)
    forward = np.concatenate([np.kron(eye, t) for t in tables])
    backward = np.concatenate([np.kron(eye, t.T) for t in tables])
    return forward, backward


def split(x):
    hi = x.astype(BF16)
    return hi, (x - hi.astype(F32)).astype(BF16)


def dot(a, b, rhs_dim=0):
    return lax.dot_general(a, b, (((1,), (rhs_dim,)), ((), ())), preferred_element_type=F32)


def exact_dot(x, onehot, rhs_dim=0):
    hi, lo = split(x)
    both = dot(jnp.concatenate([hi, lo], axis=0), onehot, rhs_dim)
    return both[: x.shape[0]] + both[x.shape[0] :]


def by_kind(x, table_ref, kind):
    rows = x.shape[0]
    t_hi, t_lo = split(table_ref[...])
    x_hi, x_lo = split(x)
    mapped = dot(
        jnp.concatenate([t_hi, t_hi, t_lo], axis=1), jnp.concatenate([x_hi, x_lo, x_hi], axis=0)
    )
    for number in range(4):
        x = jnp.where(kind == number + 1, mapped[number * rows : (number + 1) * rows], x)
    return x


def in_a_row(x):
    return jnp.concatenate([x[r : r + 1, :] for r in range(x.shape[0])], axis=1)


def gather_rows(tiles, sublane):
    tiles = [tiles[r] for r in (0, 4, 2, 6, 1, 5, 3, 7)]
    keep = (sublane & 4) == 0
    tiles = [
        jnp.where(keep, x, y) + pltpu.roll(jnp.where(keep, y, x), 4, 0)
        for x, y in zip(tiles[::2], tiles[1::2])
    ]
    for shift in (2, 1):
        keep = (sublane & shift) == 0
        tiles = [
            jnp.where(keep, x + pltpu.roll(x, 8 - shift, 0), y + pltpu.roll(y, shift, 0))
            for x, y in zip(tiles[::2], tiles[1::2])
        ]
    return tiles[0]


def rows_times(mat_ref, vec_ref, out_ref, outs, terms, group=32):
    width = vec_ref.shape[1]
    sublane = lax.broadcasted_iota(jnp.int32, (8, width), 0)
    vecs = [
        [vec_ref[c * terms + t : c * terms + t + 8, :] for t in range(0, terms, 8)]
        for c in range(COMP)
    ]

    def body(g, carry):
        for first in range(0, group, 8):
            sums = [[] for _ in range(COMP)]
            for r in range(first, first + 8):
                acc = [None] * COMP
                for j in range(terms // 8):
                    start = pl.multiple_of((g * group + r) * terms + 8 * j, 8)
                    tile = mat_ref[pl.ds(start, 8), :]
                    for c in range(COMP):
                        term = tile * vecs[c][j]
                        acc[c] = term if j == 0 else acc[c] + term
                for c in range(COMP):
                    sums[c].append(acc[c])
            for c in range(COMP):
                start = pl.multiple_of(c * outs + g * group + first, 8)
                out_ref[pl.ds(start, 8), :] = gather_rows(sums[c], sublane)
        return carry

    lax.fori_loop(0, outs // group, body, 0)


def columns_times(acc, mat_ref, vec_ref, outs, terms, unroll=16):
    def body(t, acc):
        acc = [list(a) for a in acc]
        vecs = [
            jnp.broadcast_to(vec_ref[pl.ds(c * terms + t, 1), :], (8, vec_ref.shape[1]))
            for c in range(COMP)
        ]
        for j in range(outs // 8):
            tile = mat_ref[pl.ds(pl.multiple_of(t * outs + j * 8, 8), 8), :]
            for c in range(COMP):
                acc[c][j] = acc[c][j] + tile * vecs[c]
        return acc

    return lax.fori_loop(0, terms, body, acc, unroll=unroll)


def tiles_of(ref, outs):
    return [[ref[c * outs + t : c * outs + t + 8, :] for t in range(0, outs, 8)] for c in range(COMP)]


def zeros(outs, width):
    return [[jnp.zeros((8, width), F32) for _ in range(outs // 8)] for _ in range(COMP)]


def face_columns(acc):
    half = NODES // 8
    return jnp.concatenate(
        [
            jnp.concatenate(
                [acc[c][f * half + h] for c in range(COMP) for h in range(half)], axis=0
            )
            for f in range(FACES)
        ],
        axis=1,
    )


def start_kernel(
    ranks, inner, trace, owned, cap,
    mortar_hbm, kind_hbm, force_hbm, back_hbm, inverse_hbm, couple_hbm,
    own_ref, out_ref, onehot_ref, meta_ref, load_ref, inverse_ref, couple_ref,
    mortar_ref, kind_ref, force_ref, back_ref, *sems,
):
    copies = [
        pltpu.make_async_copy(source, target, sem)
        for source, target, sem in zip(
            (mortar_hbm, kind_hbm, force_hbm, back_hbm, inverse_hbm, couple_hbm),
            (mortar_ref, kind_ref, force_ref, back_ref, inverse_ref, couple_ref),
            sems,
        )
    ]
    for copy in copies:
        copy.start()
    copies[0].wait()
    copies[1].wait()
    width = mortar_ref.shape[1]
    slots = FACES * width
    mortar = mortar_ref[...]
    owner = lax.div(mortar, owned)
    index = lax.rem(mortar, owned)
    me = lax.rem(owner[0:1, 0:1] + 2, ranks)
    distance = lax.rem(owner - me + ranks, ranks)
    slot = lax.broadcasted_iota(jnp.int32, mortar.shape, 0) * width + lax.broadcasted_iota(
        jnp.int32, mortar.shape, 1
    )
    column = index
    begin = jnp.zeros((1, 1), jnp.int32)
    for number, away in enumerate((ranks - 2, ranks - 1, 0, 1, ranks // 2)):
        inside = distance == away
        count = jnp.sum(inside.astype(F32), keepdims=True).astype(jnp.int32)
        if away:
            run = number - (number > 2)
            column = jnp.where(inside, owned + run * cap + slot - begin, column)
        begin = begin + count
    target = lax.broadcasted_iota(jnp.int32, (1, slots), 1)
    target = lax.rem(target, width) * FACES + lax.div(target, width)
    order = jnp.where(
        lax.broadcasted_iota(jnp.int32, (slots, slots), 0) == target, 1.0, 0.0
    ).astype(BF16)
    facts = jnp.concatenate(
        [in_a_row(column), in_a_row(index + 1), in_a_row(kind_ref[...]), jnp.zeros((5, slots), jnp.int32)],
        axis=0,
    ).astype(F32)
    facts = exact_dot(facts, order)
    meta_ref[...] = facts
    meta_ref[3:4, :] = jnp.broadcast_to(lax.rem(me, 2).astype(F32), (1, slots))
    column = facts[0:1, :].astype(jnp.int32)
    onehot_ref[...] = jnp.where(
        lax.broadcasted_iota(jnp.int32, onehot_ref.shape, 0) == column, 1.0, 0.0
    ).astype(BF16)
    copies[2].wait()
    copies[4].wait()
    rows_times(inverse_ref, force_ref, load_ref, inner, inner)
    copies[3].wait()
    copies[5].wait()
    y = columns_times(zeros(trace, width), couple_ref, load_ref, trace, inner)
    z = by_kind(face_columns(y), back_ref, facts[2:3, :])
    label = jnp.where(
        lax.broadcasted_iota(jnp.int32, (8, slots), 0) == 0, facts[1:2, :], 0.0
    )
    sums = exact_dot(jnp.concatenate([z, label], axis=0), onehot_ref[...], 1)
    own_ref[...] = sums[: COMP * NODES, :owned]
    out_ref[...] = sums[:, owned:]


def merged(meta_ref, first, second, third, fourth, cap, to_owner):
    lane = lax.broadcasted_iota(jnp.int32, (1, RUNS * cap), 1)
    odd = meta_ref[3:4, : RUNS * cap] == 1.0
    low = lane < 2 * cap
    take_first = (low != odd) if to_owner else (low == odd)
    middle = jnp.where(take_first, first, second)
    return jnp.where(lane < cap, fourth, jnp.where(lane < 3 * cap, middle, third))


def owner_kernel(owned, cap, initial, meta_ref, label_ref, own_ref, a_ref, b_ref, c_ref, d_ref, *outs):
    received = merged(meta_ref, a_ref[...], b_ref[...], c_ref[...], d_ref[...], cap, True)
    rows = COMP * NODES
    if initial:
        field_ref, out_ref, label_out_ref = outs
        label = received[rows : rows + 8]
        label_out_ref[...] = label
    else:
        field_ref, out_ref = outs
        label = label_ref[...]
    wanted = (
        lax.broadcasted_iota(jnp.int32, (owned, RUNS * cap), 0)
        == label[0:1, :].astype(jnp.int32) - 1
    )
    wanted = jnp.where(wanted, 1.0, 0.0).astype(BF16)
    field = own_ref[...] + exact_dot(received[:rows], wanted, 1)
    field_ref[...] = field
    out_ref[...] = exact_dot(field, wanted)


def element_values(cap, meta_ref, onehot_ref, forth_ref, field_ref, blocks, spread_ref):
    received = merged(meta_ref, *[b[...] for b in blocks], cap, False)
    source = jnp.concatenate([field_ref[...], received], axis=1)
    kind = meta_ref[2:3, :]
    faces = by_kind(exact_dot(source, onehot_ref[...]), forth_ref, kind)
    width = spread_ref.shape[1]
    for c in range(COMP):
        for f in range(FACES):
            spread_ref[(c * FACES + f) * NODES : (c * FACES + f + 1) * NODES, :] = faces[
                c * NODES : (c + 1) * NODES, f * width : (f + 1) * width
            ]
    return kind


def apply_kernel(
    inner, trace, owned, cap,
    meta_ref, onehot_ref, forth_ref, back_ref, inverse_ref, couple_ref,
    field_ref, a_ref, b_ref, c_ref, d_ref, self_hbm,
    own_ref, out_ref, spread_ref, mid_ref, weight_ref, image_ref, self_ref, sem,
):
    copy = pltpu.make_async_copy(self_hbm, self_ref, sem)
    copy.start()
    width = spread_ref.shape[1]
    kind = element_values(
        cap, meta_ref, onehot_ref, forth_ref, field_ref, (a_ref, b_ref, c_ref, d_ref), spread_ref
    )
    rows_times(couple_ref, spread_ref, mid_ref, inner, trace)
    rows_times(inverse_ref, mid_ref, weight_ref, inner, inner)
    copy.wait()
    rows_times(self_ref, spread_ref, image_ref, trace, trace)
    y = columns_times(tiles_of(image_ref, trace), couple_ref, weight_ref, trace, inner)
    z = by_kind(face_columns(y), back_ref, kind)
    sums = exact_dot(z, onehot_ref[...], 1)
    own_ref[...] = sums[:, :owned]
    out_ref[...] = sums[:, owned:]


def total(x):
    return jnp.sum(jnp.sum(x, axis=0, keepdims=True), axis=1, keepdims=True)


def last_kernel(
    inner, trace, cap,
    meta_ref, onehot_ref, forth_ref, inverse_ref, couple_ref,
    k0_ref, k1_ref, k2_ref, a_ref, b_ref, c_ref, d_ref, s0_ref, s1_ref, u0_ref, u1_ref, self_hbm,
    weight_ref, moment_ref, spread_ref, mid_ref, image_ref, self_ref, sem,
):
    copy = pltpu.make_async_copy(self_hbm, self_ref, sem)
    copy.start()
    width = spread_ref.shape[1]
    element_values(
        cap, meta_ref, onehot_ref, forth_ref, k2_ref, (a_ref, b_ref, c_ref, d_ref), spread_ref
    )
    rows_times(couple_ref, spread_ref, mid_ref, inner, trace)
    rows_times(inverse_ref, mid_ref, weight_ref, inner, inner)
    copy.wait()
    rows_times(self_ref, spread_ref, image_ref, trace, trace)
    image, weight = image_ref[...], weight_ref[...]
    ks = (k0_ref[...], k1_ref[...], k2_ref[...])
    values = [total(ks[i] * ks[j]) for i in range(3) for j in range(i, 3)]
    for s_ref, u_ref in ((s0_ref, u0_ref), (s1_ref, u1_ref), (spread_ref, mid_ref)):
        values.append(total(s_ref[...] * image) + total(u_ref[...] * weight))
    lane = lax.broadcasted_iota(jnp.int32, (1, width), 1)
    row = jnp.zeros((1, width), F32)
    for number, value in enumerate(values):
        row = jnp.where(lane == number, value, row)
    moment_ref[...] = jnp.broadcast_to(row[None], moment_ref.shape)


def finish_kernel(
    moment_ref, k0_ref, k1_ref, k2_ref, w0_ref, w1_ref, w2_ref, load_ref, field_ref, interior_ref
):
    sums = jnp.sum(moment_ref[...], axis=0)
    m = [sums[:, n : n + 1] for n in range(9)]
    gram = [[m[0], m[1], m[2]], [m[1], m[3], m[4]], [m[2], m[4], m[5]]]
    energy = [[gram[i][1], gram[i][2], m[6 + i]] for i in range(3)]

    def form(x, matrix):
        return sum(x[i] * sum(matrix[i][j] * x[j] for j in range(3)) for i in range(3))

    zero, one = jnp.zeros((1, 1), F32), jnp.ones((1, 1), F32)
    x = [zero, zero, zero]
    r = [one, zero, zero]
    d = [one, zero, zero]
    current = gram[0][0]
    for iteration in range(3):
        step = current / form(d, energy)
        x = [x[i] + step * d[i] for i in range(3)]
        if iteration < 2:
            r = [r[0], r[1] - step * d[0], r[2] - step * d[1]]
            following = form(r, gram)
            d = [r[i] + following / current * d[i] for i in range(3)]
            current = following
    field_ref[...] = x[0] * k0_ref[...] + x[1] * k1_ref[...] + x[2] * k2_ref[...]
    interior_ref[...] = load_ref[...] - (
        x[0] * w0_ref[...] + x[1] * w1_ref[...] + x[2] * w2_ref[...]
    )


def call(kernel, outs, *args, scratch=(), in_hbm=0, vmem=8):
    inside = len(args) - in_hbm
    args = args[:inside] + tuple(
        pltpu.with_memory_space_constraint(x, pltpu.HBM) for x in args[inside:]
    )
    return pl.pallas_call(
        kernel,
        out_shape=[jax.ShapeDtypeStruct(shape, dtype) for shape, dtype in outs],
        in_specs=[pl.BlockSpec(memory_space=pltpu.VMEM)] * inside
        + [pl.BlockSpec(memory_space=pltpu.HBM)] * in_hbm,
        out_specs=[pl.BlockSpec(memory_space=pltpu.VMEM)] * len(outs),
        scratch_shapes=[pltpu.VMEM(shape, dtype) for shape, dtype in scratch]
        + [pltpu.SemaphoreType.DMA(())] * in_hbm,
        compiler_params=pltpu.CompilerParams(vmem_limit_bytes=vmem * 1024 * 1024),
    )(*args)


def exchange(block, ranks, to_owner):
    away = ranks - 2 if to_owner else 2
    pairs = [
        [(r, r ^ 1) for r in range(ranks)],
        [(r, (r + (1 if r % 2 else ranks - 1)) % ranks) for r in range(ranks)],
        [(r, (r + ranks // 2) % ranks) for r in range(ranks)],
        [(r, (r + away) % ranks) for r in range(ranks)],
    ]
    return [lax.ppermute(block, AXES, p) for p in pairs]


def local(self_block, couple, inverse, body_force, face_mortar, face_kind, *, ranks):
    trace, _, elements = self_block.shape
    inner = inverse.shape[0]
    owned = 2 * elements
    cap = max(2, elements // 4)
    width = elements
    rows = COMP * NODES
    forward, backward = block_tables()
    mortar = face_mortar.reshape(FACES, width)
    kind = face_kind.reshape(FACES, width)
    self_block = self_block.reshape(trace * trace, width)
    couple = couple.reshape(inner * trace, width)
    inverse = inverse.reshape(inner * inner, width)
    force = body_force.reshape(COMP * inner, width)

    own, out, onehot, meta, load, inverse_in, couple_in = call(
        functools.partial(start_kernel, ranks, inner, trace, owned, cap),
        [
            ((rows, owned), F32),
            ((rows + 8, RUNS * cap), F32),
            ((owned + RUNS * cap, FACES * width), BF16),
            ((8, FACES * width), F32),
            ((COMP * inner, width), F32),
            (inverse.shape, F32),
            (couple.shape, F32),
        ],
        mortar, kind, force, backward, inverse, couple,
        scratch=[
            (mortar.shape, jnp.int32), (kind.shape, jnp.int32), (force.shape, F32), (backward.shape, F32)
        ],
        in_hbm=6, vmem=16,
    )
    blocks = exchange(out, ranks, True)
    field, out, label = call(
        functools.partial(owner_kernel, owned, cap, True),
        [((rows, owned), F32), ((rows, RUNS * cap), F32), ((8, RUNS * cap), F32)],
        meta, meta, own, *blocks,
    )
    fields, spreads, mids, weights = [field], [], [], []
    for _ in range(2):
        blocks = exchange(out, ranks, False)
        own, out, spread, mid, weight = call(
            functools.partial(apply_kernel, inner, trace, owned, cap),
            [
                ((rows, owned), F32),
                ((rows, RUNS * cap), F32),
                ((COMP * trace, width), F32),
                ((COMP * inner, width), F32),
                ((COMP * inner, width), F32),
            ],
            meta, onehot, forward, backward, inverse_in, couple_in, field, *blocks, self_block,
            scratch=[((COMP * trace, width), F32), (self_block.shape, F32)], in_hbm=1, vmem=12,
        )
        spreads.append(spread)
        mids.append(mid)
        weights.append(weight)
        blocks = exchange(out, ranks, True)
        field, out = call(
            functools.partial(owner_kernel, owned, cap, False),
            [((rows, owned), F32), ((rows, RUNS * cap), F32)],
            meta, label, own, *blocks,
        )
        fields.append(field)
    blocks = exchange(out, ranks, False)
    weight, moments = call(
        functools.partial(last_kernel, inner, trace, cap),
        [((COMP * inner, width), F32), ((ranks, 1, width), F32)],
        meta, onehot, forward, inverse_in, couple_in, *fields, *blocks, *spreads, *mids, self_block,
        scratch=[
            ((COMP * trace, width), F32),
            ((COMP * inner, width), F32),
            ((COMP * trace, width), F32),
            (self_block.shape, F32),
        ],
        in_hbm=1, vmem=12,
    )
    weights.append(weight)
    moments = lax.all_to_all(moments, AXES, split_axis=0, concat_axis=0, tiled=True)
    trace_field, interior = call(
        finish_kernel,
        [((rows, owned), F32), ((COMP * inner, width), F32)],
        moments, *fields, *weights, load,
    )
    return trace_field, interior.reshape(COMP, inner, elements)


def solution(mesh):
    placed = (
        P(None, None, AXES),
        P(None, None, AXES),
        P(None, None, AXES),
        P(None, None, AXES),
        P(AXES),
        P(AXES),
    )
    ranks = int(np.prod([mesh.shape[a] for a in AXES]))
    return jax.shard_map(
        functools.partial(local, ranks=ranks),
        mesh=mesh,
        in_specs=placed,
        out_specs=(P(None, AXES), P(None, None, AXES)),
        check_vma=False,
    )
```

```python
import functools

import jax
import jax.numpy as jnp
import numpy as np
from jax import lax
from jax.experimental import pallas as pl
from jax.experimental.pallas import tpu as pltpu
from jax.sharding import PartitionSpec as P

AXES = ("dom", "blk")
COMP = 3
NODES = 16
FACES = 6
RUNS = 4
F32 = jnp.float32
BF16 = jnp.bfloat16


def interp_tables():
    abscissae = -np.cos(np.pi * np.arange(4) / 3.0)

    def lagrange(points):
        columns = [
            np.prod(
                [
                    (points - abscissae[other_node])
                    / (abscissae[basis_node] - abscissae[other_node])
                    for other_node in range(4)
                    if other_node != basis_node
                ],
                axis=0,
            )
            for basis_node in range(4)
        ]
        return np.stack(columns, axis=1)

    lower_map = lagrange((abscissae - 1.0) / 2.0)
    upper_map = lagrange((abscissae + 1.0) / 2.0)
    return np.stack(
        [
            np.kron(lower_map, lower_map),
            np.kron(lower_map, upper_map),
            np.kron(upper_map, lower_map),
            np.kron(upper_map, upper_map),
        ]
    ).astype(np.float32)


def block_tables():
    tables = interp_tables()
    eye = np.eye(COMP, dtype=np.float32)
    forward = np.concatenate([np.kron(eye, t) for t in tables])
    backward = np.concatenate([np.kron(eye, t.T) for t in tables])
    return forward, backward


def split(x):
    hi = x.astype(BF16)
    return hi, (x - hi.astype(F32)).astype(BF16)


def dot(a, b, rhs_dim=0):
    return lax.dot_general(a, b, (((1,), (rhs_dim,)), ((), ())), preferred_element_type=F32)


def exact_dot(x, onehot, rhs_dim=0):
    hi, lo = split(x)
    both = dot(jnp.concatenate([hi, lo], axis=0), onehot, rhs_dim)
    return both[: x.shape[0]] + both[x.shape[0] :]


def by_kind(x, table_ref, kind):
    rows = x.shape[0]
    t_hi, t_lo = split(table_ref[...])
    x_hi, x_lo = split(x)
    mapped = dot(
        jnp.concatenate([t_hi, t_hi, t_lo], axis=1), jnp.concatenate([x_hi, x_lo, x_hi], axis=0)
    )
    for number in range(4):
        x = jnp.where(kind == number + 1, mapped[number * rows : (number + 1) * rows], x)
    return x


def in_a_row(x):
    return jnp.concatenate([x[r : r + 1, :] for r in range(x.shape[0])], axis=1)


def gather_rows(tiles, sublane):
    tiles = [tiles[r] for r in (0, 4, 2, 6, 1, 5, 3, 7)]
    keep = (sublane & 4) == 0
    tiles = [
        jnp.where(keep, x, y) + pltpu.roll(jnp.where(keep, y, x), 4, 0)
        for x, y in zip(tiles[::2], tiles[1::2])
    ]
    for shift in (2, 1):
        keep = (sublane & shift) == 0
        tiles = [
            jnp.where(keep, x + pltpu.roll(x, 8 - shift, 0), y + pltpu.roll(y, shift, 0))
            for x, y in zip(tiles[::2], tiles[1::2])
        ]
    return tiles[0]


def rows_times(mat_ref, vec_ref, out_ref, outs, terms, group=32):
    width = vec_ref.shape[1]
    sublane = lax.broadcasted_iota(jnp.int32, (8, width), 0)
    vecs = [
        [vec_ref[c * terms + t : c * terms + t + 8, :] for t in range(0, terms, 8)]
        for c in range(COMP)
    ]

    def body(g, carry):
        for first in range(0, group, 8):
            sums = [[] for _ in range(COMP)]
            for r in range(first, first + 8):
                acc = [None] * COMP
                for j in range(terms // 8):
                    start = pl.multiple_of((g * group + r) * terms + 8 * j, 8)
                    tile = mat_ref[pl.ds(start, 8), :]
                    for c in range(COMP):
                        term = tile * vecs[c][j]
                        acc[c] = term if j == 0 else acc[c] + term
                for c in range(COMP):
                    sums[c].append(acc[c])
            for c in range(COMP):
                start = pl.multiple_of(c * outs + g * group + first, 8)
                out_ref[pl.ds(start, 8), :] = gather_rows(sums[c], sublane)
        return carry

    lax.fori_loop(0, outs // group, body, 0)


def columns_times(acc, mat_ref, vec_ref, outs, terms, unroll=16):
    def body(t, acc):
        acc = [list(a) for a in acc]
        vecs = [
            jnp.broadcast_to(vec_ref[pl.ds(c * terms + t, 1), :], (8, vec_ref.shape[1]))
            for c in range(COMP)
        ]
        for j in range(outs // 8):
            tile = mat_ref[pl.ds(pl.multiple_of(t * outs + j * 8, 8), 8), :]
            for c in range(COMP):
                acc[c][j] = acc[c][j] + tile * vecs[c]
        return acc

    return lax.fori_loop(0, terms, body, acc, unroll=unroll)


def tiles_of(ref, outs):
    return [[ref[c * outs + t : c * outs + t + 8, :] for t in range(0, outs, 8)] for c in range(COMP)]


def zeros(outs, width):
    return [[jnp.zeros((8, width), F32) for _ in range(outs // 8)] for _ in range(COMP)]


def face_columns(acc):
    half = NODES // 8
    return jnp.concatenate(
        [
            jnp.concatenate(
                [acc[c][f * half + h] for c in range(COMP) for h in range(half)], axis=0
            )
            for f in range(FACES)
        ],
        axis=1,
    )


def start_kernel(
    ranks, inner, trace, owned, cap,
    mortar_hbm, kind_hbm, force_hbm, back_hbm, inverse_hbm, couple_hbm, self_hbm,
    own_ref, out_ref, onehot_ref, meta_ref, load_ref, inverse_ref, couple_ref, self_ref,
    mortar_ref, kind_ref, force_ref, back_ref, *sems,
):
    copies = [
        pltpu.make_async_copy(source, target, sem)
        for source, target, sem in zip(
            (mortar_hbm, kind_hbm, force_hbm, back_hbm, inverse_hbm, couple_hbm, self_hbm),
            (mortar_ref, kind_ref, force_ref, back_ref, inverse_ref, couple_ref, self_ref),
            sems,
        )
    ]
    for copy in copies:
        copy.start()
    copies[0].wait()
    copies[1].wait()
    width = mortar_ref.shape[1]
    slots = FACES * width
    mortar = mortar_ref[...]
    owner = lax.div(mortar, owned)
    index = lax.rem(mortar, owned)
    me = lax.rem(owner[0:1, 0:1] + 2, ranks)
    distance = lax.rem(owner - me + ranks, ranks)
    slot = lax.broadcasted_iota(jnp.int32, mortar.shape, 0) * width + lax.broadcasted_iota(
        jnp.int32, mortar.shape, 1
    )
    column = index
    begin = jnp.zeros((1, 1), jnp.int32)
    for number, away in enumerate((ranks - 2, ranks - 1, 0, 1, ranks // 2)):
        inside = distance == away
        count = jnp.sum(inside.astype(F32), keepdims=True).astype(jnp.int32)
        if away:
            run = number - (number > 2)
            column = jnp.where(inside, owned + run * cap + slot - begin, column)
        begin = begin + count
    target = lax.broadcasted_iota(jnp.int32, (1, slots), 1)
    target = lax.rem(target, width) * FACES + lax.div(target, width)
    order = jnp.where(
        lax.broadcasted_iota(jnp.int32, (slots, slots), 0) == target, 1.0, 0.0
    ).astype(BF16)
    facts = jnp.concatenate(
        [in_a_row(column), in_a_row(index + 1), in_a_row(kind_ref[...]), jnp.zeros((5, slots), jnp.int32)],
        axis=0,
    ).astype(F32)
    facts = exact_dot(facts, order)
    meta_ref[...] = facts
    meta_ref[3:4, :] = jnp.broadcast_to(lax.rem(me, 2).astype(F32), (1, slots))
    column = facts[0:1, :].astype(jnp.int32)
    onehot_ref[...] = jnp.where(
        lax.broadcasted_iota(jnp.int32, onehot_ref.shape, 0) == column, 1.0, 0.0
    ).astype(BF16)
    copies[2].wait()
    copies[4].wait()
    rows_times(inverse_ref, force_ref, load_ref, inner, inner)
    copies[3].wait()
    copies[5].wait()
    y = columns_times(zeros(trace, width), couple_ref, load_ref, trace, inner)
    z = by_kind(face_columns(y), back_ref, facts[2:3, :])
    label = jnp.where(
        lax.broadcasted_iota(jnp.int32, (8, slots), 0) == 0, facts[1:2, :], 0.0
    )
    sums = exact_dot(jnp.concatenate([z, label], axis=0), onehot_ref[...], 1)
    own_ref[...] = sums[: COMP * NODES, :owned]
    out_ref[...] = sums[:, owned:]
    copies[6].wait()


def merged(meta_ref, first, third, second, fourth, cap, to_owner):
    lane = lax.broadcasted_iota(jnp.int32, (1, RUNS * cap), 1)
    odd = meta_ref[3:4, : RUNS * cap] == 1.0
    low = lane < 2 * cap
    take_first = (low != odd) if to_owner else (low == odd)
    middle = jnp.where(take_first, first, second)
    return jnp.where(lane < cap, fourth, jnp.where(lane < 3 * cap, middle, third))


def owner_kernel(owned, cap, initial, meta_ref, label_ref, own_ref, a_ref, b_ref, c_ref, d_ref, *outs):
    received = merged(meta_ref, a_ref[...], b_ref[...], c_ref[...], d_ref[...], cap, True)
    rows = COMP * NODES
    if initial:
        field_ref, out_ref, label_out_ref = outs
        label = received[rows : rows + 8]
        label_out_ref[...] = label
    else:
        field_ref, out_ref = outs
        label = label_ref[...]
    wanted = (
        lax.broadcasted_iota(jnp.int32, (owned, RUNS * cap), 0)
        == label[0:1, :].astype(jnp.int32) - 1
    )
    wanted = jnp.where(wanted, 1.0, 0.0).astype(BF16)
    field = own_ref[...] + exact_dot(received[:rows], wanted, 1)
    field_ref[...] = field
    out_ref[...] = exact_dot(field, wanted)


def element_values(cap, meta_ref, onehot_ref, forth_ref, field_ref, blocks, spread_ref):
    received = merged(meta_ref, *[b[...] for b in blocks], cap, False)
    source = jnp.concatenate([field_ref[...], received], axis=1)
    kind = meta_ref[2:3, :]
    faces = by_kind(exact_dot(source, onehot_ref[...]), forth_ref, kind)
    width = spread_ref.shape[1]
    for c in range(COMP):
        for f in range(FACES):
            spread_ref[(c * FACES + f) * NODES : (c * FACES + f + 1) * NODES, :] = faces[
                c * NODES : (c + 1) * NODES, f * width : (f + 1) * width
            ]
    return kind


def apply_kernel(
    inner, trace, owned, cap,
    meta_ref, onehot_ref, forth_ref, back_ref, inverse_ref, couple_ref, self_ref,
    field_ref, a_ref, b_ref, c_ref, d_ref,
    own_ref, out_ref, spread_ref, mid_ref, weight_ref, image_ref,
):
    width = spread_ref.shape[1]
    kind = element_values(
        cap, meta_ref, onehot_ref, forth_ref, field_ref, (a_ref, b_ref, c_ref, d_ref), spread_ref
    )
    rows_times(couple_ref, spread_ref, mid_ref, inner, trace)
    rows_times(inverse_ref, mid_ref, weight_ref, inner, inner)
    rows_times(self_ref, spread_ref, image_ref, trace, trace)
    y = columns_times(tiles_of(image_ref, trace), couple_ref, weight_ref, trace, inner)
    z = by_kind(face_columns(y), back_ref, kind)
    sums = exact_dot(z, onehot_ref[...], 1)
    own_ref[...] = sums[:, :owned]
    out_ref[...] = sums[:, owned:]


def total(x):
    return jnp.sum(jnp.sum(x, axis=0, keepdims=True), axis=1, keepdims=True)


def last_kernel(
    inner, trace, cap,
    meta_ref, onehot_ref, forth_ref, inverse_ref, couple_ref, self_ref,
    k0_ref, k1_ref, k2_ref, a_ref, b_ref, c_ref, d_ref, s0_ref, s1_ref, u0_ref, u1_ref,
    weight_ref, moment_ref, spread_ref, mid_ref, image_ref,
):
    width = spread_ref.shape[1]
    element_values(
        cap, meta_ref, onehot_ref, forth_ref, k2_ref, (a_ref, b_ref, c_ref, d_ref), spread_ref
    )
    rows_times(couple_ref, spread_ref, mid_ref, inner, trace)
    rows_times(inverse_ref, mid_ref, weight_ref, inner, inner)
    rows_times(self_ref, spread_ref, image_ref, trace, trace)
    image, weight = image_ref[...], weight_ref[...]
    ks = (k0_ref[...], k1_ref[...], k2_ref[...])
    values = [total(ks[i] * ks[j]) for i in range(3) for j in range(i, 3)]
    for s_ref, u_ref in ((s0_ref, u0_ref), (s1_ref, u1_ref), (spread_ref, mid_ref)):
        values.append(total(s_ref[...] * image) + total(u_ref[...] * weight))
    lane = lax.broadcasted_iota(jnp.int32, (1, width), 1)
    row = jnp.zeros((1, width), F32)
    for number, value in enumerate(values):
        row = jnp.where(lane == number, value, row)
    moment_ref[...] = jnp.broadcast_to(row[None], moment_ref.shape)


def finish_kernel(
    moment_ref, k0_ref, k1_ref, k2_ref, w0_ref, w1_ref, w2_ref, load_ref, field_ref, interior_ref
):
    sums = jnp.sum(moment_ref[...], axis=0)
    m = [sums[:, n : n + 1] for n in range(9)]
    gram = [[m[0], m[1], m[2]], [m[1], m[3], m[4]], [m[2], m[4], m[5]]]
    energy = [[gram[i][1], gram[i][2], m[6 + i]] for i in range(3)]

    def form(x, matrix):
        return sum(x[i] * sum(matrix[i][j] * x[j] for j in range(3)) for i in range(3))

    zero, one = jnp.zeros((1, 1), F32), jnp.ones((1, 1), F32)
    x = [zero, zero, zero]
    r = [one, zero, zero]
    d = [one, zero, zero]
    current = gram[0][0]
    for iteration in range(3):
        step = current / form(d, energy)
        x = [x[i] + step * d[i] for i in range(3)]
        if iteration < 2:
            r = [r[0], r[1] - step * d[0], r[2] - step * d[1]]
            following = form(r, gram)
            d = [r[i] + following / current * d[i] for i in range(3)]
            current = following
    field_ref[...] = x[0] * k0_ref[...] + x[1] * k1_ref[...] + x[2] * k2_ref[...]
    interior_ref[...] = load_ref[...] - (
        x[0] * w0_ref[...] + x[1] * w1_ref[...] + x[2] * w2_ref[...]
    )


def call(kernel, outs, *args, scratch=(), in_hbm=0, vmem=8):
    inside = len(args) - in_hbm
    args = args[:inside] + tuple(
        pltpu.with_memory_space_constraint(x, pltpu.HBM) for x in args[inside:]
    )
    return pl.pallas_call(
        kernel,
        out_shape=[jax.ShapeDtypeStruct(shape, dtype) for shape, dtype in outs],
        in_specs=[pl.BlockSpec(memory_space=pltpu.VMEM)] * inside
        + [pl.BlockSpec(memory_space=pltpu.HBM)] * in_hbm,
        out_specs=[pl.BlockSpec(memory_space=pltpu.VMEM)] * len(outs),
        scratch_shapes=[pltpu.VMEM(shape, dtype) for shape, dtype in scratch]
        + [pltpu.SemaphoreType.DMA(())] * in_hbm,
        compiler_params=pltpu.CompilerParams(vmem_limit_bytes=vmem * 1024 * 1024),
    )(*args)


def exchange(block, ranks, to_owner):
    away = ranks - 2 if to_owner else 2
    pairs = [
        [(r, r ^ 1) for r in range(ranks)],
        [(r, (r + (1 if r % 2 else ranks - 1)) % ranks) for r in range(ranks)],
        [(r, (r + ranks // 2) % ranks) for r in range(ranks)],
        [(r, (r + away) % ranks) for r in range(ranks)],
    ]
    return [lax.ppermute(block, AXES, pairs[n]) for n in (0, 2, 1, 3)]


def local(self_block, couple, inverse, body_force, face_mortar, face_kind, *, ranks):
    trace, _, elements = self_block.shape
    inner = inverse.shape[0]
    owned = 2 * elements
    cap = max(2, elements // 4)
    width = elements
    rows = COMP * NODES
    forward, backward = block_tables()
    mortar = face_mortar.reshape(FACES, width)
    kind = face_kind.reshape(FACES, width)
    self_block = self_block.reshape(trace * trace, width)
    couple = couple.reshape(inner * trace, width)
    inverse = inverse.reshape(inner * inner, width)
    force = body_force.reshape(COMP * inner, width)

    own, out, onehot, meta, load, *matrices = call(
        functools.partial(start_kernel, ranks, inner, trace, owned, cap),
        [
            ((rows, owned), F32),
            ((rows + 8, RUNS * cap), F32),
            ((owned + RUNS * cap, FACES * width), BF16),
            ((8, FACES * width), F32),
            ((COMP * inner, width), F32),
            (inverse.shape, F32),
            (couple.shape, F32),
            (self_block.shape, F32),
        ],
        mortar, kind, force, backward, inverse, couple, self_block,
        scratch=[
            (mortar.shape, jnp.int32), (kind.shape, jnp.int32), (force.shape, F32), (backward.shape, F32)
        ],
        in_hbm=7, vmem=16,
    )
    blocks = exchange(out, ranks, True)
    field, out, label = call(
        functools.partial(owner_kernel, owned, cap, True),
        [((rows, owned), F32), ((rows, RUNS * cap), F32), ((8, RUNS * cap), F32)],
        meta, meta, own, *blocks,
    )
    fields, spreads, mids, weights = [field], [], [], []
    for _ in range(2):
        blocks = exchange(out, ranks, False)
        own, out, spread, mid, weight = call(
            functools.partial(apply_kernel, inner, trace, owned, cap),
            [
                ((rows, owned), F32),
                ((rows, RUNS * cap), F32),
                ((COMP * trace, width), F32),
                ((COMP * inner, width), F32),
                ((COMP * inner, width), F32),
            ],
            meta, onehot, forward, backward, *matrices, field, *blocks,
            scratch=[((COMP * trace, width), F32)],
        )
        spreads.append(spread)
        mids.append(mid)
        weights.append(weight)
        blocks = exchange(out, ranks, True)
        field, out = call(
            functools.partial(owner_kernel, owned, cap, False),
            [((rows, owned), F32), ((rows, RUNS * cap), F32)],
            meta, label, own, *blocks,
        )
        fields.append(field)
    blocks = exchange(out, ranks, False)
    weight, moments = call(
        functools.partial(last_kernel, inner, trace, cap),
        [((COMP * inner, width), F32), ((ranks, 1, width), F32)],
        meta, onehot, forward, *matrices, *fields, *blocks, *spreads, *mids,
        scratch=[
            ((COMP * trace, width), F32),
            ((COMP * inner, width), F32),
            ((COMP * trace, width), F32),
        ],
    )
    weights.append(weight)
    moments = lax.all_to_all(moments, AXES, split_axis=0, concat_axis=0, tiled=True)
    trace_field, interior = call(
        finish_kernel,
        [((rows, owned), F32), ((COMP * inner, width), F32)],
        moments, *fields, *weights, load,
    )
    return trace_field, interior.reshape(COMP, inner, elements)


def solution(mesh):
    placed = (
        P(None, None, AXES),
        P(None, None, AXES),
        P(None, None, AXES),
        P(None, None, AXES),
        P(AXES),
        P(AXES),
    )
    ranks = int(np.prod([mesh.shape[a] for a in AXES]))
    return jax.shard_map(
        functools.partial(local, ranks=ranks),
        mesh=mesh,
        in_specs=placed,
        out_specs=(P(None, AXES), P(None, None, AXES)),
        check_vma=False,
    )
```

```python
import functools

import jax
import jax.numpy as jnp
import numpy as np
from jax import lax
from jax.experimental import pallas as pl
from jax.experimental.pallas import tpu as pltpu
from jax.sharding import PartitionSpec as P

AXES = ("dom", "blk")
COMP = 3
NODES = 16
FACES = 6
RUNS = 4
F32 = jnp.float32
BF16 = jnp.bfloat16


def interp_tables():
    abscissae = -np.cos(np.pi * np.arange(4) / 3.0)

    def lagrange(points):
        columns = [
            np.prod(
                [
                    (points - abscissae[other_node])
                    / (abscissae[basis_node] - abscissae[other_node])
                    for other_node in range(4)
                    if other_node != basis_node
                ],
                axis=0,
            )
            for basis_node in range(4)
        ]
        return np.stack(columns, axis=1)

    lower_map = lagrange((abscissae - 1.0) / 2.0)
    upper_map = lagrange((abscissae + 1.0) / 2.0)
    return np.stack(
        [
            np.kron(lower_map, lower_map),
            np.kron(lower_map, upper_map),
            np.kron(upper_map, lower_map),
            np.kron(upper_map, upper_map),
        ]
    ).astype(np.float32)


def block_tables():
    tables = interp_tables()
    eye = np.eye(COMP, dtype=np.float32)
    forward = np.concatenate([np.kron(eye, t) for t in tables])
    backward = np.concatenate([np.kron(eye, t.T) for t in tables])
    return forward, backward


def split(x):
    hi = x.astype(BF16)
    return hi, (x - hi.astype(F32)).astype(BF16)


def dot(a, b, rhs_dim=0):
    return lax.dot_general(a, b, (((1,), (rhs_dim,)), ((), ())), preferred_element_type=F32)


def exact_dot(x, onehot, rhs_dim=0):
    hi, lo = split(x)
    both = dot(jnp.concatenate([hi, lo], axis=0), onehot, rhs_dim)
    return both[: x.shape[0]] + both[x.shape[0] :]


def by_kind(x, table_ref, kind):
    rows = x.shape[0]
    t_hi, t_lo = split(table_ref[...])
    x_hi, x_lo = split(x)
    mapped = dot(
        jnp.concatenate([t_hi, t_hi, t_lo], axis=1), jnp.concatenate([x_hi, x_lo, x_hi], axis=0)
    )
    for number in range(4):
        x = jnp.where(kind == number + 1, mapped[number * rows : (number + 1) * rows], x)
    return x


def in_a_row(x):
    return jnp.concatenate([x[r : r + 1, :] for r in range(x.shape[0])], axis=1)


def gather_rows(tiles, sublane):
    tiles = [tiles[r] for r in (0, 4, 2, 6, 1, 5, 3, 7)]
    keep = (sublane & 4) == 0
    tiles = [
        jnp.where(keep, x, y) + pltpu.roll(jnp.where(keep, y, x), 4, 0)
        for x, y in zip(tiles[::2], tiles[1::2])
    ]
    for shift in (2, 1):
        keep = (sublane & shift) == 0
        tiles = [
            jnp.where(keep, x + pltpu.roll(x, 8 - shift, 0), y + pltpu.roll(y, shift, 0))
            for x, y in zip(tiles[::2], tiles[1::2])
        ]
    return tiles[0]


def rows_times(mat_ref, vec_ref, out_ref, outs, terms, group=32):
    width = vec_ref.shape[1]
    sublane = lax.broadcasted_iota(jnp.int32, (8, width), 0)
    vecs = [
        [vec_ref[c * terms + t : c * terms + t + 8, :] for t in range(0, terms, 8)]
        for c in range(COMP)
    ]

    def body(g, carry):
        for first in range(0, group, 8):
            sums = [[] for _ in range(COMP)]
            for r in range(first, first + 8):
                acc = [None] * COMP
                for j in range(terms // 8):
                    start = pl.multiple_of((g * group + r) * terms + 8 * j, 8)
                    tile = mat_ref[pl.ds(start, 8), :]
                    for c in range(COMP):
                        term = tile * vecs[c][j]
                        acc[c] = term if j == 0 else acc[c] + term
                for c in range(COMP):
                    sums[c].append(acc[c])
            for c in range(COMP):
                start = pl.multiple_of(c * outs + g * group + first, 8)
                out_ref[pl.ds(start, 8), :] = gather_rows(sums[c], sublane)
        return carry

    lax.fori_loop(0, outs // group, body, 0)


def columns_times(acc, mat_ref, vec_ref, outs, terms, unroll=16):
    def body(t, acc):
        acc = [list(a) for a in acc]
        vecs = [
            jnp.broadcast_to(vec_ref[pl.ds(c * terms + t, 1), :], (8, vec_ref.shape[1]))
            for c in range(COMP)
        ]
        for j in range(outs // 8):
            tile = mat_ref[pl.ds(pl.multiple_of(t * outs + j * 8, 8), 8), :]
            for c in range(COMP):
                acc[c][j] = acc[c][j] + tile * vecs[c]
        return acc

    return lax.fori_loop(0, terms, body, acc, unroll=unroll)


def tiles_of(ref, outs):
    return [[ref[c * outs + t : c * outs + t + 8, :] for t in range(0, outs, 8)] for c in range(COMP)]


def zeros(outs, width):
    return [[jnp.zeros((8, width), F32) for _ in range(outs // 8)] for _ in range(COMP)]


def face_columns(acc):
    half = NODES // 8
    return jnp.concatenate(
        [
            jnp.concatenate(
                [acc[c][f * half + h] for c in range(COMP) for h in range(half)], axis=0
            )
            for f in range(FACES)
        ],
        axis=1,
    )


def start_kernel(
    ranks, inner, trace, owned, cap,
    mortar_hbm, kind_hbm, force_hbm, back_hbm, inverse_hbm, couple_hbm, self_hbm,
    own_ref, out_ref, gid_ref, onehot_ref, meta_ref, load_ref, inverse_ref, couple_ref, self_ref,
    mortar_ref, kind_ref, force_ref, back_ref, *sems,
):
    copies = [
        pltpu.make_async_copy(source, target, sem)
        for source, target, sem in zip(
            (mortar_hbm, kind_hbm, force_hbm, back_hbm, inverse_hbm, couple_hbm, self_hbm),
            (mortar_ref, kind_ref, force_ref, back_ref, inverse_ref, couple_ref, self_ref),
            sems,
        )
    ]
    for copy in copies:
        copy.start()
    copies[0].wait()
    copies[1].wait()
    width = mortar_ref.shape[1]
    slots = FACES * width
    mortar = mortar_ref[...]
    owner = lax.div(mortar, owned)
    index = lax.rem(mortar, owned)
    me = lax.rem(owner[0:1, 0:1] + 2, ranks)
    distance = lax.rem(owner - me + ranks, ranks)
    slot = lax.broadcasted_iota(jnp.int32, mortar.shape, 0) * width + lax.broadcasted_iota(
        jnp.int32, mortar.shape, 1
    )
    column = index
    begin = jnp.zeros((1, 1), jnp.int32)
    for number, away in enumerate((ranks - 2, ranks - 1, 0, 1, ranks // 2)):
        inside = distance == away
        count = jnp.sum(inside.astype(F32), keepdims=True).astype(jnp.int32)
        if away:
            run = number - (number > 2)
            column = jnp.where(inside, owned + run * cap + slot - begin, column)
        begin = begin + count
    target = lax.broadcasted_iota(jnp.int32, (1, slots), 1)
    target = lax.rem(target, width) * FACES + lax.div(target, width)
    order = jnp.where(
        lax.broadcasted_iota(jnp.int32, (slots, slots), 0) == target, 1.0, 0.0
    ).astype(BF16)
    facts = jnp.concatenate(
        [in_a_row(column), in_a_row(mortar + 1), in_a_row(kind_ref[...]), jnp.zeros((5, slots), jnp.int32)],
        axis=0,
    ).astype(F32)
    facts = exact_dot(facts, order)
    meta_ref[...] = facts
    meta_ref[3:4, :] = jnp.broadcast_to(lax.rem(me, 2).astype(F32), (1, slots))
    meta_ref[4:5, :] = jnp.broadcast_to((me * owned).astype(F32), (1, slots))
    column = facts[0:1, :].astype(jnp.int32)
    onehot_ref[...] = jnp.where(
        lax.broadcasted_iota(jnp.int32, onehot_ref.shape, 0) == column, 1.0, 0.0
    ).astype(BF16)
    copies[2].wait()
    copies[4].wait()
    rows_times(inverse_ref, force_ref, load_ref, inner, inner)
    copies[3].wait()
    copies[5].wait()
    y = columns_times(zeros(trace, width), couple_ref, load_ref, trace, inner)
    z = by_kind(face_columns(y), back_ref, facts[2:3, :])
    label = jnp.where(
        lax.broadcasted_iota(jnp.int32, (8, slots), 0) == 0, facts[1:2, :], 0.0
    )
    sums = exact_dot(jnp.concatenate([z, label], axis=0), onehot_ref[...], 1)
    own_ref[...] = sums[: COMP * NODES, :owned]
    out_ref[...] = sums[:, owned:]
    gid_ref[...] = sums[COMP * NODES :, owned:]
    copies[6].wait()


def merged(meta_ref, first, third, second, fourth, cap, to_owner):
    lane = lax.broadcasted_iota(jnp.int32, (1, RUNS * cap), 1)
    odd = meta_ref[3:4, : RUNS * cap] == 1.0
    low = lane < 2 * cap
    take_first = (low != odd) if to_owner else (low == odd)
    middle = jnp.where(take_first, first, second)
    return jnp.where(lane < cap, fourth, jnp.where(lane < 3 * cap, middle, third))


def onehot_of(condition):
    return jnp.where(condition, 1.0, 0.0).astype(BF16)


def own_ids(meta_ref, owned, count):
    base = meta_ref[4:5, :count].astype(jnp.int32)
    return lax.broadcasted_iota(jnp.int32, (owned, count), 0) + base + 1


def wanted_by(label, meta_ref, owned):
    count = label.shape[1]
    return onehot_of(own_ids(meta_ref, owned, count) == label.astype(jnp.int32))


def owner_kernel(owned, cap, meta_ref, own_ref, a_ref, b_ref, c_ref, d_ref, field_ref, out_ref, label_ref):
    received = merged(meta_ref, a_ref[...], b_ref[...], c_ref[...], d_ref[...], cap, True)
    rows = COMP * NODES
    label_ref[...] = received[rows : rows + 8]
    wanted = wanted_by(received[rows : rows + 1], meta_ref, owned)
    field = own_ref[...] + exact_dot(received[:rows], wanted, 1)
    field_ref[...] = field
    out_ref[...] = exact_dot(field, wanted)


def share(owned, sums, gid_ref, label_ref, meta_ref, own_ref, shared_ref):
    rows = COMP * NODES
    own = sums[:, :owned]
    own_ref[...] = own
    shared_ref[:rows, :] = sums[:, owned:]
    label = label_ref[0:1, :]
    shared_ref[rows : 2 * rows, :] = exact_dot(own, wanted_by(label, meta_ref, owned))
    row = lax.broadcasted_iota(jnp.int32, gid_ref.shape, 0)
    shared_ref[2 * rows :, :] = jnp.where(
        row == 0, gid_ref[0:1, :], jnp.where(row == 1, label, 0.0)
    )


def ids_down(ids, count):
    return jnp.broadcast_to(jnp.transpose(jnp.broadcast_to(ids, (8, ids.shape[1])))[:, 0:1], (ids.shape[1], count))


def pack_kernel(cap, meta_ref, mine_ref, other_ref, one_ref, two_ref, three_ref, four_ref):
    rows = COMP * NODES
    count = RUNS * cap
    odd = meta_ref[3:4, :count] == 1.0
    mine, other = mine_ref[...], other_ref[...]
    even_part = jnp.where(odd, other, mine)
    odd_part = jnp.where(odd, mine, other)
    source = jnp.concatenate([even_part[:rows], odd_part[:rows]], axis=1)
    gids = jnp.concatenate([even_part[2 * rows : 2 * rows + 1], odd_part[2 * rows : 2 * rows + 1]], axis=1)
    blank = jnp.zeros((8, count), F32)
    sums = []
    for part in (even_part, odd_part):
        label = part[2 * rows + 1 : 2 * rows + 2]
        match = onehot_of((ids_down(label, 2 * count) == gids) & (gids > 0.0))
        full = part[rows : 2 * rows] + exact_dot(source, match, 1)
        sums.append(jnp.concatenate([full, blank], axis=0))
    outs = [
        jnp.concatenate([part[:rows], part[2 * rows : 2 * rows + 1], blank[1:]], axis=0)
        for part in (even_part, odd_part)
    ]
    lane = lax.broadcasted_iota(jnp.int32, (1, count), 1)

    def laid(*blocks):
        result = jnp.zeros((rows + 8, count), F32)
        for place, block in enumerate(blocks):
            if block is not None:
                array, run = block
                if run != place:
                    array = pltpu.roll(array, ((place - run) % RUNS) * cap, 1)
                inside = (lane >= place * cap) & (lane < (place + 1) * cap)
                result = jnp.where(inside, array, result)
        return result

    (oe, oo), (ge, go) = outs, sums
    one_ref[...] = jnp.where(
        odd, laid((oe, 0), (oe, 1), (ge, 2), (oo, 0)), laid((ge, 0), (go, 1), (oo, 2), (go, 0))
    )
    two_ref[...] = jnp.where(odd, laid((oe, 0)), laid(None, None, (oo, 2)))
    three_ref[...] = jnp.where(
        odd, laid((oo, 3), None, (oo, 2), (oe, 3)), laid((oe, 0), (oe, 1), (oo, 0), (oe, 3))
    )
    four_ref[...] = laid((jnp.where(odd, oo, oe), 3), None, None, (jnp.where(odd, go, ge), 3))


def fused_values(owned, cap, meta_ref, own_ref, mine_ref, other_ref, got, passed):
    rows = COMP * NODES
    count = RUNS * cap
    lane = lax.broadcasted_iota(jnp.int32, (1, count), 1)
    odd = meta_ref[3:4, :count] == 1.0
    mine, other = mine_ref[...], other_ref[...]
    blocks = [r[...] for r in (*got, *passed)]
    source = jnp.concatenate([mine[:rows], other[:rows]] + [x[:rows] for x in blocks], axis=1)
    gids = jnp.concatenate(
        [mine[2 * rows : 2 * rows + 1], other[2 * rows : 2 * rows + 1]]
        + [x[rows : rows + 1] for x in blocks],
        axis=1,
    )
    total_count = gids.shape[1]
    remote = ids_down(mine[2 * rows : 2 * rows + 1], total_count)
    own = lax.broadcasted_iota(jnp.int32, (owned, total_count), 0).astype(F32) + (
        meta_ref[4:5, 0:1] + 1.0
    )
    match = onehot_of(jnp.concatenate([own, jnp.where(remote > 0.0, remote, -1.0)], axis=0) == gids)
    sums = exact_dot(source, match, 1)
    field = own_ref[...] + sums[:, :owned]
    near, far = got[0][...][:rows], got[3][...][:rows]
    across = passed[0][...][:rows]
    partner = other[rows : 2 * rows]
    even_form = jnp.where(lane < 2 * cap, across, jnp.where(lane < 3 * cap, partner, far))
    odd_form = jnp.where(
        lane < cap,
        pltpu.roll(near, cap, 1),
        jnp.where(lane < 2 * cap, partner, jnp.where(lane < 3 * cap, across, far)),
    )
    return field, jnp.where(odd, odd_form, even_form) + sums[:, owned:]


def element_values(field, received, meta_ref, onehot_ref, forth_ref, spread_ref):
    source = jnp.concatenate([field, received], axis=1)
    kind = meta_ref[2:3, :]
    faces = by_kind(exact_dot(source, onehot_ref[...]), forth_ref, kind)
    width = spread_ref.shape[1]
    for c in range(COMP):
        for f in range(FACES):
            spread_ref[(c * FACES + f) * NODES : (c * FACES + f + 1) * NODES, :] = faces[
                c * NODES : (c + 1) * NODES, f * width : (f + 1) * width
            ]
    return kind


def apply_kernel(
    inner, trace, owned, cap, fused,
    meta_ref, onehot_ref, forth_ref, back_ref, gid_ref, label_ref, inverse_ref, couple_ref, self_ref,
    *refs,
):
    if fused:
        before_ref, mine_ref, other_ref, *received = refs[:11]
        refs = refs[11:]
        field_ref, refs = refs[0], refs[1:]
        field, received = fused_values(
            owned, cap, meta_ref, before_ref, mine_ref, other_ref, received[:4], received[4:]
        )
        field_ref[...] = field
    else:
        field = refs[0][...]
        received = merged(meta_ref, *[r[...] for r in refs[1:5]], cap, False)
        refs = refs[5:]
    own_ref, shared_ref, spread_ref, mid_ref, weight_ref, image_ref = refs
    width = spread_ref.shape[1]
    kind = element_values(field, received, meta_ref, onehot_ref, forth_ref, spread_ref)
    rows_times(couple_ref, spread_ref, mid_ref, inner, trace)
    rows_times(inverse_ref, mid_ref, weight_ref, inner, inner)
    rows_times(self_ref, spread_ref, image_ref, trace, trace)
    y = columns_times(tiles_of(image_ref, trace), couple_ref, weight_ref, trace, inner)
    z = by_kind(face_columns(y), back_ref, kind)
    sums = exact_dot(z, onehot_ref[...], 1)
    share(owned, sums, gid_ref, label_ref, meta_ref, own_ref, shared_ref)


def total(x):
    return jnp.sum(jnp.sum(x, axis=0, keepdims=True), axis=1, keepdims=True)


def last_kernel(
    inner, trace, owned, cap,
    meta_ref, onehot_ref, forth_ref, inverse_ref, couple_ref, self_ref,
    k0_ref, k1_ref, s0_ref, s1_ref, u0_ref, u1_ref, before_ref, mine_ref, other_ref, *refs,
):
    received, refs = refs[:8], refs[8:]
    k2_ref, weight_ref, moment_ref, spread_ref, mid_ref, image_ref = refs
    width = spread_ref.shape[1]
    field, received = fused_values(
        owned, cap, meta_ref, before_ref, mine_ref, other_ref, received[:4], received[4:]
    )
    k2_ref[...] = field
    element_values(field, received, meta_ref, onehot_ref, forth_ref, spread_ref)
    rows_times(couple_ref, spread_ref, mid_ref, inner, trace)
    rows_times(inverse_ref, mid_ref, weight_ref, inner, inner)
    rows_times(self_ref, spread_ref, image_ref, trace, trace)
    image, weight = image_ref[...], weight_ref[...]
    ks = (k0_ref[...], k1_ref[...], field)
    values = [total(ks[i] * ks[j]) for i in range(3) for j in range(i, 3)]
    for s_ref, u_ref in ((s0_ref, u0_ref), (s1_ref, u1_ref), (spread_ref, mid_ref)):
        values.append(total(s_ref[...] * image) + total(u_ref[...] * weight))
    lane = lax.broadcasted_iota(jnp.int32, (1, width), 1)
    row = jnp.zeros((1, width), F32)
    for number, value in enumerate(values):
        row = jnp.where(lane == number, value, row)
    moment_ref[...] = jnp.broadcast_to(row[None], moment_ref.shape)


def finish_kernel(
    moment_ref, k0_ref, k1_ref, k2_ref, w0_ref, w1_ref, w2_ref, load_ref, field_ref, interior_ref
):
    sums = jnp.sum(moment_ref[...], axis=0)
    m = [sums[:, n : n + 1] for n in range(9)]
    gram = [[m[0], m[1], m[2]], [m[1], m[3], m[4]], [m[2], m[4], m[5]]]
    energy = [[gram[i][1], gram[i][2], m[6 + i]] for i in range(3)]

    def form(x, matrix):
        return sum(x[i] * sum(matrix[i][j] * x[j] for j in range(3)) for i in range(3))

    zero, one = jnp.zeros((1, 1), F32), jnp.ones((1, 1), F32)
    x = [zero, zero, zero]
    r = [one, zero, zero]
    d = [one, zero, zero]
    current = gram[0][0]
    for iteration in range(3):
        step = current / form(d, energy)
        x = [x[i] + step * d[i] for i in range(3)]
        if iteration < 2:
            r = [r[0], r[1] - step * d[0], r[2] - step * d[1]]
            following = form(r, gram)
            d = [r[i] + following / current * d[i] for i in range(3)]
            current = following
    field_ref[...] = x[0] * k0_ref[...] + x[1] * k1_ref[...] + x[2] * k2_ref[...]
    interior_ref[...] = load_ref[...] - (
        x[0] * w0_ref[...] + x[1] * w1_ref[...] + x[2] * w2_ref[...]
    )


def call(kernel, outs, *args, scratch=(), in_hbm=0, vmem=8):
    inside = len(args) - in_hbm
    args = args[:inside] + tuple(
        pltpu.with_memory_space_constraint(x, pltpu.HBM) for x in args[inside:]
    )
    return pl.pallas_call(
        kernel,
        out_shape=[jax.ShapeDtypeStruct(shape, dtype) for shape, dtype in outs],
        in_specs=[pl.BlockSpec(memory_space=pltpu.VMEM)] * inside
        + [pl.BlockSpec(memory_space=pltpu.HBM)] * in_hbm,
        out_specs=[pl.BlockSpec(memory_space=pltpu.VMEM)] * len(outs),
        scratch_shapes=[pltpu.VMEM(shape, dtype) for shape, dtype in scratch]
        + [pltpu.SemaphoreType.DMA(())] * in_hbm,
        compiler_params=pltpu.CompilerParams(vmem_limit_bytes=vmem * 1024 * 1024),
    )(*args)


def exchange(block, ranks, to_owner):
    away = ranks - 2 if to_owner else 2
    pairs = [
        [(r, r ^ 1) for r in range(ranks)],
        [(r, (r + (1 if r % 2 else ranks - 1)) % ranks) for r in range(ranks)],
        [(r, (r + ranks // 2) % ranks) for r in range(ranks)],
        [(r, (r + away) % ranks) for r in range(ranks)],
    ]
    return [lax.ppermute(block, AXES, pairs[n]) for n in (0, 2, 1, 3)]


def fused_exchange(cap, meta, shared, ranks):
    pair = [(r, r ^ 1) for r in range(ranks)]

    def both_ways(chips):
        ahead = [(r, (r + 2 * chips + 1) % ranks) for r in range(0, ranks, 2)]
        return ahead + [(t, r) for r, t in ahead]

    other = lax.ppermute(shared, AXES, pair)
    shape = (COMP * NODES + 8, RUNS * cap)
    packed = call(
        functools.partial(pack_kernel, cap), [(shape, F32)] * 4, meta, shared, other
    )
    ways = [
        both_ways(1),
        both_ways(2),
        both_ways(ranks // 4 - 1),
        [(r, (r + ranks // 2) % ranks) for r in range(ranks)],
    ]
    got = [lax.ppermute(block, AXES, way) for block, way in zip(packed, ways)]
    passed = [lax.ppermute(block, AXES, pair) for block in got]
    return [shared, other, *got, *passed]


def local(self_block, couple, inverse, body_force, face_mortar, face_kind, *, ranks):
    trace, _, elements = self_block.shape
    inner = inverse.shape[0]
    owned = 2 * elements
    cap = max(2, elements // 4)
    width = elements
    rows = COMP * NODES
    forward, backward = block_tables()
    mortar = face_mortar.reshape(FACES, width)
    kind = face_kind.reshape(FACES, width)
    self_block = self_block.reshape(trace * trace, width)
    couple = couple.reshape(inner * trace, width)
    inverse = inverse.reshape(inner * inner, width)
    force = body_force.reshape(COMP * inner, width)

    own, out, gid, onehot, meta, load, *matrices = call(
        functools.partial(start_kernel, ranks, inner, trace, owned, cap),
        [
            ((rows, owned), F32),
            ((rows + 8, RUNS * cap), F32),
            ((8, RUNS * cap), F32),
            ((owned + RUNS * cap, FACES * width), BF16),
            ((8, FACES * width), F32),
            ((COMP * inner, width), F32),
            (inverse.shape, F32),
            (couple.shape, F32),
            (self_block.shape, F32),
        ],
        mortar, kind, force, backward, inverse, couple, self_block,
        scratch=[
            (mortar.shape, jnp.int32), (kind.shape, jnp.int32), (force.shape, F32), (backward.shape, F32)
        ],
        in_hbm=7, vmem=16,
    )
    blocks = exchange(out, ranks, True)
    field, out, label = call(
        functools.partial(owner_kernel, owned, cap),
        [((rows, owned), F32), ((rows, RUNS * cap), F32), ((8, RUNS * cap), F32)],
        meta, own, *blocks,
    )
    blocks = exchange(out, ranks, False)
    fields, spreads, mids, weights = [field], [], [], []
    for iteration in range(2):
        fused = iteration > 0
        first = [((rows, owned), F32)] if fused else []
        results = call(
            functools.partial(apply_kernel, inner, trace, owned, cap, fused),
            first + [
                ((rows, owned), F32),
                ((2 * rows + 8, RUNS * cap), F32),
                ((COMP * trace, width), F32),
                ((COMP * inner, width), F32),
                ((COMP * inner, width), F32),
            ],
            meta, onehot, forward, backward, gid, label, *matrices, own if fused else field, *blocks,
            scratch=[((COMP * trace, width), F32)],
        )
        fields += results[: len(first)]
        own, shared, spread, mid, weight = results[len(first) :]
        spreads.append(spread)
        mids.append(mid)
        weights.append(weight)
        blocks = fused_exchange(cap, meta, shared, ranks)
    field, weight, moments = call(
        functools.partial(last_kernel, inner, trace, owned, cap),
        [((rows, owned), F32), ((COMP * inner, width), F32), ((ranks, 1, width), F32)],
        meta, onehot, forward, *matrices, *fields, *spreads, *mids, own, *blocks,
        scratch=[
            ((COMP * trace, width), F32),
            ((COMP * inner, width), F32),
            ((COMP * trace, width), F32),
        ],
    )
    fields.append(field)
    weights.append(weight)
    moments = lax.all_to_all(moments, AXES, split_axis=0, concat_axis=0, tiled=True)
    trace_field, interior = call(
        finish_kernel,
        [((rows, owned), F32), ((COMP * inner, width), F32)],
        moments, *fields, *weights, load,
    )
    return trace_field, interior.reshape(COMP, inner, elements)


def solution(mesh):
    placed = (
        P(None, None, AXES),
        P(None, None, AXES),
        P(None, None, AXES),
        P(None, None, AXES),
        P(AXES),
        P(AXES),
    )
    ranks = int(np.prod([mesh.shape[a] for a in AXES]))
    return jax.shard_map(
        functools.partial(local, ranks=ranks),
        mesh=mesh,
        in_specs=placed,
        out_specs=(P(None, AXES), P(None, None, AXES)),
        check_vma=False,
    )
```

```python
import functools

import jax
import jax.numpy as jnp
import numpy as np
from jax import lax
from jax.experimental import pallas as pl
from jax.experimental.pallas import tpu as pltpu
from jax.sharding import PartitionSpec as P

AXES = ("dom", "blk")
COMP = 3
NODES = 16
FACES = 6
RUNS = 4
F32 = jnp.float32
BF16 = jnp.bfloat16


def interp_tables():
    abscissae = -np.cos(np.pi * np.arange(4) / 3.0)

    def lagrange(points):
        columns = [
            np.prod(
                [
                    (points - abscissae[other_node])
                    / (abscissae[basis_node] - abscissae[other_node])
                    for other_node in range(4)
                    if other_node != basis_node
                ],
                axis=0,
            )
            for basis_node in range(4)
        ]
        return np.stack(columns, axis=1)

    lower_map = lagrange((abscissae - 1.0) / 2.0)
    upper_map = lagrange((abscissae + 1.0) / 2.0)
    return np.stack(
        [
            np.kron(lower_map, lower_map),
            np.kron(lower_map, upper_map),
            np.kron(upper_map, lower_map),
            np.kron(upper_map, upper_map),
        ]
    ).astype(np.float32)


def block_tables():
    tables = interp_tables()
    eye = np.eye(COMP, dtype=np.float32)
    forward = np.concatenate([np.kron(eye, t) for t in tables])
    backward = np.concatenate([np.kron(eye, t.T) for t in tables])
    return forward, backward


def split(x):
    hi = x.astype(BF16)
    return hi, (x - hi.astype(F32)).astype(BF16)


def dot(a, b, rhs_dim=0):
    return lax.dot_general(a, b, (((1,), (rhs_dim,)), ((), ())), preferred_element_type=F32)


def exact_dot(x, onehot, rhs_dim=0):
    hi, lo = split(x)
    both = dot(jnp.concatenate([hi, lo], axis=0), onehot, rhs_dim)
    return both[: x.shape[0]] + both[x.shape[0] :]


def by_kind(x, table_ref, kind):
    rows = x.shape[0]
    t_hi, t_lo = split(table_ref[...])
    x_hi, x_lo = split(x)
    mapped = dot(
        jnp.concatenate([t_hi, t_hi, t_lo], axis=1), jnp.concatenate([x_hi, x_lo, x_hi], axis=0)
    )
    for number in range(4):
        x = jnp.where(kind == number + 1, mapped[number * rows : (number + 1) * rows], x)
    return x


def in_a_row(x):
    return jnp.concatenate([x[r : r + 1, :] for r in range(x.shape[0])], axis=1)


def gather_rows(tiles, sublane):
    tiles = [tiles[r] for r in (0, 4, 2, 6, 1, 5, 3, 7)]
    keep = (sublane & 4) == 0
    tiles = [
        jnp.where(keep, x, y) + pltpu.roll(jnp.where(keep, y, x), 4, 0)
        for x, y in zip(tiles[::2], tiles[1::2])
    ]
    for shift in (2, 1):
        keep = (sublane & shift) == 0
        tiles = [
            jnp.where(keep, x + pltpu.roll(x, 8 - shift, 0), y + pltpu.roll(y, shift, 0))
            for x, y in zip(tiles[::2], tiles[1::2])
        ]
    return tiles[0]


def rows_times(mat_ref, vec_ref, out_ref, outs, terms, group=32):
    width = vec_ref.shape[1]
    sublane = lax.broadcasted_iota(jnp.int32, (8, width), 0)
    vecs = [
        [vec_ref[c * terms + t : c * terms + t + 8, :] for t in range(0, terms, 8)]
        for c in range(COMP)
    ]

    def body(g, carry):
        for first in range(0, group, 8):
            sums = [[] for _ in range(COMP)]
            for r in range(first, first + 8):
                acc = [None] * COMP
                for j in range(terms // 8):
                    start = pl.multiple_of((g * group + r) * terms + 8 * j, 8)
                    tile = mat_ref[pl.ds(start, 8), :]
                    for c in range(COMP):
                        term = tile * vecs[c][j]
                        acc[c] = term if j == 0 else acc[c] + term
                for c in range(COMP):
                    sums[c].append(acc[c])
            for c in range(COMP):
                start = pl.multiple_of(c * outs + g * group + first, 8)
                out_ref[pl.ds(start, 8), :] = gather_rows(sums[c], sublane)
        return carry

    lax.fori_loop(0, outs // group, body, 0)


def columns_times(acc, mat_ref, vec_ref, outs, terms, unroll=16):
    def body(t, acc):
        acc = [list(a) for a in acc]
        vecs = [
            jnp.broadcast_to(vec_ref[pl.ds(c * terms + t, 1), :], (8, vec_ref.shape[1]))
            for c in range(COMP)
        ]
        for j in range(outs // 8):
            tile = mat_ref[pl.ds(pl.multiple_of(t * outs + j * 8, 8), 8), :]
            for c in range(COMP):
                acc[c][j] = acc[c][j] + tile * vecs[c]
        return acc

    return lax.fori_loop(0, terms, body, acc, unroll=unroll)


def tiles_of(ref, outs):
    return [[ref[c * outs + t : c * outs + t + 8, :] for t in range(0, outs, 8)] for c in range(COMP)]


def zeros(outs, width):
    return [[jnp.zeros((8, width), F32) for _ in range(outs // 8)] for _ in range(COMP)]


def face_columns(acc):
    half = NODES // 8
    return jnp.concatenate(
        [
            jnp.concatenate(
                [acc[c][f * half + h] for c in range(COMP) for h in range(half)], axis=0
            )
            for f in range(FACES)
        ],
        axis=1,
    )


def start_kernel(
    ranks, inner, trace, owned, cap,
    mortar_hbm, kind_hbm, force_hbm, back_hbm, inverse_hbm, couple_hbm, self_hbm,
    own_ref, out_ref, gid_ref, onehot_ref, meta_ref, load_ref, inverse_ref, couple_ref, self_ref,
    mortar_ref, kind_ref, force_ref, back_ref, *sems,
):
    copies = [
        pltpu.make_async_copy(source, target, sem)
        for source, target, sem in zip(
            (mortar_hbm, kind_hbm, force_hbm, back_hbm, inverse_hbm, couple_hbm, self_hbm),
            (mortar_ref, kind_ref, force_ref, back_ref, inverse_ref, couple_ref, self_ref),
            sems,
        )
    ]
    for copy in copies:
        copy.start()
    copies[0].wait()
    copies[1].wait()
    width = mortar_ref.shape[1]
    slots = FACES * width
    mortar = mortar_ref[...]
    owner = lax.div(mortar, owned)
    index = lax.rem(mortar, owned)
    me = lax.rem(owner[0:1, 0:1] + 2, ranks)
    distance = lax.rem(owner - me + ranks, ranks)
    slot = lax.broadcasted_iota(jnp.int32, mortar.shape, 0) * width + lax.broadcasted_iota(
        jnp.int32, mortar.shape, 1
    )
    column = index
    begin = jnp.zeros((1, 1), jnp.int32)
    for number, away in enumerate((ranks - 2, ranks - 1, 0, 1, ranks // 2)):
        inside = distance == away
        count = jnp.sum(inside.astype(F32), keepdims=True).astype(jnp.int32)
        if away:
            run = number - (number > 2)
            column = jnp.where(inside, owned + run * cap + slot - begin, column)
        begin = begin + count
    target = lax.broadcasted_iota(jnp.int32, (1, slots), 1)
    target = lax.rem(target, width) * FACES + lax.div(target, width)
    order = jnp.where(
        lax.broadcasted_iota(jnp.int32, (slots, slots), 0) == target, 1.0, 0.0
    ).astype(BF16)
    facts = jnp.concatenate(
        [in_a_row(column), in_a_row(mortar + 1), in_a_row(kind_ref[...]), jnp.zeros((5, slots), jnp.int32)],
        axis=0,
    ).astype(F32)
    facts = exact_dot(facts, order)
    meta_ref[...] = facts
    meta_ref[3:4, :] = jnp.broadcast_to(lax.rem(me, 2).astype(F32), (1, slots))
    meta_ref[4:5, :] = jnp.broadcast_to((me * owned).astype(F32), (1, slots))
    column = facts[0:1, :].astype(jnp.int32)
    onehot_ref[...] = jnp.where(
        lax.broadcasted_iota(jnp.int32, onehot_ref.shape, 0) == column, 1.0, 0.0
    ).astype(BF16)
    copies[2].wait()
    copies[4].wait()
    rows_times(inverse_ref, force_ref, load_ref, inner, inner)
    copies[3].wait()
    copies[5].wait()
    y = columns_times(zeros(trace, width), couple_ref, load_ref, trace, inner)
    z = by_kind(face_columns(y), back_ref, facts[2:3, :])
    label = jnp.where(
        lax.broadcasted_iota(jnp.int32, (8, slots), 0) == 0, facts[1:2, :], 0.0
    )
    sums = exact_dot(jnp.concatenate([z, label], axis=0), onehot_ref[...], 1)
    own_ref[...] = sums[: COMP * NODES, :owned]
    out_ref[...] = sums[:, owned:]
    gid_ref[...] = sums[COMP * NODES :, owned:]
    copies[6].wait()


def merged(meta_ref, first, third, second, fourth, cap, to_owner):
    lane = lax.broadcasted_iota(jnp.int32, (1, RUNS * cap), 1)
    odd = meta_ref[3:4, : RUNS * cap] == 1.0
    low = lane < 2 * cap
    take_first = (low != odd) if to_owner else (low == odd)
    middle = jnp.where(take_first, first, second)
    return jnp.where(lane < cap, fourth, jnp.where(lane < 3 * cap, middle, third))


def onehot_of(condition):
    return jnp.where(condition, 1.0, 0.0).astype(BF16)


def own_ids(meta_ref, owned, count):
    base = meta_ref[4:5, :count].astype(jnp.int32)
    return lax.broadcasted_iota(jnp.int32, (owned, count), 0) + base + 1


def wanted_by(label, meta_ref, owned):
    count = label.shape[1]
    return onehot_of(own_ids(meta_ref, owned, count) == label.astype(jnp.int32))


def owner_kernel(owned, cap, meta_ref, own_ref, a_ref, b_ref, c_ref, d_ref, field_ref, out_ref, label_ref):
    received = merged(meta_ref, a_ref[...], b_ref[...], c_ref[...], d_ref[...], cap, True)
    rows = COMP * NODES
    label_ref[...] = received[rows : rows + 8]
    wanted = wanted_by(received[rows : rows + 1], meta_ref, owned)
    field = own_ref[...] + exact_dot(received[:rows], wanted, 1)
    field_ref[...] = field
    out_ref[...] = exact_dot(field, wanted)


def share(owned, sums, gid_ref, label_ref, meta_ref, own_ref, shared_ref):
    rows = COMP * NODES
    own = sums[:, :owned]
    own_ref[...] = own
    shared_ref[:rows, :] = sums[:, owned:]
    label = label_ref[0:1, :]
    shared_ref[rows : 2 * rows, :] = exact_dot(own, wanted_by(label, meta_ref, owned))
    row = lax.broadcasted_iota(jnp.int32, gid_ref.shape, 0)
    shared_ref[2 * rows :, :] = jnp.where(
        row == 0, gid_ref[0:1, :], jnp.where(row == 1, label, 0.0)
    )


def ids_down(ids, count):
    return jnp.broadcast_to(jnp.transpose(jnp.broadcast_to(ids, (8, ids.shape[1])))[:, 0:1], (ids.shape[1], count))


def pack_kernel(cap, meta_ref, mine_ref, other_ref, one_ref, three_ref, four_ref):
    rows = COMP * NODES
    count = RUNS * cap
    odd = meta_ref[3:4, :count] == 1.0
    mine, other = mine_ref[...], other_ref[...]
    even_part = jnp.where(odd, other, mine)
    odd_part = jnp.where(odd, mine, other)
    source = jnp.concatenate([even_part[:rows], odd_part[:rows]], axis=1)
    gids = jnp.concatenate([even_part[2 * rows : 2 * rows + 1], odd_part[2 * rows : 2 * rows + 1]], axis=1)
    blank = jnp.zeros((8, count), F32)
    sums = []
    for part in (even_part, odd_part):
        label = part[2 * rows + 1 : 2 * rows + 2]
        match = onehot_of((ids_down(label, 2 * count) == gids) & (gids > 0.0))
        full = part[rows : 2 * rows] + exact_dot(source, match, 1)
        sums.append(jnp.concatenate([full, blank], axis=0))
    outs = [
        jnp.concatenate([part[:rows], part[2 * rows : 2 * rows + 1], blank[1:]], axis=0)
        for part in (even_part, odd_part)
    ]
    lane = lax.broadcasted_iota(jnp.int32, (1, count), 1)

    def laid(*blocks):
        result = jnp.zeros((rows + 8, count), F32)
        for place, block in enumerate(blocks):
            if block is not None:
                array, run = block
                if run != place:
                    array = pltpu.roll(array, ((place - run) % RUNS) * cap, 1)
                inside = (lane >= place * cap) & (lane < (place + 1) * cap)
                result = jnp.where(inside, array, result)
        return result

    (oe, oo), (ge, go) = outs, sums
    one_ref[...] = jnp.where(
        odd, laid((oe, 0), (oe, 1), (ge, 2), (oo, 0)), laid((ge, 0), (go, 1), (oo, 2), (go, 0))
    )
    three_ref[...] = jnp.where(
        odd, laid((oo, 3), None, (oo, 2), (oe, 3)), laid((oe, 0), (oe, 1), (oo, 0), (oe, 3))
    )
    four_ref[...] = laid((oe, 3), (oo, 3), None, (jnp.where(odd, go, ge), 3))


def fused_values(owned, cap, meta_ref, own_ref, offers, blocks):
    rows = COMP * NODES
    count = RUNS * cap
    lane = lax.broadcasted_iota(jnp.int32, (1, count), 1)
    odd = meta_ref[3:4, :count] == 1.0
    offers = [r[...] for r in offers]
    blocks = [r[...] for r in blocks]
    mine, other, _ = offers
    source = jnp.concatenate([x[:rows] for x in offers + blocks], axis=1)
    gids = jnp.concatenate(
        [x[2 * rows : 2 * rows + 1] for x in offers] + [x[rows : rows + 1] for x in blocks], axis=1
    )
    total_count = gids.shape[1]
    remote = ids_down(mine[2 * rows : 2 * rows + 1], total_count)
    own = lax.broadcasted_iota(jnp.int32, (owned, total_count), 0).astype(F32) + (
        meta_ref[4:5, 0:1] + 1.0
    )
    match = onehot_of(jnp.concatenate([own, jnp.where(remote > 0.0, remote, -1.0)], axis=0) == gids)
    sums = exact_dot(source, match, 1)
    field = own_ref[...] + sums[:, :owned]
    near, _, far, across, _ = (x[:rows] for x in blocks)
    partner = other[rows : 2 * rows]
    even_form = jnp.where(lane < 2 * cap, across, jnp.where(lane < 3 * cap, partner, far))
    odd_form = jnp.where(
        lane < cap,
        pltpu.roll(near, cap, 1),
        jnp.where(lane < 2 * cap, partner, jnp.where(lane < 3 * cap, across, far)),
    )
    return field, jnp.where(odd, odd_form, even_form) + sums[:, owned:]


def element_values(field, received, meta_ref, onehot_ref, forth_ref, spread_ref):
    source = jnp.concatenate([field, received], axis=1)
    kind = meta_ref[2:3, :]
    faces = by_kind(exact_dot(source, onehot_ref[...]), forth_ref, kind)
    width = spread_ref.shape[1]
    for c in range(COMP):
        for f in range(FACES):
            spread_ref[(c * FACES + f) * NODES : (c * FACES + f + 1) * NODES, :] = faces[
                c * NODES : (c + 1) * NODES, f * width : (f + 1) * width
            ]
    return kind


def apply_kernel(
    inner, trace, owned, cap, fused,
    meta_ref, onehot_ref, forth_ref, back_ref, gid_ref, label_ref, inverse_ref, couple_ref, self_ref,
    *refs,
):
    if fused:
        before_ref, *received = refs[:9]
        refs = refs[9:]
        field_ref, refs = refs[0], refs[1:]
        field, received = fused_values(
            owned, cap, meta_ref, before_ref, received[:3], received[3:]
        )
        field_ref[...] = field
    else:
        field = refs[0][...]
        received = merged(meta_ref, *[r[...] for r in refs[1:5]], cap, False)
        refs = refs[5:]
    own_ref, shared_ref, spread_ref, mid_ref, weight_ref, image_ref = refs
    width = spread_ref.shape[1]
    kind = element_values(field, received, meta_ref, onehot_ref, forth_ref, spread_ref)
    rows_times(couple_ref, spread_ref, mid_ref, inner, trace)
    rows_times(inverse_ref, mid_ref, weight_ref, inner, inner)
    rows_times(self_ref, spread_ref, image_ref, trace, trace)
    y = columns_times(tiles_of(image_ref, trace), couple_ref, weight_ref, trace, inner)
    z = by_kind(face_columns(y), back_ref, kind)
    sums = exact_dot(z, onehot_ref[...], 1)
    share(owned, sums, gid_ref, label_ref, meta_ref, own_ref, shared_ref)


def total(x):
    return jnp.sum(jnp.sum(x, axis=0, keepdims=True), axis=1, keepdims=True)


def last_kernel(
    inner, trace, owned, cap,
    meta_ref, onehot_ref, forth_ref, inverse_ref, couple_ref, self_ref,
    k0_ref, k1_ref, s0_ref, s1_ref, u0_ref, u1_ref, before_ref, *refs,
):
    received, refs = refs[:8], refs[8:]
    k2_ref, weight_ref, moment_ref, spread_ref, mid_ref, image_ref = refs
    width = spread_ref.shape[1]
    field, received = fused_values(
        owned, cap, meta_ref, before_ref, received[:3], received[3:]
    )
    k2_ref[...] = field
    element_values(field, received, meta_ref, onehot_ref, forth_ref, spread_ref)
    rows_times(couple_ref, spread_ref, mid_ref, inner, trace)
    rows_times(inverse_ref, mid_ref, weight_ref, inner, inner)
    rows_times(self_ref, spread_ref, image_ref, trace, trace)
    image, weight = image_ref[...], weight_ref[...]
    ks = (k0_ref[...], k1_ref[...], field)
    values = [total(ks[i] * ks[j]) for i in range(3) for j in range(i, 3)]
    for s_ref, u_ref in ((s0_ref, u0_ref), (s1_ref, u1_ref), (spread_ref, mid_ref)):
        values.append(total(s_ref[...] * image) + total(u_ref[...] * weight))
    lane = lax.broadcasted_iota(jnp.int32, (1, width), 1)
    row = jnp.zeros((1, width), F32)
    for number, value in enumerate(values):
        row = jnp.where(lane == number, value, row)
    moment_ref[...] = jnp.broadcast_to(row[None], moment_ref.shape)


def finish_kernel(
    moment_ref, k0_ref, k1_ref, k2_ref, w0_ref, w1_ref, w2_ref, load_ref, field_ref, interior_ref
):
    sums = jnp.sum(moment_ref[...], axis=0)
    m = [sums[:, n : n + 1] for n in range(9)]
    gram = [[m[0], m[1], m[2]], [m[1], m[3], m[4]], [m[2], m[4], m[5]]]
    energy = [[gram[i][1], gram[i][2], m[6 + i]] for i in range(3)]

    def form(x, matrix):
        return sum(x[i] * sum(matrix[i][j] * x[j] for j in range(3)) for i in range(3))

    zero, one = jnp.zeros((1, 1), F32), jnp.ones((1, 1), F32)
    x = [zero, zero, zero]
    r = [one, zero, zero]
    d = [one, zero, zero]
    current = gram[0][0]
    for iteration in range(3):
        step = current / form(d, energy)
        x = [x[i] + step * d[i] for i in range(3)]
        if iteration < 2:
            r = [r[0], r[1] - step * d[0], r[2] - step * d[1]]
            following = form(r, gram)
            d = [r[i] + following / current * d[i] for i in range(3)]
            current = following
    field_ref[...] = x[0] * k0_ref[...] + x[1] * k1_ref[...] + x[2] * k2_ref[...]
    interior_ref[...] = load_ref[...] - (
        x[0] * w0_ref[...] + x[1] * w1_ref[...] + x[2] * w2_ref[...]
    )


def call(kernel, outs, *args, scratch=(), in_hbm=0, vmem=8):
    inside = len(args) - in_hbm
    args = args[:inside] + tuple(
        pltpu.with_memory_space_constraint(x, pltpu.HBM) for x in args[inside:]
    )
    return pl.pallas_call(
        kernel,
        out_shape=[jax.ShapeDtypeStruct(shape, dtype) for shape, dtype in outs],
        in_specs=[pl.BlockSpec(memory_space=pltpu.VMEM)] * inside
        + [pl.BlockSpec(memory_space=pltpu.HBM)] * in_hbm,
        out_specs=[pl.BlockSpec(memory_space=pltpu.VMEM)] * len(outs),
        scratch_shapes=[pltpu.VMEM(shape, dtype) for shape, dtype in scratch]
        + [pltpu.SemaphoreType.DMA(())] * in_hbm,
        compiler_params=pltpu.CompilerParams(vmem_limit_bytes=vmem * 1024 * 1024),
    )(*args)


def exchange(block, ranks, to_owner):
    away = ranks - 2 if to_owner else 2
    pairs = [
        [(r, r ^ 1) for r in range(ranks)],
        [(r, (r + (1 if r % 2 else ranks - 1)) % ranks) for r in range(ranks)],
        [(r, (r + ranks // 2) % ranks) for r in range(ranks)],
        [(r, (r + away) % ranks) for r in range(ranks)],
    ]
    return [lax.ppermute(block, AXES, pairs[n]) for n in (0, 2, 1, 3)]


def fused_exchange(cap, meta, shared, ranks):
    pair = [(r, r ^ 1) for r in range(ranks)]

    def both_ways(chips):
        ahead = [(r, (r + 2 * chips + 1) % ranks) for r in range(0, ranks, 2)]
        return ahead + [(t, r) for r, t in ahead]

    skip = [(r, (r + (3 if r % 2 else ranks - 3)) % ranks) for r in range(ranks)]
    far = [(r, (r + ranks // 2) % ranks) for r in range(ranks)]
    second = lax.ppermute(shared, AXES, skip)
    other = lax.ppermute(shared, AXES, pair)
    shape = (COMP * NODES + 8, RUNS * cap)
    packed = call(
        functools.partial(pack_kernel, cap), [(shape, F32)] * 3, meta, shared, other
    )
    got = [
        lax.ppermute(block, AXES, way)
        for block, way in zip(packed, (both_ways(1), both_ways(ranks // 4 - 1), far))
    ]
    passed = [lax.ppermute(block, AXES, pair) for block in got[:2]]
    return [shared, other, second, *got, *passed]


def local(self_block, couple, inverse, body_force, face_mortar, face_kind, *, ranks):
    trace, _, elements = self_block.shape
    inner = inverse.shape[0]
    owned = 2 * elements
    cap = max(2, elements // 4)
    width = elements
    rows = COMP * NODES
    forward, backward = block_tables()
    mortar = face_mortar.reshape(FACES, width)
    kind = face_kind.reshape(FACES, width)
    self_block = self_block.reshape(trace * trace, width)
    couple = couple.reshape(inner * trace, width)
    inverse = inverse.reshape(inner * inner, width)
    force = body_force.reshape(COMP * inner, width)

    own, out, gid, onehot, meta, load, *matrices = call(
        functools.partial(start_kernel, ranks, inner, trace, owned, cap),
        [
            ((rows, owned), F32),
            ((rows + 8, RUNS * cap), F32),
            ((8, RUNS * cap), F32),
            ((owned + RUNS * cap, FACES * width), BF16),
            ((8, FACES * width), F32),
            ((COMP * inner, width), F32),
            (inverse.shape, F32),
            (couple.shape, F32),
            (self_block.shape, F32),
        ],
        mortar, kind, force, backward, inverse, couple, self_block,
        scratch=[
            (mortar.shape, jnp.int32), (kind.shape, jnp.int32), (force.shape, F32), (backward.shape, F32)
        ],
        in_hbm=7, vmem=16,
    )
    blocks = exchange(out, ranks, True)
    field, out, label = call(
        functools.partial(owner_kernel, owned, cap),
        [((rows, owned), F32), ((rows, RUNS * cap), F32), ((8, RUNS * cap), F32)],
        meta, own, *blocks,
    )
    blocks = exchange(out, ranks, False)
    fields, spreads, mids, weights = [field], [], [], []
    for iteration in range(2):
        fused = iteration > 0
        first = [((rows, owned), F32)] if fused else []
        results = call(
            functools.partial(apply_kernel, inner, trace, owned, cap, fused),
            first + [
                ((rows, owned), F32),
                ((2 * rows + 8, RUNS * cap), F32),
                ((COMP * trace, width), F32),
                ((COMP * inner, width), F32),
                ((COMP * inner, width), F32),
            ],
            meta, onehot, forward, backward, gid, label, *matrices, own if fused else field, *blocks,
            scratch=[((COMP * trace, width), F32)],
        )
        fields += results[: len(first)]
        own, shared, spread, mid, weight = results[len(first) :]
        spreads.append(spread)
        mids.append(mid)
        weights.append(weight)
        blocks = fused_exchange(cap, meta, shared, ranks)
    field, weight, moments = call(
        functools.partial(last_kernel, inner, trace, owned, cap),
        [((rows, owned), F32), ((COMP * inner, width), F32), ((ranks, 1, width), F32)],
        meta, onehot, forward, *matrices, *fields, *spreads, *mids, own, *blocks,
        scratch=[
            ((COMP * trace, width), F32),
            ((COMP * inner, width), F32),
            ((COMP * trace, width), F32),
        ],
    )
    fields.append(field)
    weights.append(weight)
    moments = lax.all_to_all(moments, AXES, split_axis=0, concat_axis=0, tiled=True)
    trace_field, interior = call(
        finish_kernel,
        [((rows, owned), F32), ((COMP * inner, width), F32)],
        moments, *fields, *weights, load,
    )
    return trace_field, interior.reshape(COMP, inner, elements)


def solution(mesh):
    placed = (
        P(None, None, AXES),
        P(None, None, AXES),
        P(None, None, AXES),
        P(None, None, AXES),
        P(AXES),
        P(AXES),
    )
    ranks = int(np.prod([mesh.shape[a] for a in AXES]))
    return jax.shard_map(
        functools.partial(local, ranks=ranks),
        mesh=mesh,
        in_specs=placed,
        out_specs=(P(None, AXES), P(None, None, AXES)),
        check_vma=False,
    )
```

```python
import functools

import jax
import jax.numpy as jnp
import numpy as np
from jax import lax
from jax.experimental import pallas as pl
from jax.experimental.pallas import tpu as pltpu
from jax.sharding import PartitionSpec as P

AXES = ("dom", "blk")
COMP = 3
NODES = 16
FACES = 6
RUNS = 4
F32 = jnp.float32
BF16 = jnp.bfloat16


def interp_tables():
    abscissae = -np.cos(np.pi * np.arange(4) / 3.0)

    def lagrange(points):
        columns = [
            np.prod(
                [
                    (points - abscissae[other_node])
                    / (abscissae[basis_node] - abscissae[other_node])
                    for other_node in range(4)
                    if other_node != basis_node
                ],
                axis=0,
            )
            for basis_node in range(4)
        ]
        return np.stack(columns, axis=1)

    lower_map = lagrange((abscissae - 1.0) / 2.0)
    upper_map = lagrange((abscissae + 1.0) / 2.0)
    return np.stack(
        [
            np.kron(lower_map, lower_map),
            np.kron(lower_map, upper_map),
            np.kron(upper_map, lower_map),
            np.kron(upper_map, upper_map),
        ]
    ).astype(np.float32)


def block_tables():
    tables = interp_tables()
    eye = np.eye(COMP, dtype=np.float32)
    forward = np.concatenate([np.kron(eye, t) for t in tables])
    backward = np.concatenate([np.kron(eye, t.T) for t in tables])
    return forward, backward


def split(x):
    hi = x.astype(BF16)
    return hi, (x - hi.astype(F32)).astype(BF16)


def dot(a, b, rhs_dim=0):
    return lax.dot_general(a, b, (((1,), (rhs_dim,)), ((), ())), preferred_element_type=F32)


def exact_dot(x, onehot, rhs_dim=0):
    hi, lo = split(x)
    both = dot(jnp.concatenate([hi, lo], axis=0), onehot, rhs_dim)
    return both[: x.shape[0]] + both[x.shape[0] :]


def by_kind(x, table_ref, kind):
    rows = x.shape[0]
    t_hi, t_lo = split(table_ref[...])
    x_hi, x_lo = split(x)
    mapped = dot(
        jnp.concatenate([t_hi, t_hi, t_lo], axis=1), jnp.concatenate([x_hi, x_lo, x_hi], axis=0)
    )
    for number in range(4):
        x = jnp.where(kind == number + 1, mapped[number * rows : (number + 1) * rows], x)
    return x


def in_a_row(x):
    return jnp.concatenate([x[r : r + 1, :] for r in range(x.shape[0])], axis=1)


def gather_rows(tiles, sublane):
    tiles = [tiles[r] for r in (0, 4, 2, 6, 1, 5, 3, 7)]
    keep = (sublane & 4) == 0
    tiles = [
        jnp.where(keep, x, y) + pltpu.roll(jnp.where(keep, y, x), 4, 0)
        for x, y in zip(tiles[::2], tiles[1::2])
    ]
    for shift in (2, 1):
        keep = (sublane & shift) == 0
        tiles = [
            jnp.where(keep, x + pltpu.roll(x, 8 - shift, 0), y + pltpu.roll(y, shift, 0))
            for x, y in zip(tiles[::2], tiles[1::2])
        ]
    return tiles[0]


def rows_times(mat_ref, vec_ref, out_ref, outs, terms, group=32):
    width = vec_ref.shape[1]
    sublane = lax.broadcasted_iota(jnp.int32, (8, width), 0)
    vecs = [
        [vec_ref[c * terms + t : c * terms + t + 8, :] for t in range(0, terms, 8)]
        for c in range(COMP)
    ]

    def body(g, carry):
        for first in range(0, group, 8):
            sums = [[] for _ in range(COMP)]
            for r in range(first, first + 8):
                acc = [None] * COMP
                for j in range(terms // 8):
                    start = pl.multiple_of((g * group + r) * terms + 8 * j, 8)
                    tile = mat_ref[pl.ds(start, 8), :]
                    for c in range(COMP):
                        term = tile * vecs[c][j]
                        acc[c] = term if j == 0 else acc[c] + term
                for c in range(COMP):
                    sums[c].append(acc[c])
            for c in range(COMP):
                start = pl.multiple_of(c * outs + g * group + first, 8)
                out_ref[pl.ds(start, 8), :] = gather_rows(sums[c], sublane)
        return carry

    lax.fori_loop(0, outs // group, body, 0)


def columns_times(acc, mat_ref, vec_ref, outs, terms, unroll=16):
    def body(t, acc):
        acc = [list(a) for a in acc]
        vecs = [
            jnp.broadcast_to(vec_ref[pl.ds(c * terms + t, 1), :], (8, vec_ref.shape[1]))
            for c in range(COMP)
        ]
        for j in range(outs // 8):
            tile = mat_ref[pl.ds(pl.multiple_of(t * outs + j * 8, 8), 8), :]
            for c in range(COMP):
                acc[c][j] = acc[c][j] + tile * vecs[c]
        return acc

    return lax.fori_loop(0, terms, body, acc, unroll=unroll)


def tiles_of(ref, outs):
    return [[ref[c * outs + t : c * outs + t + 8, :] for t in range(0, outs, 8)] for c in range(COMP)]


def zeros(outs, width):
    return [[jnp.zeros((8, width), F32) for _ in range(outs // 8)] for _ in range(COMP)]


def face_columns(acc):
    half = NODES // 8
    return jnp.concatenate(
        [
            jnp.concatenate(
                [acc[c][f * half + h] for c in range(COMP) for h in range(half)], axis=0
            )
            for f in range(FACES)
        ],
        axis=1,
    )


def start_kernel(
    ranks, inner, trace, owned, cap,
    mortar_hbm, kind_hbm, force_hbm, back_hbm, inverse_hbm, couple_hbm, self_hbm,
    offer_ref, out_ref, onehot_ref, meta_ref, load_ref, inverse_ref, couple_ref, self_ref,
    mortar_ref, kind_ref, force_ref, back_ref, *sems,
):
    copies = [
        pltpu.make_async_copy(source, target, sem)
        for source, target, sem in zip(
            (mortar_hbm, kind_hbm, force_hbm, back_hbm, inverse_hbm, couple_hbm, self_hbm),
            (mortar_ref, kind_ref, force_ref, back_ref, inverse_ref, couple_ref, self_ref),
            sems,
        )
    ]
    for copy in copies:
        copy.start()
    copies[0].wait()
    copies[1].wait()
    width = mortar_ref.shape[1]
    slots = FACES * width
    mortar = mortar_ref[...]
    owner = lax.div(mortar, owned)
    index = lax.rem(mortar, owned)
    me = lax.rem(owner[0:1, 0:1] + 2, ranks)
    distance = lax.rem(owner - me + ranks, ranks)
    slot = lax.broadcasted_iota(jnp.int32, mortar.shape, 0) * width + lax.broadcasted_iota(
        jnp.int32, mortar.shape, 1
    )
    column = index
    begin = jnp.zeros((1, 1), jnp.int32)
    for number, away in enumerate((ranks - 2, ranks - 1, 0, 1, ranks // 2)):
        inside = distance == away
        count = jnp.sum(inside.astype(F32), keepdims=True).astype(jnp.int32)
        if away:
            run = number - (number > 2)
            column = jnp.where(inside, owned + run * cap + slot - begin, column)
        begin = begin + count
    target = lax.broadcasted_iota(jnp.int32, (1, slots), 1)
    target = lax.rem(target, width) * FACES + lax.div(target, width)
    order = jnp.where(
        lax.broadcasted_iota(jnp.int32, (slots, slots), 0) == target, 1.0, 0.0
    ).astype(BF16)
    facts = jnp.concatenate(
        [in_a_row(column), in_a_row(mortar + 1), in_a_row(kind_ref[...]), jnp.zeros((5, slots), jnp.int32)],
        axis=0,
    ).astype(F32)
    facts = exact_dot(facts, order)
    meta_ref[...] = facts
    meta_ref[3:4, :] = jnp.broadcast_to(lax.rem(me, 2).astype(F32), (1, slots))
    meta_ref[4:5, :] = jnp.broadcast_to((me * owned).astype(F32), (1, slots))
    column = facts[0:1, :].astype(jnp.int32)
    onehot_ref[...] = jnp.where(
        lax.broadcasted_iota(jnp.int32, onehot_ref.shape, 0) == column, 1.0, 0.0
    ).astype(BF16)
    copies[2].wait()
    copies[4].wait()
    rows_times(inverse_ref, force_ref, load_ref, inner, inner)
    copies[3].wait()
    copies[5].wait()
    y = columns_times(zeros(trace, width), couple_ref, load_ref, trace, inner)
    z = by_kind(face_columns(y), back_ref, facts[2:3, :])
    label = jnp.where(
        lax.broadcasted_iota(jnp.int32, (8, slots), 0) == 0, facts[1:2, :], 0.0
    )
    sums = exact_dot(jnp.concatenate([z, label], axis=0), onehot_ref[...], 1)
    count = RUNS * cap
    ids = lax.broadcasted_iota(jnp.int32, (8, owned), 1) + (me * owned + 1)
    ids = jnp.where(lax.broadcasted_iota(jnp.int32, (8, owned), 0) == 0, ids, 0)
    out_ref[...] = sums[:, owned:]
    offer_ref[:, :count] = sums[:, owned:]
    offer_ref[: COMP * NODES, count:] = sums[: COMP * NODES, :owned]
    offer_ref[COMP * NODES :, count:] = ids.astype(F32)
    copies[6].wait()


def onehot_of(condition):
    return jnp.where(condition, 1.0, 0.0).astype(BF16)


def own_ids(meta_ref, owned, count):
    base = meta_ref[4:5, :count].astype(jnp.int32)
    return lax.broadcasted_iota(jnp.int32, (owned, count), 0) + base + 1


def wanted_by(label, meta_ref, owned):
    count = label.shape[1]
    return onehot_of(own_ids(meta_ref, owned, count) == label.astype(jnp.int32))


def share(owned, sums, gid, label, meta_ref, own_ref, shared_ref):
    rows = COMP * NODES
    own = sums[:, :owned]
    own_ref[...] = own
    shared_ref[:rows, :] = sums[:, owned:]
    shared_ref[rows : 2 * rows, :] = exact_dot(own, wanted_by(label, meta_ref, owned))
    row = lax.broadcasted_iota(jnp.int32, (8, gid.shape[1]), 0)
    shared_ref[2 * rows :, :] = jnp.where(row == 0, gid, jnp.where(row == 1, label, 0.0))


def ids_down(ids, count):
    return jnp.broadcast_to(jnp.transpose(jnp.broadcast_to(ids, (8, ids.shape[1])))[:, 0:1], (ids.shape[1], count))


def laid_out(cap, *blocks):
    count = RUNS * cap
    lane = lax.broadcasted_iota(jnp.int32, (1, count), 1)
    result = jnp.zeros((COMP * NODES + 8, count), F32)
    for place, block in enumerate(blocks):
        if block is not None:
            array, run = block
            if run != place:
                array = pltpu.roll(array, ((place - run) % RUNS) * cap, 1)
            inside = (lane >= place * cap) & (lane < (place + 1) * cap)
            result = jnp.where(inside, array, result)
    return result


def first_pack_kernel(owned, cap, meta_ref, mine_ref, other_ref, one_ref, three_ref, four_ref):
    rows = COMP * NODES
    count = RUNS * cap
    laid = functools.partial(laid_out, cap)
    odd = meta_ref[3:4, :count] == 1.0
    odd_own = meta_ref[3:4, :owned] == 1.0
    outs = [mine_ref[:, :count], other_ref[:, :count]]
    fulls = []
    for source, target_ref, swap in ((outs[1], mine_ref, False), (outs[0], other_ref, True)):
        base = meta_ref[4:5, 0:1] + 1.0
        if swap:
            base = base + jnp.where(meta_ref[3:4, 0:1] == 1.0, -float(owned), float(owned))
        ids = lax.broadcasted_iota(jnp.int32, (owned, count), 0).astype(F32) + base
        match = onehot_of(ids == source[rows : rows + 1])
        full = target_ref[:rows, count:] + exact_dot(source[:rows], match, 1)
        fulls.append(jnp.concatenate([full, target_ref[rows:, count:]], axis=0))
    oe, oo = jnp.where(odd, outs[1], outs[0]), jnp.where(odd, outs[0], outs[1])
    one_ref[:, :count] = jnp.where(
        odd, laid((oe, 0), (oe, 1), None, (oo, 0)), laid(None, None, (oo, 2))
    )
    one_ref[:, count : count + owned] = jnp.where(odd_own, fulls[1], fulls[0])
    one_ref[:, count + owned :] = jnp.where(odd_own, fulls[0], fulls[1])
    three_ref[...] = jnp.where(
        odd, laid((oo, 3), None, (oo, 2), (oe, 3)), laid((oe, 0), (oe, 1), (oo, 0), (oe, 3))
    )
    four_ref[:, :count] = laid((oe, 3), (oo, 3))
    four_ref[:, count:] = fulls[0]


def pack_kernel(cap, meta_ref, mine_ref, other_ref, one_ref, three_ref, four_ref):
    rows = COMP * NODES
    count = RUNS * cap
    odd = meta_ref[3:4, :count] == 1.0
    mine, other = mine_ref[...], other_ref[...]
    even_part = jnp.where(odd, other, mine)
    odd_part = jnp.where(odd, mine, other)
    source = jnp.concatenate([even_part[:rows], odd_part[:rows]], axis=1)
    gids = jnp.concatenate([even_part[2 * rows : 2 * rows + 1], odd_part[2 * rows : 2 * rows + 1]], axis=1)
    blank = jnp.zeros((8, count), F32)
    sums = []
    for part in (even_part, odd_part):
        label = part[2 * rows + 1 : 2 * rows + 2]
        match = onehot_of((ids_down(label, 2 * count) == gids) & (gids > 0.0))
        full = part[rows : 2 * rows] + exact_dot(source, match, 1)
        sums.append(jnp.concatenate([full, blank], axis=0))
    outs = [
        jnp.concatenate([part[:rows], part[2 * rows : 2 * rows + 1], blank[1:]], axis=0)
        for part in (even_part, odd_part)
    ]
    laid = functools.partial(laid_out, cap)
    (oe, oo), (ge, go) = outs, sums
    one_ref[...] = jnp.where(
        odd, laid((oe, 0), (oe, 1), (ge, 2), (oo, 0)), laid((ge, 0), (go, 1), (oo, 2), (go, 0))
    )
    three_ref[...] = jnp.where(
        odd, laid((oo, 3), None, (oo, 2), (oe, 3)), laid((oe, 0), (oe, 1), (oo, 0), (oe, 3))
    )
    four_ref[...] = laid((oe, 3), (oo, 3), None, (jnp.where(odd, go, ge), 3))


def matched(owned, meta_ref, gid, sources, remote_sources=()):
    values = jnp.concatenate([v for v, _ in sources], axis=1)
    ids = jnp.concatenate([i for _, i in sources], axis=1)
    number = ids.shape[1]
    own = lax.broadcasted_iota(jnp.int32, (owned, number), 0).astype(F32) + (
        meta_ref[4:5, 0:1] + 1.0
    )
    gid = jnp.where(gid > 0.0, gid, -1.0)
    match = onehot_of(jnp.concatenate([own, ids_down(gid, number)], axis=0) == ids)
    sums = exact_dot(values, match, 1)
    field, remote = sums[:, :owned], sums[:, owned:]
    if remote_sources:
        values = jnp.concatenate([v for v, _ in remote_sources], axis=1)
        ids = jnp.concatenate([i for _, i in remote_sources], axis=1)
        remote = remote + exact_dot(values, onehot_of(ids_down(gid, ids.shape[1]) == ids), 1)
    return field, remote


def first_values(owned, cap, meta_ref, offers, blocks):
    rows = COMP * NODES
    count = RUNS * cap
    lane = lax.broadcasted_iota(jnp.int32, (1, count), 1)
    odd = meta_ref[3:4, :count] == 1.0
    mine_ref, other_ref, _ = offers
    one_ref, _, far_ref, passed_ref, _ = blocks
    sources = [(r[:rows, :count], r[rows : rows + 1, :count]) for r in (*offers, *blocks)]
    owners = [
        (r[:rows, count:], r[rows : rows + 1, count:])
        for r in (other_ref, one_ref, far_ref, passed_ref)
    ]
    gid = mine_ref[rows : rows + 1, :count]
    field, remote = matched(owned, meta_ref, gid, sources, owners)
    label_rows = slice(rows, rows + 8)
    other = other_ref[label_rows, :count]
    one = one_ref[label_rows, :count]
    far = far_ref[label_rows, :count]
    passed = passed_ref[label_rows, :count]
    even_form = jnp.where(
        lane < cap,
        one,
        jnp.where(
            lane < 2 * cap, other, jnp.where(lane < 3 * cap, passed, pltpu.roll(far, 3 * cap, 1))
        ),
    )
    odd_form = jnp.where(
        lane < cap,
        pltpu.roll(passed, cap, 1),
        jnp.where(
            lane < 2 * cap, passed, jnp.where(lane < 3 * cap, other, pltpu.roll(far, 2 * cap, 1))
        ),
    )
    label = jnp.where(odd, odd_form, even_form)
    return mine_ref[:rows, count:] + field, remote, gid, label


def fused_values(owned, cap, meta_ref, own_ref, offers, blocks):
    rows = COMP * NODES
    count = RUNS * cap
    lane = lax.broadcasted_iota(jnp.int32, (1, count), 1)
    odd = meta_ref[3:4, :count] == 1.0
    sources = [(r[:rows], r[2 * rows : 2 * rows + 1]) for r in offers]
    sources += [(r[:rows], r[rows : rows + 1]) for r in blocks]
    field, remote = matched(owned, meta_ref, offers[0][2 * rows : 2 * rows + 1], sources)
    near, _, far, across, _ = (r[:rows] for r in blocks)
    partner = offers[1][rows : 2 * rows]
    even_form = jnp.where(lane < 2 * cap, across, jnp.where(lane < 3 * cap, partner, far))
    odd_form = jnp.where(
        lane < cap,
        pltpu.roll(near, cap, 1),
        jnp.where(lane < 2 * cap, partner, jnp.where(lane < 3 * cap, across, far)),
    )
    return own_ref[...] + field, jnp.where(odd, odd_form, even_form) + remote


def element_values(field, received, meta_ref, onehot_ref, forth_ref, spread_ref):
    source = jnp.concatenate([field, received], axis=1)
    kind = meta_ref[2:3, :]
    faces = by_kind(exact_dot(source, onehot_ref[...]), forth_ref, kind)
    width = spread_ref.shape[1]
    for c in range(COMP):
        for f in range(FACES):
            spread_ref[(c * FACES + f) * NODES : (c * FACES + f + 1) * NODES, :] = faces[
                c * NODES : (c + 1) * NODES, f * width : (f + 1) * width
            ]
    return kind


def apply_kernel(
    inner, trace, owned, cap, fused,
    meta_ref, onehot_ref, forth_ref, back_ref, inverse_ref, couple_ref, self_ref,
    *refs,
):
    if fused:
        gid_ref, label_ref, before_ref, *received = refs[:11]
        field_ref, *refs = refs[11:]
        gid, label = gid_ref[0:1, :], label_ref[0:1, :]
        field, received = fused_values(
            owned, cap, meta_ref, before_ref, received[:3], received[3:]
        )
    else:
        field_ref, gid_ref, label_ref, *after = refs[8:]
        field, received, gid, label = first_values(owned, cap, meta_ref, refs[:3], refs[3:8])
        refs = after
        gid_ref[...] = jnp.broadcast_to(gid, gid_ref.shape)
        label_ref[...] = label
        label = label[0:1, :]
    field_ref[...] = field
    own_ref, shared_ref, spread_ref, mid_ref, weight_ref, image_ref = refs
    width = spread_ref.shape[1]
    kind = element_values(field, received, meta_ref, onehot_ref, forth_ref, spread_ref)
    rows_times(couple_ref, spread_ref, mid_ref, inner, trace)
    rows_times(inverse_ref, mid_ref, weight_ref, inner, inner)
    rows_times(self_ref, spread_ref, image_ref, trace, trace)
    y = columns_times(tiles_of(image_ref, trace), couple_ref, weight_ref, trace, inner)
    z = by_kind(face_columns(y), back_ref, kind)
    sums = exact_dot(z, onehot_ref[...], 1)
    share(owned, sums, gid, label, meta_ref, own_ref, shared_ref)


def total(x):
    return jnp.sum(jnp.sum(x, axis=0, keepdims=True), axis=1, keepdims=True)


def last_kernel(
    inner, trace, owned, cap,
    meta_ref, onehot_ref, forth_ref, inverse_ref, couple_ref, self_ref,
    k0_ref, k1_ref, s0_ref, s1_ref, u0_ref, u1_ref, before_ref, *refs,
):
    received, refs = refs[:8], refs[8:]
    k2_ref, weight_ref, moment_ref, spread_ref, mid_ref, image_ref = refs
    width = spread_ref.shape[1]
    field, received = fused_values(
        owned, cap, meta_ref, before_ref, received[:3], received[3:]
    )
    k2_ref[...] = field
    element_values(field, received, meta_ref, onehot_ref, forth_ref, spread_ref)
    rows_times(couple_ref, spread_ref, mid_ref, inner, trace)
    rows_times(inverse_ref, mid_ref, weight_ref, inner, inner)
    rows_times(self_ref, spread_ref, image_ref, trace, trace)
    image, weight = image_ref[...], weight_ref[...]
    ks = (k0_ref[...], k1_ref[...], field)
    values = [total(ks[i] * ks[j]) for i in range(3) for j in range(i, 3)]
    for s_ref, u_ref in ((s0_ref, u0_ref), (s1_ref, u1_ref), (spread_ref, mid_ref)):
        values.append(total(s_ref[...] * image) + total(u_ref[...] * weight))
    lane = lax.broadcasted_iota(jnp.int32, (1, width), 1)
    row = jnp.zeros((1, width), F32)
    for number, value in enumerate(values):
        row = jnp.where(lane == number, value, row)
    moment_ref[...] = jnp.broadcast_to(row[None], moment_ref.shape)


def finish_kernel(
    moment_ref, k0_ref, k1_ref, k2_ref, w0_ref, w1_ref, w2_ref, load_ref, field_ref, interior_ref
):
    sums = jnp.sum(moment_ref[...], axis=0)
    m = [sums[:, n : n + 1] for n in range(9)]
    gram = [[m[0], m[1], m[2]], [m[1], m[3], m[4]], [m[2], m[4], m[5]]]
    energy = [[gram[i][1], gram[i][2], m[6 + i]] for i in range(3)]

    def form(x, matrix):
        return sum(x[i] * sum(matrix[i][j] * x[j] for j in range(3)) for i in range(3))

    zero, one = jnp.zeros((1, 1), F32), jnp.ones((1, 1), F32)
    x = [zero, zero, zero]
    r = [one, zero, zero]
    d = [one, zero, zero]
    current = gram[0][0]
    for iteration in range(3):
        step = current / form(d, energy)
        x = [x[i] + step * d[i] for i in range(3)]
        if iteration < 2:
            r = [r[0], r[1] - step * d[0], r[2] - step * d[1]]
            following = form(r, gram)
            d = [r[i] + following / current * d[i] for i in range(3)]
            current = following
    field_ref[...] = x[0] * k0_ref[...] + x[1] * k1_ref[...] + x[2] * k2_ref[...]
    interior_ref[...] = load_ref[...] - (
        x[0] * w0_ref[...] + x[1] * w1_ref[...] + x[2] * w2_ref[...]
    )


def call(kernel, outs, *args, scratch=(), in_hbm=0, vmem=8):
    inside = len(args) - in_hbm
    args = args[:inside] + tuple(
        pltpu.with_memory_space_constraint(x, pltpu.HBM) for x in args[inside:]
    )
    return pl.pallas_call(
        kernel,
        out_shape=[jax.ShapeDtypeStruct(shape, dtype) for shape, dtype in outs],
        in_specs=[pl.BlockSpec(memory_space=pltpu.VMEM)] * inside
        + [pl.BlockSpec(memory_space=pltpu.HBM)] * in_hbm,
        out_specs=[pl.BlockSpec(memory_space=pltpu.VMEM)] * len(outs),
        scratch_shapes=[pltpu.VMEM(shape, dtype) for shape, dtype in scratch]
        + [pltpu.SemaphoreType.DMA(())] * in_hbm,
        compiler_params=pltpu.CompilerParams(vmem_limit_bytes=vmem * 1024 * 1024),
    )(*args)


def fused_exchange(meta, shared, out, ranks, kernel, widths):
    pair = [(r, r ^ 1) for r in range(ranks)]

    def both_ways(chips):
        ahead = [(r, (r + 2 * chips + 1) % ranks) for r in range(0, ranks, 2)]
        return ahead + [(t, r) for r, t in ahead]

    skip = [(r, (r + (3 if r % 2 else ranks - 3)) % ranks) for r in range(ranks)]
    far = [(r, (r + ranks // 2) % ranks) for r in range(ranks)]
    second = lax.ppermute(out, AXES, skip)
    other = lax.ppermute(shared, AXES, pair)
    packed = call(
        kernel, [((COMP * NODES + 8, width), F32) for width in widths], meta, shared, other
    )
    got = [
        lax.ppermute(block, AXES, way)
        for block, way in zip(packed, (both_ways(1), both_ways(ranks // 4 - 1), far))
    ]
    passed = [lax.ppermute(block, AXES, pair) for block in got[:2]]
    return [shared, other, second, *got, *passed]


def local(self_block, couple, inverse, body_force, face_mortar, face_kind, *, ranks):
    trace, _, elements = self_block.shape
    inner = inverse.shape[0]
    owned = 2 * elements
    cap = max(2, elements // 4)
    width = elements
    rows = COMP * NODES
    count = RUNS * cap
    forward, backward = block_tables()
    mortar = face_mortar.reshape(FACES, width)
    kind = face_kind.reshape(FACES, width)
    self_block = self_block.reshape(trace * trace, width)
    couple = couple.reshape(inner * trace, width)
    inverse = inverse.reshape(inner * inner, width)
    force = body_force.reshape(COMP * inner, width)

    offer, out, onehot, meta, load, *matrices = call(
        functools.partial(start_kernel, ranks, inner, trace, owned, cap),
        [
            ((rows + 8, count + owned), F32),
            ((rows + 8, count), F32),
            ((owned + count, FACES * width), BF16),
            ((8, FACES * width), F32),
            ((COMP * inner, width), F32),
            (inverse.shape, F32),
            (couple.shape, F32),
            (self_block.shape, F32),
        ],
        mortar, kind, force, backward, inverse, couple, self_block,
        scratch=[
            (mortar.shape, jnp.int32), (kind.shape, jnp.int32), (force.shape, F32), (backward.shape, F32)
        ],
        in_hbm=7, vmem=16,
    )
    blocks = fused_exchange(
        meta, offer, out, ranks,
        functools.partial(first_pack_kernel, owned, cap),
        (count + 2 * owned, count, count + owned),
    )
    fields, spreads, mids, weights, ids, own = [], [], [], [], [], None
    for iteration in range(2):
        fused = iteration > 0
        first = [((rows, owned), F32)] + ([] if fused else [((8, count), F32)] * 2)
        results = call(
            functools.partial(apply_kernel, inner, trace, owned, cap, fused),
            first + [
                ((rows, owned), F32),
                ((2 * rows + 8, count), F32),
                ((COMP * trace, width), F32),
                ((COMP * inner, width), F32),
                ((COMP * inner, width), F32),
            ],
            meta, onehot, forward, backward, *matrices, *([*ids, own] if fused else []), *blocks,
            scratch=[((COMP * trace, width), F32)],
        )
        fields.append(results[0])
        ids = ids or results[1 : len(first)]
        own, shared, spread, mid, weight = results[len(first) :]
        spreads.append(spread)
        mids.append(mid)
        weights.append(weight)
        blocks = fused_exchange(
            meta, shared, shared, ranks, functools.partial(pack_kernel, cap), (count,) * 3
        )
    field, weight, moments = call(
        functools.partial(last_kernel, inner, trace, owned, cap),
        [((rows, owned), F32), ((COMP * inner, width), F32), ((ranks, 1, width), F32)],
        meta, onehot, forward, *matrices, *fields, *spreads, *mids, own, *blocks,
        scratch=[
            ((COMP * trace, width), F32),
            ((COMP * inner, width), F32),
            ((COMP * trace, width), F32),
        ],
    )
    fields.append(field)
    weights.append(weight)
    moments = lax.all_to_all(moments, AXES, split_axis=0, concat_axis=0, tiled=True)
    trace_field, interior = call(
        finish_kernel,
        [((rows, owned), F32), ((COMP * inner, width), F32)],
        moments, *fields, *weights, load,
    )
    return trace_field, interior.reshape(COMP, inner, elements)


def solution(mesh):
    placed = (
        P(None, None, AXES),
        P(None, None, AXES),
        P(None, None, AXES),
        P(None, None, AXES),
        P(AXES),
        P(AXES),
    )
    ranks = int(np.prod([mesh.shape[a] for a in AXES]))
    return jax.shard_map(
        functools.partial(local, ranks=ranks),
        mesh=mesh,
        in_specs=placed,
        out_specs=(P(None, AXES), P(None, None, AXES)),
        check_vma=False,
    )
```

```python
import functools

import jax
import jax.numpy as jnp
import numpy as np
from jax import lax
from jax.experimental import pallas as pl
from jax.experimental.pallas import tpu as pltpu
from jax.sharding import PartitionSpec as P

AXES = ("dom", "blk")
COMP = 3
NODES = 16
FACES = 6
RUNS = 4
F32 = jnp.float32
BF16 = jnp.bfloat16


def interp_tables():
    abscissae = -np.cos(np.pi * np.arange(4) / 3.0)

    def lagrange(points):
        columns = [
            np.prod(
                [
                    (points - abscissae[other_node])
                    / (abscissae[basis_node] - abscissae[other_node])
                    for other_node in range(4)
                    if other_node != basis_node
                ],
                axis=0,
            )
            for basis_node in range(4)
        ]
        return np.stack(columns, axis=1)

    lower_map = lagrange((abscissae - 1.0) / 2.0)
    upper_map = lagrange((abscissae + 1.0) / 2.0)
    return np.stack(
        [
            np.kron(lower_map, lower_map),
            np.kron(lower_map, upper_map),
            np.kron(upper_map, lower_map),
            np.kron(upper_map, upper_map),
        ]
    ).astype(np.float32)


def block_tables():
    tables = interp_tables()
    eye = np.eye(COMP, dtype=np.float32)
    forward = np.concatenate([np.kron(eye, t) for t in tables])
    backward = np.concatenate([np.kron(eye, t.T) for t in tables])
    return forward, backward


def split(x):
    hi = x.astype(BF16)
    return hi, (x - hi.astype(F32)).astype(BF16)


def dot(a, b, rhs_dim=0):
    return lax.dot_general(a, b, (((1,), (rhs_dim,)), ((), ())), preferred_element_type=F32)


def exact_dot(x, onehot, rhs_dim=0):
    hi, lo = split(x)
    both = dot(jnp.concatenate([hi, lo], axis=0), onehot, rhs_dim)
    return both[: x.shape[0]] + both[x.shape[0] :]


def by_kind(x, table_ref, kind):
    rows = x.shape[0]
    t_hi, t_lo = split(table_ref[...])
    x_hi, x_lo = split(x)
    mapped = dot(
        jnp.concatenate([t_hi, t_hi, t_lo], axis=1), jnp.concatenate([x_hi, x_lo, x_hi], axis=0)
    )
    for number in range(4):
        x = jnp.where(kind == number + 1, mapped[number * rows : (number + 1) * rows], x)
    return x


def in_a_row(x):
    return jnp.concatenate([x[r : r + 1, :] for r in range(x.shape[0])], axis=1)


def gather_rows(tiles, sublane):
    tiles = [tiles[r] for r in (0, 4, 2, 6, 1, 5, 3, 7)]
    keep = (sublane & 4) == 0
    tiles = [
        jnp.where(keep, x, y) + pltpu.roll(jnp.where(keep, y, x), 4, 0)
        for x, y in zip(tiles[::2], tiles[1::2])
    ]
    for shift in (2, 1):
        keep = (sublane & shift) == 0
        tiles = [
            jnp.where(keep, x + pltpu.roll(x, 8 - shift, 0), y + pltpu.roll(y, shift, 0))
            for x, y in zip(tiles[::2], tiles[1::2])
        ]
    return tiles[0]


def rows_times(mat_ref, vec_ref, out_ref, outs, terms, group=32):
    width = vec_ref.shape[1]
    sublane = lax.broadcasted_iota(jnp.int32, (8, width), 0)
    vecs = [
        [vec_ref[c * terms + t : c * terms + t + 8, :] for t in range(0, terms, 8)]
        for c in range(COMP)
    ]

    def body(g, carry):
        for first in range(0, group, 8):
            sums = [[] for _ in range(COMP)]
            for r in range(first, first + 8):
                acc = [None] * COMP
                for j in range(terms // 8):
                    start = pl.multiple_of((g * group + r) * terms + 8 * j, 8)
                    tile = mat_ref[pl.ds(start, 8), :]
                    for c in range(COMP):
                        term = tile * vecs[c][j]
                        acc[c] = term if j == 0 else acc[c] + term
                for c in range(COMP):
                    sums[c].append(acc[c])
            for c in range(COMP):
                start = pl.multiple_of(c * outs + g * group + first, 8)
                out_ref[pl.ds(start, 8), :] = gather_rows(sums[c], sublane)
        return carry

    lax.fori_loop(0, outs // group, body, 0)


def columns_times(acc, mat_ref, vec_ref, outs, terms, unroll=16):
    def body(t, acc):
        acc = [list(a) for a in acc]
        vecs = [
            jnp.broadcast_to(vec_ref[pl.ds(c * terms + t, 1), :], (8, vec_ref.shape[1]))
            for c in range(COMP)
        ]
        for j in range(outs // 8):
            tile = mat_ref[pl.ds(pl.multiple_of(t * outs + j * 8, 8), 8), :]
            for c in range(COMP):
                acc[c][j] = acc[c][j] + tile * vecs[c]
        return acc

    return lax.fori_loop(0, terms, body, acc, unroll=unroll)


def tiles_of(ref, outs):
    return [[ref[c * outs + t : c * outs + t + 8, :] for t in range(0, outs, 8)] for c in range(COMP)]


def zeros(outs, width):
    return [[jnp.zeros((8, width), F32) for _ in range(outs // 8)] for _ in range(COMP)]


def face_columns(acc):
    half = NODES // 8
    return jnp.concatenate(
        [
            jnp.concatenate(
                [acc[c][f * half + h] for c in range(COMP) for h in range(half)], axis=0
            )
            for f in range(FACES)
        ],
        axis=1,
    )


def start_kernel(
    ranks, inner, trace, owned, cap,
    mortar_hbm, kind_hbm, force_hbm, back_hbm, inverse_hbm, couple_hbm, self_hbm,
    offer_ref, out_ref, onehot_ref, meta_ref, load_ref, inverse_ref, couple_ref, self_ref,
    mortar_ref, kind_ref, force_ref, back_ref, *sems,
):
    copies = [
        pltpu.make_async_copy(source, target, sem)
        for source, target, sem in zip(
            (mortar_hbm, kind_hbm, force_hbm, back_hbm, inverse_hbm, couple_hbm, self_hbm),
            (mortar_ref, kind_ref, force_ref, back_ref, inverse_ref, couple_ref, self_ref),
            sems,
        )
    ]
    for copy in copies:
        copy.start()
    copies[0].wait()
    copies[1].wait()
    width = mortar_ref.shape[1]
    slots = FACES * width
    mortar = mortar_ref[...]
    owner = lax.div(mortar, owned)
    index = lax.rem(mortar, owned)
    me = lax.rem(owner[0:1, 0:1] + 2, ranks)
    distance = lax.rem(owner - me + ranks, ranks)
    slot = lax.broadcasted_iota(jnp.int32, mortar.shape, 0) * width + lax.broadcasted_iota(
        jnp.int32, mortar.shape, 1
    )
    column = index
    begin = jnp.zeros((1, 1), jnp.int32)
    for number, away in enumerate((ranks - 2, ranks - 1, 0, 1, ranks // 2)):
        inside = distance == away
        count = jnp.sum(inside.astype(F32), keepdims=True).astype(jnp.int32)
        if away:
            run = number - (number > 2)
            column = jnp.where(inside, owned + run * cap + slot - begin, column)
        begin = begin + count
    target = lax.broadcasted_iota(jnp.int32, (1, slots), 1)
    target = lax.rem(target, width) * FACES + lax.div(target, width)
    order = jnp.where(
        lax.broadcasted_iota(jnp.int32, (slots, slots), 0) == target, 1.0, 0.0
    ).astype(BF16)
    facts = jnp.concatenate(
        [in_a_row(column), in_a_row(mortar + 1), in_a_row(kind_ref[...]), jnp.zeros((5, slots), jnp.int32)],
        axis=0,
    ).astype(F32)
    facts = exact_dot(facts, order)
    meta_ref[...] = facts
    meta_ref[3:4, :] = jnp.broadcast_to(lax.rem(me, 2).astype(F32), (1, slots))
    meta_ref[4:5, :] = jnp.broadcast_to((me * owned).astype(F32), (1, slots))
    column = facts[0:1, :].astype(jnp.int32)
    onehot_ref[...] = jnp.where(
        lax.broadcasted_iota(jnp.int32, onehot_ref.shape, 0) == column, 1.0, 0.0
    ).astype(BF16)
    copies[2].wait()
    copies[4].wait()
    rows_times(inverse_ref, force_ref, load_ref, inner, inner)
    copies[3].wait()
    copies[5].wait()
    y = columns_times(zeros(trace, width), couple_ref, load_ref, trace, inner)
    z = by_kind(face_columns(y), back_ref, facts[2:3, :])
    label = jnp.where(
        lax.broadcasted_iota(jnp.int32, (8, slots), 0) == 0, facts[1:2, :], 0.0
    )
    sums = exact_dot(jnp.concatenate([z, label], axis=0), onehot_ref[...], 1)
    count = RUNS * cap
    ids = lax.broadcasted_iota(jnp.int32, (8, owned), 1) + (me * owned + 1)
    ids = jnp.where(lax.broadcasted_iota(jnp.int32, (8, owned), 0) == 0, ids, 0)
    out_ref[...] = sums[:, owned:]
    offer_ref[:, :count] = sums[:, owned:]
    offer_ref[: COMP * NODES, count:] = sums[: COMP * NODES, :owned]
    offer_ref[COMP * NODES :, count:] = ids.astype(F32)
    copies[6].wait()


def onehot_of(condition):
    return jnp.where(condition, 1.0, 0.0).astype(BF16)


def own_ids(meta_ref, owned, count):
    base = meta_ref[4:5, :count].astype(jnp.int32)
    return lax.broadcasted_iota(jnp.int32, (owned, count), 0) + base + 1


def wanted_by(label, meta_ref, owned):
    count = label.shape[1]
    return onehot_of(own_ids(meta_ref, owned, count) == label.astype(jnp.int32))


def share(owned, sums, gid, label, meta_ref, own_ref, shared_ref):
    rows = COMP * NODES
    own = sums[:, :owned]
    own_ref[...] = own
    shared_ref[:rows, :] = sums[:, owned:]
    shared_ref[rows : 2 * rows, :] = exact_dot(own, wanted_by(label, meta_ref, owned))
    row = lax.broadcasted_iota(jnp.int32, (8, gid.shape[1]), 0)
    shared_ref[2 * rows :, :] = jnp.where(row == 0, gid, jnp.where(row == 1, label, 0.0))


def ids_down(ids, count):
    return jnp.broadcast_to(jnp.transpose(jnp.broadcast_to(ids, (8, ids.shape[1])))[:, 0:1], (ids.shape[1], count))


def laid_out(cap, *blocks):
    count = RUNS * cap
    lane = lax.broadcasted_iota(jnp.int32, (1, count), 1)
    result = jnp.zeros((COMP * NODES + 8, count), F32)
    for place, block in enumerate(blocks):
        if block is not None:
            array, run = block
            if run != place:
                array = pltpu.roll(array, ((place - run) % RUNS) * cap, 1)
            inside = (lane >= place * cap) & (lane < (place + 1) * cap)
            result = jnp.where(inside, array, result)
    return result


def first_pack_kernel(owned, cap, meta_ref, mine_ref, other_ref, one_ref, three_ref, four_ref):
    rows = COMP * NODES
    count = RUNS * cap
    laid = functools.partial(laid_out, cap)
    odd = meta_ref[3:4, :count] == 1.0
    odd_own = meta_ref[3:4, :owned] == 1.0
    outs = [mine_ref[:, :count], other_ref[:, :count]]
    fulls = []
    for source, target_ref, swap in ((outs[1], mine_ref, False), (outs[0], other_ref, True)):
        base = meta_ref[4:5, 0:1] + 1.0
        if swap:
            base = base + jnp.where(meta_ref[3:4, 0:1] == 1.0, -float(owned), float(owned))
        ids = lax.broadcasted_iota(jnp.int32, (owned, count), 0).astype(F32) + base
        match = onehot_of(ids == source[rows : rows + 1])
        full = target_ref[:rows, count:] + exact_dot(source[:rows], match, 1)
        fulls.append(jnp.concatenate([full, target_ref[rows:, count:]], axis=0))
    oe, oo = jnp.where(odd, outs[1], outs[0]), jnp.where(odd, outs[0], outs[1])
    one_ref[:, :count] = jnp.where(
        odd, laid((oe, 0), (oe, 1), None, (oo, 0)), laid(None, None, (oo, 2))
    )
    one_ref[:, count : count + owned] = jnp.where(odd_own, fulls[1], fulls[0])
    one_ref[:, count + owned :] = jnp.where(odd_own, fulls[0], fulls[1])
    three_ref[...] = jnp.where(
        odd, laid((oo, 3), None, (oo, 2), (oe, 3)), laid((oe, 0), (oe, 1), (oo, 0), (oe, 3))
    )
    four_ref[:, :count] = laid((oe, 3), (oo, 3))
    four_ref[:, count:] = fulls[0]


def pack_kernel(cap, meta_ref, mine_ref, other_ref, one_ref, three_ref, four_ref):
    rows = COMP * NODES
    count = RUNS * cap
    odd = meta_ref[3:4, :count] == 1.0
    mine, other = mine_ref[...], other_ref[...]
    even_part = jnp.where(odd, other, mine)
    odd_part = jnp.where(odd, mine, other)
    source = jnp.concatenate([even_part[:rows], odd_part[:rows]], axis=1)
    gids = jnp.concatenate([even_part[2 * rows : 2 * rows + 1], odd_part[2 * rows : 2 * rows + 1]], axis=1)
    blank = jnp.zeros((8, count), F32)
    sums = []
    for part in (even_part, odd_part):
        label = part[2 * rows + 1 : 2 * rows + 2]
        match = onehot_of((ids_down(label, 2 * count) == gids) & (gids > 0.0))
        full = part[rows : 2 * rows] + exact_dot(source, match, 1)
        sums.append(jnp.concatenate([full, blank], axis=0))
    outs = [
        jnp.concatenate([part[:rows], part[2 * rows : 2 * rows + 1], blank[1:]], axis=0)
        for part in (even_part, odd_part)
    ]
    laid = functools.partial(laid_out, cap)
    (oe, oo), (ge, go) = outs, sums
    one_ref[...] = jnp.where(
        odd, laid((oe, 0), (oe, 1), (ge, 2), (oo, 0)), laid((ge, 0), (go, 1), (oo, 2), (go, 0))
    )
    three_ref[...] = jnp.where(
        odd, laid((oo, 3), None, (oo, 2), (oe, 3)), laid((oe, 0), (oe, 1), (oo, 0), (oe, 3))
    )
    four_ref[...] = laid((oe, 3), (oo, 3), None, (jnp.where(odd, go, ge), 3))


def matched(owned, meta_ref, gid, sources, remote_sources=()):
    values = jnp.concatenate([v for v, _ in sources], axis=1)
    ids = jnp.concatenate([i for _, i in sources], axis=1)
    number = ids.shape[1]
    own = lax.broadcasted_iota(jnp.int32, (owned, number), 0).astype(F32) + (
        meta_ref[4:5, 0:1] + 1.0
    )
    gid = jnp.where(gid > 0.0, gid, -1.0)
    match = onehot_of(jnp.concatenate([own, ids_down(gid, number)], axis=0) == ids)
    sums = exact_dot(values, match, 1)
    field, remote = sums[:, :owned], sums[:, owned:]
    if remote_sources:
        values = jnp.concatenate([v for v, _ in remote_sources], axis=1)
        ids = jnp.concatenate([i for _, i in remote_sources], axis=1)
        remote = remote + exact_dot(values, onehot_of(ids_down(gid, ids.shape[1]) == ids), 1)
    return field, remote


def first_values(owned, cap, meta_ref, offers, blocks):
    rows = COMP * NODES
    count = RUNS * cap
    lane = lax.broadcasted_iota(jnp.int32, (1, count), 1)
    odd = meta_ref[3:4, :count] == 1.0
    mine_ref, other_ref, _ = offers
    one_ref, _, far_ref, passed_ref, _ = blocks
    sources = [(r[:rows, :count], r[rows : rows + 1, :count]) for r in (*offers, *blocks)]
    owners = [
        (r[:rows, count:], r[rows : rows + 1, count:])
        for r in (other_ref, one_ref, far_ref, passed_ref)
    ]
    gid = mine_ref[rows : rows + 1, :count]
    field, remote = matched(owned, meta_ref, gid, sources, owners)
    label_rows = slice(rows, rows + 8)
    other = other_ref[label_rows, :count]
    one = one_ref[label_rows, :count]
    far = far_ref[label_rows, :count]
    passed = passed_ref[label_rows, :count]
    even_form = jnp.where(
        lane < cap,
        one,
        jnp.where(
            lane < 2 * cap, other, jnp.where(lane < 3 * cap, passed, pltpu.roll(far, 3 * cap, 1))
        ),
    )
    odd_form = jnp.where(
        lane < cap,
        pltpu.roll(passed, cap, 1),
        jnp.where(
            lane < 2 * cap, passed, jnp.where(lane < 3 * cap, other, pltpu.roll(far, 2 * cap, 1))
        ),
    )
    label = jnp.where(odd, odd_form, even_form)
    return mine_ref[:rows, count:] + field, remote, gid, label


def fused_values(owned, cap, meta_ref, own_ref, offers, blocks):
    rows = COMP * NODES
    count = RUNS * cap
    lane = lax.broadcasted_iota(jnp.int32, (1, count), 1)
    odd = meta_ref[3:4, :count] == 1.0
    sources = [(r[:rows], r[2 * rows : 2 * rows + 1]) for r in offers]
    sources += [(r[:rows], r[rows : rows + 1]) for r in blocks]
    field, remote = matched(owned, meta_ref, offers[0][2 * rows : 2 * rows + 1], sources)
    near, _, far, across, _ = (r[:rows] for r in blocks)
    partner = offers[1][rows : 2 * rows]
    even_form = jnp.where(lane < 2 * cap, across, jnp.where(lane < 3 * cap, partner, far))
    odd_form = jnp.where(
        lane < cap,
        pltpu.roll(near, cap, 1),
        jnp.where(lane < 2 * cap, partner, jnp.where(lane < 3 * cap, across, far)),
    )
    return own_ref[...] + field, jnp.where(odd, odd_form, even_form) + remote


def element_values(field, received, meta_ref, onehot_ref, forth_ref, spread_ref):
    source = jnp.concatenate([field, received], axis=1)
    kind = meta_ref[2:3, :]
    faces = by_kind(exact_dot(source, onehot_ref[...]), forth_ref, kind)
    width = spread_ref.shape[1]
    for c in range(COMP):
        for f in range(FACES):
            spread_ref[(c * FACES + f) * NODES : (c * FACES + f + 1) * NODES, :] = faces[
                c * NODES : (c + 1) * NODES, f * width : (f + 1) * width
            ]
    return kind


def apply_kernel(
    inner, trace, owned, cap, fused,
    meta_ref, onehot_ref, forth_ref, back_ref, inverse_ref, couple_ref, self_ref,
    *refs,
):
    if fused:
        gid_ref, label_ref, before_ref, *received = refs[:11]
        field_ref, *refs = refs[11:]
        gid, label = gid_ref[0:1, :], label_ref[0:1, :]
        field, received = fused_values(
            owned, cap, meta_ref, before_ref, received[:3], received[3:]
        )
    else:
        field_ref, gid_ref, label_ref, *after = refs[8:]
        field, received, gid, label = first_values(owned, cap, meta_ref, refs[:3], refs[3:8])
        refs = after
        gid_ref[...] = jnp.broadcast_to(gid, gid_ref.shape)
        label_ref[...] = label
        label = label[0:1, :]
    field_ref[...] = field
    own_ref, shared_ref, spread_ref, mid_ref, weight_ref, image_ref = refs
    width = spread_ref.shape[1]
    kind = element_values(field, received, meta_ref, onehot_ref, forth_ref, spread_ref)
    rows_times(couple_ref, spread_ref, mid_ref, inner, trace)
    rows_times(inverse_ref, mid_ref, weight_ref, inner, inner)
    rows_times(self_ref, spread_ref, image_ref, trace, trace)
    y = columns_times(tiles_of(image_ref, trace), couple_ref, weight_ref, trace, inner)
    z = by_kind(face_columns(y), back_ref, kind)
    sums = exact_dot(z, onehot_ref[...], 1)
    share(owned, sums, gid, label, meta_ref, own_ref, shared_ref)


def total(x):
    return jnp.sum(jnp.sum(x, axis=0, keepdims=True), axis=1, keepdims=True)


def last_kernel(
    inner, trace, owned, cap,
    meta_ref, onehot_ref, forth_ref, inverse_ref, couple_ref, self_ref,
    k0_ref, k1_ref, s0_ref, s1_ref, u0_ref, u1_ref, before_ref, *refs,
):
    received, refs = refs[:8], refs[8:]
    k2_ref, weight_ref, moment_ref, spread_ref, mid_ref, image_ref = refs
    width = spread_ref.shape[1]
    field, received = fused_values(
        owned, cap, meta_ref, before_ref, received[:3], received[3:]
    )
    k2_ref[...] = field
    element_values(field, received, meta_ref, onehot_ref, forth_ref, spread_ref)
    rows_times(couple_ref, spread_ref, mid_ref, inner, trace)
    rows_times(inverse_ref, mid_ref, weight_ref, inner, inner)
    rows_times(self_ref, spread_ref, image_ref, trace, trace)
    image, weight = image_ref[...], weight_ref[...]
    ks = (k0_ref[...], k1_ref[...], field)
    values = [total(ks[i] * ks[j]) for i in range(3) for j in range(i, 3)]
    for s_ref, u_ref in ((s0_ref, u0_ref), (s1_ref, u1_ref), (spread_ref, mid_ref)):
        values.append(total(s_ref[...] * image) + total(u_ref[...] * weight))
    lane = lax.broadcasted_iota(jnp.int32, (1, width), 1)
    row = jnp.zeros((1, width), F32)
    for number, value in enumerate(values):
        row = jnp.where(lane == number, value, row)
    moment_ref[...] = jnp.broadcast_to(row[None], moment_ref.shape)


def finish_kernel(
    moment_ref, k0_ref, k1_ref, k2_ref, w0_ref, w1_ref, w2_ref, load_ref, field_ref, interior_ref
):
    sums = jnp.sum(moment_ref[...], axis=0)
    m = [sums[:, n : n + 1] for n in range(9)]
    gram = [[m[0], m[1], m[2]], [m[1], m[3], m[4]], [m[2], m[4], m[5]]]
    energy = [[gram[i][1], gram[i][2], m[6 + i]] for i in range(3)]

    def form(x, matrix):
        return sum(x[i] * sum(matrix[i][j] * x[j] for j in range(3)) for i in range(3))

    zero, one = jnp.zeros((1, 1), F32), jnp.ones((1, 1), F32)
    x = [zero, zero, zero]
    r = [one, zero, zero]
    d = [one, zero, zero]
    current = gram[0][0]
    for iteration in range(3):
        step = current / form(d, energy)
        x = [x[i] + step * d[i] for i in range(3)]
        if iteration < 2:
            r = [r[0], r[1] - step * d[0], r[2] - step * d[1]]
            following = form(r, gram)
            d = [r[i] + following / current * d[i] for i in range(3)]
            current = following
    field_ref[...] = x[0] * k0_ref[...] + x[1] * k1_ref[...] + x[2] * k2_ref[...]
    interior_ref[...] = load_ref[...] - (
        x[0] * w0_ref[...] + x[1] * w1_ref[...] + x[2] * w2_ref[...]
    )


def call(kernel, outs, *args, scratch=(), in_hbm=0, vmem=8):
    inside = len(args) - in_hbm
    args = args[:inside] + tuple(
        pltpu.with_memory_space_constraint(x, pltpu.HBM) for x in args[inside:]
    )
    return pl.pallas_call(
        kernel,
        out_shape=[jax.ShapeDtypeStruct(shape, dtype) for shape, dtype in outs],
        in_specs=[pl.BlockSpec(memory_space=pltpu.VMEM)] * inside
        + [pl.BlockSpec(memory_space=pltpu.HBM)] * in_hbm,
        out_specs=[pl.BlockSpec(memory_space=pltpu.VMEM)] * len(outs),
        scratch_shapes=[pltpu.VMEM(shape, dtype) for shape, dtype in scratch]
        + [pltpu.SemaphoreType.DMA(())] * in_hbm,
        compiler_params=pltpu.CompilerParams(vmem_limit_bytes=vmem * 1024 * 1024),
    )(*args)


def fused_exchange(meta, shared, out, ranks, kernel, widths):
    pair = [(r, r ^ 1) for r in range(ranks)]

    def both_ways(chips):
        ahead = [(r, (r + 2 * chips + 1) % ranks) for r in range(0, ranks, 2)]
        return ahead + [(t, r) for r, t in ahead]

    skip = [(r, (r + (3 if r % 2 else ranks - 3)) % ranks) for r in range(ranks)]
    far = [(r, (r + ranks // 2) % ranks) for r in range(ranks)]
    second = lax.ppermute(out, AXES, skip)
    other = lax.ppermute(shared, AXES, pair)
    packed = call(
        kernel, [((COMP * NODES + 8, width), F32) for width in widths], meta, shared, other
    )
    got = [
        lax.ppermute(block, AXES, way)
        for block, way in zip(packed, (both_ways(1), both_ways(ranks // 4 - 1), far))
    ]
    second, *got = lax.optimization_barrier((second, *got))
    passed = [lax.ppermute(block, AXES, pair) for block in got[:2]]
    return [shared, other, second, *got, *passed]


def local(self_block, couple, inverse, body_force, face_mortar, face_kind, *, ranks):
    trace, _, elements = self_block.shape
    inner = inverse.shape[0]
    owned = 2 * elements
    cap = max(2, elements // 4)
    width = elements
    rows = COMP * NODES
    count = RUNS * cap
    forward, backward = block_tables()
    mortar = face_mortar.reshape(FACES, width)
    kind = face_kind.reshape(FACES, width)
    self_block = self_block.reshape(trace * trace, width)
    couple = couple.reshape(inner * trace, width)
    inverse = inverse.reshape(inner * inner, width)
    force = body_force.reshape(COMP * inner, width)

    offer, out, onehot, meta, load, *matrices = call(
        functools.partial(start_kernel, ranks, inner, trace, owned, cap),
        [
            ((rows + 8, count + owned), F32),
            ((rows + 8, count), F32),
            ((owned + count, FACES * width), BF16),
            ((8, FACES * width), F32),
            ((COMP * inner, width), F32),
            (inverse.shape, F32),
            (couple.shape, F32),
            (self_block.shape, F32),
        ],
        mortar, kind, force, backward, inverse, couple, self_block,
        scratch=[
            (mortar.shape, jnp.int32), (kind.shape, jnp.int32), (force.shape, F32), (backward.shape, F32)
        ],
        in_hbm=7, vmem=16,
    )
    blocks = fused_exchange(
        meta, offer, out, ranks,
        functools.partial(first_pack_kernel, owned, cap),
        (count + 2 * owned, count, count + owned),
    )
    fields, spreads, mids, weights, ids, own = [], [], [], [], [], None
    for iteration in range(2):
        fused = iteration > 0
        first = [((rows, owned), F32)] + ([] if fused else [((8, count), F32)] * 2)
        results = call(
            functools.partial(apply_kernel, inner, trace, owned, cap, fused),
            first + [
                ((rows, owned), F32),
                ((2 * rows + 8, count), F32),
                ((COMP * trace, width), F32),
                ((COMP * inner, width), F32),
                ((COMP * inner, width), F32),
            ],
            meta, onehot, forward, backward, *matrices, *([*ids, own] if fused else []), *blocks,
            scratch=[((COMP * trace, width), F32)],
        )
        fields.append(results[0])
        ids = ids or results[1 : len(first)]
        own, shared, spread, mid, weight = results[len(first) :]
        spreads.append(spread)
        mids.append(mid)
        weights.append(weight)
        blocks = fused_exchange(
            meta, shared, shared, ranks, functools.partial(pack_kernel, cap), (count,) * 3
        )
    field, weight, moments = call(
        functools.partial(last_kernel, inner, trace, owned, cap),
        [((rows, owned), F32), ((COMP * inner, width), F32), ((ranks, 1, width), F32)],
        meta, onehot, forward, *matrices, *fields, *spreads, *mids, own, *blocks,
        scratch=[
            ((COMP * trace, width), F32),
            ((COMP * inner, width), F32),
            ((COMP * trace, width), F32),
        ],
    )
    fields.append(field)
    weights.append(weight)
    moments = lax.all_to_all(moments, AXES, split_axis=0, concat_axis=0, tiled=True)
    trace_field, interior = call(
        finish_kernel,
        [((rows, owned), F32), ((COMP * inner, width), F32)],
        moments, *fields, *weights, load,
    )
    return trace_field, interior.reshape(COMP, inner, elements)


def solution(mesh):
    placed = (
        P(None, None, AXES),
        P(None, None, AXES),
        P(None, None, AXES),
        P(None, None, AXES),
        P(AXES),
        P(AXES),
    )
    ranks = int(np.prod([mesh.shape[a] for a in AXES]))
    return jax.shard_map(
        functools.partial(local, ranks=ranks),
        mesh=mesh,
        in_specs=placed,
        out_specs=(P(None, AXES), P(None, None, AXES)),
        check_vma=False,
    )
```

```python
import functools

import jax
import jax.numpy as jnp
import numpy as np
from jax import lax
from jax.experimental import pallas as pl
from jax.experimental.pallas import tpu as pltpu
from jax.sharding import PartitionSpec as P

AXES = ("dom", "blk")
COMP = 3
NODES = 16
FACES = 6
RUNS = 4
F32 = jnp.float32
BF16 = jnp.bfloat16


def interp_tables():
    abscissae = -np.cos(np.pi * np.arange(4) / 3.0)

    def lagrange(points):
        columns = [
            np.prod(
                [
                    (points - abscissae[other_node])
                    / (abscissae[basis_node] - abscissae[other_node])
                    for other_node in range(4)
                    if other_node != basis_node
                ],
                axis=0,
            )
            for basis_node in range(4)
        ]
        return np.stack(columns, axis=1)

    lower_map = lagrange((abscissae - 1.0) / 2.0)
    upper_map = lagrange((abscissae + 1.0) / 2.0)
    return np.stack(
        [
            np.kron(lower_map, lower_map),
            np.kron(lower_map, upper_map),
            np.kron(upper_map, lower_map),
            np.kron(upper_map, upper_map),
        ]
    ).astype(np.float32)


def block_tables():
    tables = interp_tables()
    eye = np.eye(COMP, dtype=np.float32)
    forward = np.concatenate([np.kron(eye, t) for t in tables])
    backward = np.concatenate([np.kron(eye, t.T) for t in tables])
    return forward, backward


def split(x):
    hi = x.astype(BF16)
    return hi, (x - hi.astype(F32)).astype(BF16)


def dot(a, b, rhs_dim=0):
    return lax.dot_general(a, b, (((1,), (rhs_dim,)), ((), ())), preferred_element_type=F32)


def exact_dot(x, onehot, rhs_dim=0):
    hi, lo = split(x)
    both = dot(jnp.concatenate([hi, lo], axis=0), onehot, rhs_dim)
    return both[: x.shape[0]] + both[x.shape[0] :]


def by_kind(x, table_ref, kind):
    rows = x.shape[0]
    t_hi, t_lo = split(table_ref[...])
    x_hi, x_lo = split(x)
    mapped = dot(
        jnp.concatenate([t_hi, t_hi, t_lo], axis=1), jnp.concatenate([x_hi, x_lo, x_hi], axis=0)
    )
    for number in range(4):
        x = jnp.where(kind == number + 1, mapped[number * rows : (number + 1) * rows], x)
    return x


def in_a_row(x):
    return jnp.concatenate([x[r : r + 1, :] for r in range(x.shape[0])], axis=1)


def gather_rows(tiles, sublane):
    tiles = [tiles[r] for r in (0, 4, 2, 6, 1, 5, 3, 7)]
    keep = (sublane & 4) == 0
    tiles = [
        jnp.where(keep, x, y) + pltpu.roll(jnp.where(keep, y, x), 4, 0)
        for x, y in zip(tiles[::2], tiles[1::2])
    ]
    for shift in (2, 1):
        keep = (sublane & shift) == 0
        tiles = [
            jnp.where(keep, x + pltpu.roll(x, 8 - shift, 0), y + pltpu.roll(y, shift, 0))
            for x, y in zip(tiles[::2], tiles[1::2])
        ]
    return tiles[0]


def rows_times(mat_ref, vec_ref, out_ref, outs, terms, group=32):
    width = vec_ref.shape[1]
    sublane = lax.broadcasted_iota(jnp.int32, (8, width), 0)
    vecs = [
        [vec_ref[c * terms + t : c * terms + t + 8, :] for t in range(0, terms, 8)]
        for c in range(COMP)
    ]

    def body(g, carry):
        for first in range(0, group, 8):
            sums = [[] for _ in range(COMP)]
            for r in range(first, first + 8):
                acc = [None] * COMP
                for j in range(terms // 8):
                    start = pl.multiple_of((g * group + r) * terms + 8 * j, 8)
                    tile = mat_ref[pl.ds(start, 8), :]
                    for c in range(COMP):
                        term = tile * vecs[c][j]
                        acc[c] = term if j == 0 else acc[c] + term
                for c in range(COMP):
                    sums[c].append(acc[c])
            for c in range(COMP):
                start = pl.multiple_of(c * outs + g * group + first, 8)
                out_ref[pl.ds(start, 8), :] = gather_rows(sums[c], sublane)
        return carry

    lax.fori_loop(0, outs // group, body, 0)


def columns_times(acc, mat_ref, vec_ref, outs, terms, unroll=16):
    def body(t, acc):
        acc = [list(a) for a in acc]
        vecs = [
            jnp.broadcast_to(vec_ref[pl.ds(c * terms + t, 1), :], (8, vec_ref.shape[1]))
            for c in range(COMP)
        ]
        for j in range(outs // 8):
            tile = mat_ref[pl.ds(pl.multiple_of(t * outs + j * 8, 8), 8), :]
            for c in range(COMP):
                acc[c][j] = acc[c][j] + tile * vecs[c]
        return acc

    return lax.fori_loop(0, terms, body, acc, unroll=unroll)


def tiles_of(ref, outs):
    return [[ref[c * outs + t : c * outs + t + 8, :] for t in range(0, outs, 8)] for c in range(COMP)]


def zeros(outs, width):
    return [[jnp.zeros((8, width), F32) for _ in range(outs // 8)] for _ in range(COMP)]


def face_columns(acc):
    half = NODES // 8
    return jnp.concatenate(
        [
            jnp.concatenate(
                [acc[c][f * half + h] for c in range(COMP) for h in range(half)], axis=0
            )
            for f in range(FACES)
        ],
        axis=1,
    )


def start_kernel(
    ranks, inner, trace, owned, cap,
    mortar_hbm, kind_hbm, force_hbm, back_hbm, inverse_hbm, couple_hbm,
    offer_ref, out_ref, onehot_ref, meta_ref, load_ref, inverse_ref, couple_ref,
    mortar_ref, kind_ref, force_ref, back_ref, *sems,
):
    copies = [
        pltpu.make_async_copy(source, target, sem)
        for source, target, sem in zip(
            (mortar_hbm, kind_hbm, force_hbm, back_hbm, inverse_hbm, couple_hbm),
            (mortar_ref, kind_ref, force_ref, back_ref, inverse_ref, couple_ref),
            sems,
        )
    ]
    for copy in copies:
        copy.start()
    copies[0].wait()
    copies[1].wait()
    width = mortar_ref.shape[1]
    slots = FACES * width
    mortar = mortar_ref[...]
    owner = lax.div(mortar, owned)
    index = lax.rem(mortar, owned)
    me = lax.rem(owner[0:1, 0:1] + 2, ranks)
    distance = lax.rem(owner - me + ranks, ranks)
    slot = lax.broadcasted_iota(jnp.int32, mortar.shape, 0) * width + lax.broadcasted_iota(
        jnp.int32, mortar.shape, 1
    )
    column = index
    begin = jnp.zeros((1, 1), jnp.int32)
    for number, away in enumerate((ranks - 2, ranks - 1, 0, 1, ranks // 2)):
        inside = distance == away
        count = jnp.sum(inside.astype(F32), keepdims=True).astype(jnp.int32)
        if away:
            run = number - (number > 2)
            column = jnp.where(inside, owned + run * cap + slot - begin, column)
        begin = begin + count
    target = lax.broadcasted_iota(jnp.int32, (1, slots), 1)
    target = lax.rem(target, width) * FACES + lax.div(target, width)
    order = jnp.where(
        lax.broadcasted_iota(jnp.int32, (slots, slots), 0) == target, 1.0, 0.0
    ).astype(BF16)
    facts = jnp.concatenate(
        [in_a_row(column), in_a_row(mortar + 1), in_a_row(kind_ref[...]), jnp.zeros((5, slots), jnp.int32)],
        axis=0,
    ).astype(F32)
    facts = exact_dot(facts, order)
    meta_ref[...] = facts
    meta_ref[3:4, :] = jnp.broadcast_to(lax.rem(me, 2).astype(F32), (1, slots))
    meta_ref[4:5, :] = jnp.broadcast_to((me * owned).astype(F32), (1, slots))
    column = facts[0:1, :].astype(jnp.int32)
    onehot_ref[...] = jnp.where(
        lax.broadcasted_iota(jnp.int32, onehot_ref.shape, 0) == column, 1.0, 0.0
    ).astype(BF16)
    copies[2].wait()
    copies[4].wait()
    rows_times(inverse_ref, force_ref, load_ref, inner, inner)
    copies[3].wait()
    copies[5].wait()
    y = columns_times(zeros(trace, width), couple_ref, load_ref, trace, inner)
    z = by_kind(face_columns(y), back_ref, facts[2:3, :])
    label = jnp.where(
        lax.broadcasted_iota(jnp.int32, (8, slots), 0) == 0, facts[1:2, :], 0.0
    )
    sums = exact_dot(jnp.concatenate([z, label], axis=0), onehot_ref[...], 1)
    count = RUNS * cap
    ids = lax.broadcasted_iota(jnp.int32, (8, owned), 1) + (me * owned + 1)
    ids = jnp.where(lax.broadcasted_iota(jnp.int32, (8, owned), 0) == 0, ids, 0)
    out_ref[...] = sums[:, owned:]
    offer_ref[:, :count] = sums[:, owned:]
    offer_ref[: COMP * NODES, count:] = sums[: COMP * NODES, :owned]
    offer_ref[COMP * NODES :, count:] = ids.astype(F32)


def onehot_of(condition):
    return jnp.where(condition, 1.0, 0.0).astype(BF16)


def own_ids(meta_ref, owned, count):
    base = meta_ref[4:5, :count].astype(jnp.int32)
    return lax.broadcasted_iota(jnp.int32, (owned, count), 0) + base + 1


def wanted_by(label, meta_ref, owned):
    count = label.shape[1]
    return onehot_of(own_ids(meta_ref, owned, count) == label.astype(jnp.int32))


def share(owned, sums, gid, label, meta_ref, own_ref, shared_ref):
    rows = COMP * NODES
    own = sums[:, :owned]
    own_ref[...] = own
    shared_ref[:rows, :] = sums[:, owned:]
    shared_ref[rows : 2 * rows, :] = exact_dot(own, wanted_by(label, meta_ref, owned))
    row = lax.broadcasted_iota(jnp.int32, (8, gid.shape[1]), 0)
    shared_ref[2 * rows :, :] = jnp.where(row == 0, gid, jnp.where(row == 1, label, 0.0))


def ids_down(ids, count):
    return jnp.broadcast_to(jnp.transpose(jnp.broadcast_to(ids, (8, ids.shape[1])))[:, 0:1], (ids.shape[1], count))


def laid_out(cap, *blocks):
    count = RUNS * cap
    lane = lax.broadcasted_iota(jnp.int32, (1, count), 1)
    result = jnp.zeros((COMP * NODES + 8, count), F32)
    for place, block in enumerate(blocks):
        if block is not None:
            array, run = block
            if run != place:
                array = pltpu.roll(array, ((place - run) % RUNS) * cap, 1)
            inside = (lane >= place * cap) & (lane < (place + 1) * cap)
            result = jnp.where(inside, array, result)
    return result


def first_pack_kernel(owned, cap, meta_ref, mine_ref, other_ref, one_ref, three_ref, four_ref):
    rows = COMP * NODES
    count = RUNS * cap
    laid = functools.partial(laid_out, cap)
    odd = meta_ref[3:4, :count] == 1.0
    odd_own = meta_ref[3:4, :owned] == 1.0
    outs = [mine_ref[:, :count], other_ref[:, :count]]
    fulls = []
    for source, target_ref, swap in ((outs[1], mine_ref, False), (outs[0], other_ref, True)):
        base = meta_ref[4:5, 0:1] + 1.0
        if swap:
            base = base + jnp.where(meta_ref[3:4, 0:1] == 1.0, -float(owned), float(owned))
        ids = lax.broadcasted_iota(jnp.int32, (owned, count), 0).astype(F32) + base
        match = onehot_of(ids == source[rows : rows + 1])
        full = target_ref[:rows, count:] + exact_dot(source[:rows], match, 1)
        fulls.append(jnp.concatenate([full, target_ref[rows:, count:]], axis=0))
    oe, oo = jnp.where(odd, outs[1], outs[0]), jnp.where(odd, outs[0], outs[1])
    one_ref[:, :count] = jnp.where(
        odd, laid((oe, 0), (oe, 1), None, (oo, 0)), laid(None, None, (oo, 2))
    )
    one_ref[:, count : count + owned] = jnp.where(odd_own, fulls[1], fulls[0])
    one_ref[:, count + owned :] = jnp.where(odd_own, fulls[0], fulls[1])
    three_ref[...] = jnp.where(
        odd, laid((oo, 3), None, (oo, 2), (oe, 3)), laid((oe, 0), (oe, 1), (oo, 0), (oe, 3))
    )
    four_ref[:, :count] = laid((oe, 3), (oo, 3))
    four_ref[:, count:] = fulls[0]


def pack_kernel(cap, meta_ref, mine_ref, other_ref, one_ref, three_ref, four_ref):
    rows = COMP * NODES
    count = RUNS * cap
    odd = meta_ref[3:4, :count] == 1.0
    mine, other = mine_ref[...], other_ref[...]
    even_part = jnp.where(odd, other, mine)
    odd_part = jnp.where(odd, mine, other)
    source = jnp.concatenate([even_part[:rows], odd_part[:rows]], axis=1)
    gids = jnp.concatenate([even_part[2 * rows : 2 * rows + 1], odd_part[2 * rows : 2 * rows + 1]], axis=1)
    blank = jnp.zeros((8, count), F32)
    sums = []
    for part in (even_part, odd_part):
        label = part[2 * rows + 1 : 2 * rows + 2]
        match = onehot_of((ids_down(label, 2 * count) == gids) & (gids > 0.0))
        full = part[rows : 2 * rows] + exact_dot(source, match, 1)
        sums.append(jnp.concatenate([full, blank], axis=0))
    outs = [
        jnp.concatenate([part[:rows], part[2 * rows : 2 * rows + 1], blank[1:]], axis=0)
        for part in (even_part, odd_part)
    ]
    laid = functools.partial(laid_out, cap)
    (oe, oo), (ge, go) = outs, sums
    one_ref[...] = jnp.where(
        odd, laid((oe, 0), (oe, 1), (ge, 2), (oo, 0)), laid((ge, 0), (go, 1), (oo, 2), (go, 0))
    )
    three_ref[...] = jnp.where(
        odd, laid((oo, 3), None, (oo, 2), (oe, 3)), laid((oe, 0), (oe, 1), (oo, 0), (oe, 3))
    )
    four_ref[...] = laid((oe, 3), (oo, 3), None, (jnp.where(odd, go, ge), 3))


def first_match(owned, meta_ref, gid, ids):
    number = ids.shape[1]
    own = lax.broadcasted_iota(jnp.int32, (owned, number), 0).astype(F32) + (
        meta_ref[4:5, 0:1] + 1.0
    )
    return onehot_of(jnp.concatenate([own, ids_down(gid, number)], axis=0) == ids)


def first_values(owned, cap, meta_ref, offers, blocks, match_ref):
    rows = COMP * NODES
    count = RUNS * cap
    lane = lax.broadcasted_iota(jnp.int32, (1, count), 1)
    odd = meta_ref[3:4, :count] == 1.0
    mine_ref, other_ref, _ = offers
    one_ref, _, far_ref, passed_ref, _ = blocks
    refs = (*offers, *blocks)
    owners = (other_ref, one_ref, far_ref, passed_ref)
    gid = mine_ref[rows : rows + 1, :count]
    wish = jnp.where(gid > 0.0, gid, -1.0)
    ids = jnp.concatenate([r[rows : rows + 1, :count] for r in refs], axis=1)
    match_ref[...] = first_match(owned, meta_ref, wish, ids)
    source = jnp.concatenate([r[:rows, :count] for r in refs], axis=1)
    sums = exact_dot(source, match_ref[...], 1)
    ids = jnp.concatenate([r[rows : rows + 1, count:] for r in owners], axis=1)
    source = jnp.concatenate([r[:rows, count:] for r in owners], axis=1)
    field = sums[:, :owned]
    remote = sums[:, owned:] + exact_dot(source, onehot_of(ids_down(wish, ids.shape[1]) == ids), 1)
    label_rows = slice(rows, rows + 8)
    other = other_ref[label_rows, :count]
    one = one_ref[label_rows, :count]
    far = far_ref[label_rows, :count]
    passed = passed_ref[label_rows, :count]
    even_form = jnp.where(
        lane < cap,
        one,
        jnp.where(
            lane < 2 * cap, other, jnp.where(lane < 3 * cap, passed, pltpu.roll(far, 3 * cap, 1))
        ),
    )
    odd_form = jnp.where(
        lane < cap,
        pltpu.roll(passed, cap, 1),
        jnp.where(
            lane < 2 * cap, passed, jnp.where(lane < 3 * cap, other, pltpu.roll(far, 2 * cap, 1))
        ),
    )
    label = jnp.where(odd, odd_form, even_form)
    return mine_ref[:rows, count:] + field, remote, gid, label


def fused_values(owned, cap, meta_ref, own_ref, match_ref, offers, blocks):
    rows = COMP * NODES
    count = RUNS * cap
    lane = lax.broadcasted_iota(jnp.int32, (1, count), 1)
    odd = meta_ref[3:4, :count] == 1.0
    source = jnp.concatenate([r[:rows] for r in (*offers, *blocks)], axis=1)
    sums = exact_dot(source, match_ref[...], 1)
    field, remote = sums[:, :owned], sums[:, owned:]
    near, _, far, across, _ = (r[:rows] for r in blocks)
    partner = offers[1][rows : 2 * rows]
    even_form = jnp.where(lane < 2 * cap, across, jnp.where(lane < 3 * cap, partner, far))
    odd_form = jnp.where(
        lane < cap,
        pltpu.roll(near, cap, 1),
        jnp.where(lane < 2 * cap, partner, jnp.where(lane < 3 * cap, across, far)),
    )
    return own_ref[...] + field, jnp.where(odd, odd_form, even_form) + remote


def element_values(field, received, meta_ref, onehot_ref, forth_ref, spread_ref):
    source = jnp.concatenate([field, received], axis=1)
    kind = meta_ref[2:3, :]
    faces = by_kind(exact_dot(source, onehot_ref[...]), forth_ref, kind)
    width = spread_ref.shape[1]
    for c in range(COMP):
        for f in range(FACES):
            spread_ref[(c * FACES + f) * NODES : (c * FACES + f + 1) * NODES, :] = faces[
                c * NODES : (c + 1) * NODES, f * width : (f + 1) * width
            ]
    return kind


def apply_kernel(
    inner, trace, owned, cap, fused,
    meta_ref, onehot_ref, forth_ref, back_ref, inverse_ref, couple_ref,
    *refs,
):
    copy = None
    if fused:
        self_ref, gid_ref, label_ref, match_ref, before_ref, *received = refs[:13]
        field_ref, *refs = refs[13:]
        gid, label = gid_ref[0:1, :], label_ref[0:1, :]
        field, received = fused_values(
            owned, cap, meta_ref, before_ref, match_ref, received[:3], received[3:]
        )
    else:
        self_hbm, field_ref, self_ref, gid_ref, label_ref, match_ref, *after, sem = refs[8:]
        copy = pltpu.make_async_copy(self_hbm, self_ref, sem)
        copy.start()
        field, received, gid, label = first_values(
            owned, cap, meta_ref, refs[:3], refs[3:8], match_ref
        )
        refs = after
        gid_ref[...] = jnp.broadcast_to(gid, gid_ref.shape)
        label_ref[...] = label
        label = label[0:1, :]
    field_ref[...] = field
    own_ref, shared_ref, spread_ref, mid_ref, weight_ref, image_ref = refs
    width = spread_ref.shape[1]
    kind = element_values(field, received, meta_ref, onehot_ref, forth_ref, spread_ref)
    rows_times(couple_ref, spread_ref, mid_ref, inner, trace)
    rows_times(inverse_ref, mid_ref, weight_ref, inner, inner)
    if copy is not None:
        copy.wait()
    rows_times(self_ref, spread_ref, image_ref, trace, trace)
    y = columns_times(tiles_of(image_ref, trace), couple_ref, weight_ref, trace, inner)
    z = by_kind(face_columns(y), back_ref, kind)
    sums = exact_dot(z, onehot_ref[...], 1)
    share(owned, sums, gid, label, meta_ref, own_ref, shared_ref)


def total(x):
    return jnp.sum(jnp.sum(x, axis=0, keepdims=True), axis=1, keepdims=True)


def last_kernel(
    inner, trace, owned, cap,
    meta_ref, onehot_ref, forth_ref, inverse_ref, couple_ref, self_ref,
    match_ref, k0_ref, k1_ref, s0_ref, s1_ref, u0_ref, u1_ref, before_ref, *refs,
):
    received, refs = refs[:8], refs[8:]
    k2_ref, weight_ref, moment_ref, spread_ref, mid_ref, image_ref = refs
    width = spread_ref.shape[1]
    field, received = fused_values(
        owned, cap, meta_ref, before_ref, match_ref, received[:3], received[3:]
    )
    k2_ref[...] = field
    element_values(field, received, meta_ref, onehot_ref, forth_ref, spread_ref)
    rows_times(couple_ref, spread_ref, mid_ref, inner, trace)
    rows_times(inverse_ref, mid_ref, weight_ref, inner, inner)
    rows_times(self_ref, spread_ref, image_ref, trace, trace)
    image, weight = image_ref[...], weight_ref[...]
    ks = (k0_ref[...], k1_ref[...], field)
    values = [total(ks[i] * ks[j]) for i in range(3) for j in range(i, 3)]
    for s_ref, u_ref in ((s0_ref, u0_ref), (s1_ref, u1_ref), (spread_ref, mid_ref)):
        values.append(total(s_ref[...] * image) + total(u_ref[...] * weight))
    lane = lax.broadcasted_iota(jnp.int32, (1, width), 1)
    row = jnp.zeros((1, width), F32)
    for number, value in enumerate(values):
        row = jnp.where(lane == number, value, row)
    moment_ref[...] = jnp.broadcast_to(row[None], moment_ref.shape)


def finish_kernel(
    moment_ref, k0_ref, k1_ref, k2_ref, w0_ref, w1_ref, w2_ref, load_ref, field_ref, interior_ref
):
    sums = jnp.sum(moment_ref[...], axis=0)
    m = [sums[:, n : n + 1] for n in range(9)]
    gram = [[m[0], m[1], m[2]], [m[1], m[3], m[4]], [m[2], m[4], m[5]]]
    energy = [[gram[i][1], gram[i][2], m[6 + i]] for i in range(3)]

    def form(x, matrix):
        return sum(x[i] * sum(matrix[i][j] * x[j] for j in range(3)) for i in range(3))

    zero, one = jnp.zeros((1, 1), F32), jnp.ones((1, 1), F32)
    x = [zero, zero, zero]
    r = [one, zero, zero]
    d = [one, zero, zero]
    current = gram[0][0]
    for iteration in range(3):
        step = current / form(d, energy)
        x = [x[i] + step * d[i] for i in range(3)]
        if iteration < 2:
            r = [r[0], r[1] - step * d[0], r[2] - step * d[1]]
            following = form(r, gram)
            d = [r[i] + following / current * d[i] for i in range(3)]
            current = following
    field_ref[...] = x[0] * k0_ref[...] + x[1] * k1_ref[...] + x[2] * k2_ref[...]
    interior_ref[...] = load_ref[...] - (
        x[0] * w0_ref[...] + x[1] * w1_ref[...] + x[2] * w2_ref[...]
    )


def call(kernel, outs, *args, scratch=(), in_hbm=0, vmem=8):
    inside = len(args) - in_hbm
    args = args[:inside] + tuple(
        pltpu.with_memory_space_constraint(x, pltpu.HBM) for x in args[inside:]
    )
    return pl.pallas_call(
        kernel,
        out_shape=[jax.ShapeDtypeStruct(shape, dtype) for shape, dtype in outs],
        in_specs=[pl.BlockSpec(memory_space=pltpu.VMEM)] * inside
        + [pl.BlockSpec(memory_space=pltpu.HBM)] * in_hbm,
        out_specs=[pl.BlockSpec(memory_space=pltpu.VMEM)] * len(outs),
        scratch_shapes=[pltpu.VMEM(shape, dtype) for shape, dtype in scratch]
        + [pltpu.SemaphoreType.DMA(())] * in_hbm,
        compiler_params=pltpu.CompilerParams(vmem_limit_bytes=vmem * 1024 * 1024),
    )(*args)


def fused_exchange(meta, shared, out, ranks, kernel, widths):
    pair = [(r, r ^ 1) for r in range(ranks)]

    def both_ways(chips):
        ahead = [(r, (r + 2 * chips + 1) % ranks) for r in range(0, ranks, 2)]
        return ahead + [(t, r) for r, t in ahead]

    skip = [(r, (r + (3 if r % 2 else ranks - 3)) % ranks) for r in range(ranks)]
    far = [(r, (r + ranks // 2) % ranks) for r in range(ranks)]
    second = lax.ppermute(out, AXES, skip)
    other = lax.ppermute(shared, AXES, pair)
    packed = call(
        kernel, [((COMP * NODES + 8, width), F32) for width in widths], meta, shared, other
    )
    got = [
        lax.ppermute(block, AXES, way)
        for block, way in zip(packed, (both_ways(1), both_ways(ranks // 4 - 1), far))
    ]
    second, *got = lax.optimization_barrier((second, *got))
    passed = [lax.ppermute(block, AXES, pair) for block in got[:2]]
    return [shared, other, second, *got, *passed]


def local(self_block, couple, inverse, body_force, face_mortar, face_kind, *, ranks):
    trace, _, elements = self_block.shape
    inner = inverse.shape[0]
    owned = 2 * elements
    cap = max(2, elements // 4)
    width = elements
    rows = COMP * NODES
    count = RUNS * cap
    forward, backward = block_tables()
    mortar = face_mortar.reshape(FACES, width)
    kind = face_kind.reshape(FACES, width)
    self_block = self_block.reshape(trace * trace, width)
    couple = couple.reshape(inner * trace, width)
    inverse = inverse.reshape(inner * inner, width)
    force = body_force.reshape(COMP * inner, width)

    offer, out, onehot, meta, load, *matrices = call(
        functools.partial(start_kernel, ranks, inner, trace, owned, cap),
        [
            ((rows + 8, count + owned), F32),
            ((rows + 8, count), F32),
            ((owned + count, FACES * width), BF16),
            ((8, FACES * width), F32),
            ((COMP * inner, width), F32),
            (inverse.shape, F32),
            (couple.shape, F32),
        ],
        mortar, kind, force, backward, inverse, couple,
        scratch=[
            (mortar.shape, jnp.int32), (kind.shape, jnp.int32), (force.shape, F32), (backward.shape, F32)
        ],
        in_hbm=6, vmem=16,
    )
    blocks = fused_exchange(
        meta, offer, out, ranks,
        functools.partial(first_pack_kernel, owned, cap),
        (count + 2 * owned, count, count + owned),
    )
    fields, spreads, mids, weights, kept, own = [], [], [], [], [], None
    for iteration in range(2):
        fused = iteration > 0
        first = [((rows, owned), F32)]
        if not fused:
            first += [
                (self_block.shape, F32),
                ((8, count), F32),
                ((8, count), F32),
                ((owned + count, 8 * count), BF16),
            ]
        results = call(
            functools.partial(apply_kernel, inner, trace, owned, cap, fused),
            first + [
                ((rows, owned), F32),
                ((2 * rows + 8, count), F32),
                ((COMP * trace, width), F32),
                ((COMP * inner, width), F32),
                ((COMP * inner, width), F32),
            ],
            meta, onehot, forward, backward, *matrices,
            *([*kept, own, *blocks] if fused else [*blocks, self_block]),
            scratch=[((COMP * trace, width), F32)], in_hbm=0 if fused else 1,
        )
        fields.append(results[0])
        kept = kept or results[1 : len(first)]
        own, shared, spread, mid, weight = results[len(first) :]
        spreads.append(spread)
        mids.append(mid)
        weights.append(weight)
        blocks = fused_exchange(
            meta, shared, shared, ranks, functools.partial(pack_kernel, cap), (count,) * 3
        )
    field, weight, moments = call(
        functools.partial(last_kernel, inner, trace, owned, cap),
        [((rows, owned), F32), ((COMP * inner, width), F32), ((ranks, 1, width), F32)],
        meta, onehot, forward, *matrices, kept[0], kept[3], *fields, *spreads, *mids, own, *blocks,
        scratch=[
            ((COMP * trace, width), F32),
            ((COMP * inner, width), F32),
            ((COMP * trace, width), F32),
        ],
    )
    fields.append(field)
    weights.append(weight)
    moments = lax.all_to_all(moments, AXES, split_axis=0, concat_axis=0, tiled=True)
    trace_field, interior = call(
        finish_kernel,
        [((rows, owned), F32), ((COMP * inner, width), F32)],
        moments, *fields, *weights, load,
    )
    return trace_field, interior.reshape(COMP, inner, elements)


def solution(mesh):
    placed = (
        P(None, None, AXES),
        P(None, None, AXES),
        P(None, None, AXES),
        P(None, None, AXES),
        P(AXES),
        P(AXES),
    )
    ranks = int(np.prod([mesh.shape[a] for a in AXES]))
    return jax.shard_map(
        functools.partial(local, ranks=ranks),
        mesh=mesh,
        in_specs=placed,
        out_specs=(P(None, AXES), P(None, None, AXES)),
        check_vma=False,
    )
```

```python
import functools

import jax
import jax.numpy as jnp
import numpy as np
from jax import lax
from jax.experimental import pallas as pl
from jax.experimental.pallas import tpu as pltpu
from jax.sharding import PartitionSpec as P

AXES = ("dom", "blk")
COMP = 3
NODES = 16
FACES = 6
RUNS = 4
F32 = jnp.float32
BF16 = jnp.bfloat16


def interp_tables():
    abscissae = -np.cos(np.pi * np.arange(4) / 3.0)

    def lagrange(points):
        columns = [
            np.prod(
                [
                    (points - abscissae[other_node])
                    / (abscissae[basis_node] - abscissae[other_node])
                    for other_node in range(4)
                    if other_node != basis_node
                ],
                axis=0,
            )
            for basis_node in range(4)
        ]
        return np.stack(columns, axis=1)

    lower_map = lagrange((abscissae - 1.0) / 2.0)
    upper_map = lagrange((abscissae + 1.0) / 2.0)
    return np.stack(
        [
            np.kron(lower_map, lower_map),
            np.kron(lower_map, upper_map),
            np.kron(upper_map, lower_map),
            np.kron(upper_map, upper_map),
        ]
    ).astype(np.float32)


def block_tables():
    tables = interp_tables()
    eye = np.eye(COMP, dtype=np.float32)
    forward = np.concatenate([np.kron(eye, t) for t in tables])
    backward = np.concatenate([np.kron(eye, t.T) for t in tables])
    return forward, backward


def split(x):
    hi = x.astype(BF16)
    return hi, (x - hi.astype(F32)).astype(BF16)


def dot(a, b, rhs_dim=0):
    return lax.dot_general(a, b, (((1,), (rhs_dim,)), ((), ())), preferred_element_type=F32)


def exact_dot(x, onehot, rhs_dim=0):
    hi, lo = split(x)
    both = dot(jnp.concatenate([hi, lo], axis=0), onehot, rhs_dim)
    return both[: x.shape[0]] + both[x.shape[0] :]


def by_kind(x, table_ref, kind):
    rows = x.shape[0]
    t_hi, t_lo = split(table_ref[...])
    x_hi, x_lo = split(x)
    mapped = dot(
        jnp.concatenate([t_hi, t_hi, t_lo], axis=1), jnp.concatenate([x_hi, x_lo, x_hi], axis=0)
    )
    for number in range(4):
        x = jnp.where(kind == number + 1, mapped[number * rows : (number + 1) * rows], x)
    return x


def in_a_row(x):
    return jnp.concatenate([x[r : r + 1, :] for r in range(x.shape[0])], axis=1)


def gather_rows(tiles, sublane):
    tiles = [tiles[r] for r in (0, 4, 2, 6, 1, 5, 3, 7)]
    keep = (sublane & 4) == 0
    tiles = [
        jnp.where(keep, x, y) + pltpu.roll(jnp.where(keep, y, x), 4, 0)
        for x, y in zip(tiles[::2], tiles[1::2])
    ]
    for shift in (2, 1):
        keep = (sublane & shift) == 0
        tiles = [
            jnp.where(keep, x + pltpu.roll(x, 8 - shift, 0), y + pltpu.roll(y, shift, 0))
            for x, y in zip(tiles[::2], tiles[1::2])
        ]
    return tiles[0]


def rows_times(mat_ref, vec_ref, out_ref, outs, terms, group=32):
    width = vec_ref.shape[1]
    sublane = lax.broadcasted_iota(jnp.int32, (8, width), 0)
    vecs = [
        [vec_ref[c * terms + t : c * terms + t + 8, :] for t in range(0, terms, 8)]
        for c in range(COMP)
    ]

    def body(g, carry):
        for first in range(0, group, 8):
            sums = [[] for _ in range(COMP)]
            for r in range(first, first + 8):
                acc = [None] * COMP
                for j in range(terms // 8):
                    start = pl.multiple_of((g * group + r) * terms + 8 * j, 8)
                    tile = mat_ref[pl.ds(start, 8), :]
                    for c in range(COMP):
                        term = tile * vecs[c][j]
                        acc[c] = term if j == 0 else acc[c] + term
                for c in range(COMP):
                    sums[c].append(acc[c])
            for c in range(COMP):
                start = pl.multiple_of(c * outs + g * group + first, 8)
                out_ref[pl.ds(start, 8), :] = gather_rows(sums[c], sublane)
        return carry

    lax.fori_loop(0, outs // group, body, 0)


def columns_times(acc, mat_ref, vec_ref, outs, terms, unroll=16):
    def body(t, acc):
        acc = [list(a) for a in acc]
        vecs = [
            jnp.broadcast_to(vec_ref[pl.ds(c * terms + t, 1), :], (8, vec_ref.shape[1]))
            for c in range(COMP)
        ]
        for j in range(outs // 8):
            tile = mat_ref[pl.ds(pl.multiple_of(t * outs + j * 8, 8), 8), :]
            for c in range(COMP):
                acc[c][j] = acc[c][j] + tile * vecs[c]
        return acc

    return lax.fori_loop(0, terms, body, acc, unroll=unroll)


def tiles_of(ref, outs):
    return [[ref[c * outs + t : c * outs + t + 8, :] for t in range(0, outs, 8)] for c in range(COMP)]


def zeros(outs, width):
    return [[jnp.zeros((8, width), F32) for _ in range(outs // 8)] for _ in range(COMP)]


def face_columns(acc):
    half = NODES // 8
    return jnp.concatenate(
        [
            jnp.concatenate(
                [acc[c][f * half + h] for c in range(COMP) for h in range(half)], axis=0
            )
            for f in range(FACES)
        ],
        axis=1,
    )


def start_kernel(
    ranks, inner, trace, owned, cap,
    mortar_hbm, kind_hbm, force_hbm, back_hbm, inverse_hbm, couple_hbm, self_hbm,
    offer_ref, out_ref, onehot_ref, meta_ref, load_ref, inverse_ref, couple_ref, self_ref,
    mortar_ref, kind_ref, force_ref, back_ref, *sems,
):
    copies = [
        pltpu.make_async_copy(source, target, sem)
        for source, target, sem in zip(
            (mortar_hbm, kind_hbm, force_hbm, back_hbm, inverse_hbm, couple_hbm, self_hbm),
            (mortar_ref, kind_ref, force_ref, back_ref, inverse_ref, couple_ref, self_ref),
            sems,
        )
    ]
    for copy in copies:
        copy.start()
    width = mortar_ref.shape[1]
    slots = FACES * width
    target = lax.broadcasted_iota(jnp.int32, (1, slots), 1)
    target = lax.rem(target, width) * FACES + lax.div(target, width)
    order = jnp.where(
        lax.broadcasted_iota(jnp.int32, (slots, slots), 0) == target, 1.0, 0.0
    ).astype(BF16)
    copies[0].wait()
    copies[1].wait()
    mortar = mortar_ref[...]
    owner = lax.div(mortar, owned)
    index = lax.rem(mortar, owned)
    me = lax.rem(owner[0:1, 0:1] + 2, ranks)
    distance = lax.rem(owner - me + ranks, ranks)
    slot = lax.broadcasted_iota(jnp.int32, mortar.shape, 0) * width + lax.broadcasted_iota(
        jnp.int32, mortar.shape, 1
    )
    column = index
    begin = jnp.zeros((1, 1), jnp.int32)
    for number, away in enumerate((ranks - 2, ranks - 1, 0, 1, ranks // 2)):
        inside = distance == away
        count = jnp.sum(inside.astype(F32), keepdims=True).astype(jnp.int32)
        if away:
            run = number - (number > 2)
            column = jnp.where(inside, owned + run * cap + slot - begin, column)
        begin = begin + count
    facts = jnp.concatenate(
        [in_a_row(column), in_a_row(mortar + 1), in_a_row(kind_ref[...]), jnp.zeros((5, slots), jnp.int32)],
        axis=0,
    ).astype(F32)
    facts = exact_dot(facts, order)
    meta_ref[...] = facts
    meta_ref[3:4, :] = jnp.broadcast_to(lax.rem(me, 2).astype(F32), (1, slots))
    meta_ref[4:5, :] = jnp.broadcast_to((me * owned).astype(F32), (1, slots))
    column = facts[0:1, :].astype(jnp.int32)
    onehot_ref[...] = jnp.where(
        lax.broadcasted_iota(jnp.int32, onehot_ref.shape, 0) == column, 1.0, 0.0
    ).astype(BF16)
    copies[2].wait()
    copies[4].wait()
    rows_times(inverse_ref, force_ref, load_ref, inner, inner)
    copies[3].wait()
    copies[5].wait()
    y = columns_times(zeros(trace, width), couple_ref, load_ref, trace, inner)
    z = by_kind(face_columns(y), back_ref, facts[2:3, :])
    label = jnp.where(
        lax.broadcasted_iota(jnp.int32, (8, slots), 0) == 0, facts[1:2, :], 0.0
    )
    sums = exact_dot(jnp.concatenate([z, label], axis=0), onehot_ref[...], 1)
    count = RUNS * cap
    ids = lax.broadcasted_iota(jnp.int32, (8, owned), 1) + (me * owned + 1)
    ids = jnp.where(lax.broadcasted_iota(jnp.int32, (8, owned), 0) == 0, ids, 0)
    out_ref[...] = sums[:, owned:]
    offer_ref[:, :count] = sums[:, owned:]
    offer_ref[: COMP * NODES, count:] = sums[: COMP * NODES, :owned]
    offer_ref[COMP * NODES :, count:] = ids.astype(F32)
    copies[6].wait()


def onehot_of(condition):
    return jnp.where(condition, 1.0, 0.0).astype(BF16)


def own_ids(meta_ref, owned, count):
    base = meta_ref[4:5, :count].astype(jnp.int32)
    return lax.broadcasted_iota(jnp.int32, (owned, count), 0) + base + 1


def wanted_by(label, meta_ref, owned):
    count = label.shape[1]
    return onehot_of(own_ids(meta_ref, owned, count) == label.astype(jnp.int32))


def share(owned, sums, gid, label, meta_ref, own_ref, shared_ref):
    rows = COMP * NODES
    own = sums[:, :owned]
    own_ref[...] = own
    shared_ref[:rows, :] = sums[:, owned:]
    shared_ref[rows : 2 * rows, :] = exact_dot(own, wanted_by(label, meta_ref, owned))
    row = lax.broadcasted_iota(jnp.int32, (8, gid.shape[1]), 0)
    shared_ref[2 * rows :, :] = jnp.where(row == 0, gid, jnp.where(row == 1, label, 0.0))


def ids_down(ids, count):
    return jnp.broadcast_to(jnp.transpose(jnp.broadcast_to(ids, (8, ids.shape[1])))[:, 0:1], (ids.shape[1], count))


def laid_out(cap, *blocks):
    count = RUNS * cap
    lane = lax.broadcasted_iota(jnp.int32, (1, count), 1)
    result = jnp.zeros((COMP * NODES + 8, count), F32)
    for place, block in enumerate(blocks):
        if block is not None:
            array, run = block
            if run != place:
                array = pltpu.roll(array, ((place - run) % RUNS) * cap, 1)
            inside = (lane >= place * cap) & (lane < (place + 1) * cap)
            result = jnp.where(inside, array, result)
    return result


def first_pack_kernel(owned, cap, meta_ref, mine_ref, other_ref, one_ref, three_ref, four_ref):
    rows = COMP * NODES
    count = RUNS * cap
    laid = functools.partial(laid_out, cap)
    odd = meta_ref[3:4, :count] == 1.0
    odd_own = meta_ref[3:4, :owned] == 1.0
    outs = [mine_ref[:, :count], other_ref[:, :count]]
    fulls = []
    for source, target_ref, swap in ((outs[1], mine_ref, False), (outs[0], other_ref, True)):
        base = meta_ref[4:5, 0:1] + 1.0
        if swap:
            base = base + jnp.where(meta_ref[3:4, 0:1] == 1.0, -float(owned), float(owned))
        ids = lax.broadcasted_iota(jnp.int32, (owned, count), 0).astype(F32) + base
        match = onehot_of(ids == source[rows : rows + 1])
        full = target_ref[:rows, count:] + exact_dot(source[:rows], match, 1)
        fulls.append(jnp.concatenate([full, target_ref[rows:, count:]], axis=0))
    oe, oo = jnp.where(odd, outs[1], outs[0]), jnp.where(odd, outs[0], outs[1])
    one_ref[:, :count] = jnp.where(
        odd, laid((oe, 0), (oe, 1), None, (oo, 0)), laid(None, None, (oo, 2))
    )
    one_ref[:, count : count + owned] = jnp.where(odd_own, fulls[1], fulls[0])
    one_ref[:, count + owned :] = jnp.where(odd_own, fulls[0], fulls[1])
    three_ref[...] = jnp.where(
        odd, laid((oo, 3), None, (oo, 2), (oe, 3)), laid((oe, 0), (oe, 1), (oo, 0), (oe, 3))
    )
    four_ref[:, :count] = laid((oe, 3), (oo, 3))
    four_ref[:, count:] = fulls[0]


def pack_kernel(cap, meta_ref, mine_ref, other_ref, one_ref, three_ref, four_ref):
    rows = COMP * NODES
    count = RUNS * cap
    odd = meta_ref[3:4, :count] == 1.0
    mine, other = mine_ref[...], other_ref[...]
    even_part = jnp.where(odd, other, mine)
    odd_part = jnp.where(odd, mine, other)
    source = jnp.concatenate([even_part[:rows], odd_part[:rows]], axis=1)
    gids = jnp.concatenate([even_part[2 * rows : 2 * rows + 1], odd_part[2 * rows : 2 * rows + 1]], axis=1)
    blank = jnp.zeros((8, count), F32)
    sums = []
    for part in (even_part, odd_part):
        label = part[2 * rows + 1 : 2 * rows + 2]
        match = onehot_of((ids_down(label, 2 * count) == gids) & (gids > 0.0))
        full = part[rows : 2 * rows] + exact_dot(source, match, 1)
        sums.append(jnp.concatenate([full, blank], axis=0))
    outs = [
        jnp.concatenate([part[:rows], part[2 * rows : 2 * rows + 1], blank[1:]], axis=0)
        for part in (even_part, odd_part)
    ]
    laid = functools.partial(laid_out, cap)
    (oe, oo), (ge, go) = outs, sums
    one_ref[...] = jnp.where(
        odd, laid((oe, 0), (oe, 1), (ge, 2), (oo, 0)), laid((ge, 0), (go, 1), (oo, 2), (go, 0))
    )
    three_ref[...] = jnp.where(
        odd, laid((oo, 3), None, (oo, 2), (oe, 3)), laid((oe, 0), (oe, 1), (oo, 0), (oe, 3))
    )
    four_ref[...] = laid((oe, 3), (oo, 3), None, (jnp.where(odd, go, ge), 3))


def matched(owned, meta_ref, gid, sources, remote_sources=()):
    values = jnp.concatenate([v for v, _ in sources], axis=1)
    ids = jnp.concatenate([i for _, i in sources], axis=1)
    number = ids.shape[1]
    own = lax.broadcasted_iota(jnp.int32, (owned, number), 0).astype(F32) + (
        meta_ref[4:5, 0:1] + 1.0
    )
    gid = jnp.where(gid > 0.0, gid, -1.0)
    match = onehot_of(jnp.concatenate([own, ids_down(gid, number)], axis=0) == ids)
    sums = exact_dot(values, match, 1)
    field, remote = sums[:, :owned], sums[:, owned:]
    if remote_sources:
        values = jnp.concatenate([v for v, _ in remote_sources], axis=1)
        ids = jnp.concatenate([i for _, i in remote_sources], axis=1)
        remote = remote + exact_dot(values, onehot_of(ids_down(gid, ids.shape[1]) == ids), 1)
    return field, remote


def first_values(owned, cap, meta_ref, offers, blocks):
    rows = COMP * NODES
    count = RUNS * cap
    lane = lax.broadcasted_iota(jnp.int32, (1, count), 1)
    odd = meta_ref[3:4, :count] == 1.0
    mine_ref, other_ref, _ = offers
    one_ref, _, far_ref, passed_ref, _ = blocks
    sources = [(r[:rows, :count], r[rows : rows + 1, :count]) for r in (*offers, *blocks)]
    owners = [
        (r[:rows, count:], r[rows : rows + 1, count:])
        for r in (other_ref, one_ref, far_ref, passed_ref)
    ]
    gid = mine_ref[rows : rows + 1, :count]
    field, remote = matched(owned, meta_ref, gid, sources, owners)
    label_rows = slice(rows, rows + 8)
    other = other_ref[label_rows, :count]
    one = one_ref[label_rows, :count]
    far = far_ref[label_rows, :count]
    passed = passed_ref[label_rows, :count]
    even_form = jnp.where(
        lane < cap,
        one,
        jnp.where(
            lane < 2 * cap, other, jnp.where(lane < 3 * cap, passed, pltpu.roll(far, 3 * cap, 1))
        ),
    )
    odd_form = jnp.where(
        lane < cap,
        pltpu.roll(passed, cap, 1),
        jnp.where(
            lane < 2 * cap, passed, jnp.where(lane < 3 * cap, other, pltpu.roll(far, 2 * cap, 1))
        ),
    )
    label = jnp.where(odd, odd_form, even_form)
    return mine_ref[:rows, count:] + field, remote, gid, label


def fused_values(owned, cap, meta_ref, own_ref, offers, blocks):
    rows = COMP * NODES
    count = RUNS * cap
    lane = lax.broadcasted_iota(jnp.int32, (1, count), 1)
    odd = meta_ref[3:4, :count] == 1.0
    sources = [(r[:rows], r[2 * rows : 2 * rows + 1]) for r in offers]
    sources += [(r[:rows], r[rows : rows + 1]) for r in blocks]
    field, remote = matched(owned, meta_ref, offers[0][2 * rows : 2 * rows + 1], sources)
    near, _, far, across, _ = (r[:rows] for r in blocks)
    partner = offers[1][rows : 2 * rows]
    even_form = jnp.where(lane < 2 * cap, across, jnp.where(lane < 3 * cap, partner, far))
    odd_form = jnp.where(
        lane < cap,
        pltpu.roll(near, cap, 1),
        jnp.where(lane < 2 * cap, partner, jnp.where(lane < 3 * cap, across, far)),
    )
    return own_ref[...] + field, jnp.where(odd, odd_form, even_form) + remote


def element_values(field, received, meta_ref, onehot_ref, forth_ref, spread_ref):
    source = jnp.concatenate([field, received], axis=1)
    kind = meta_ref[2:3, :]
    faces = by_kind(exact_dot(source, onehot_ref[...]), forth_ref, kind)
    width = spread_ref.shape[1]
    for c in range(COMP):
        for f in range(FACES):
            spread_ref[(c * FACES + f) * NODES : (c * FACES + f + 1) * NODES, :] = faces[
                c * NODES : (c + 1) * NODES, f * width : (f + 1) * width
            ]
    return kind


def apply_kernel(
    inner, trace, owned, cap, fused,
    meta_ref, onehot_ref, forth_ref, back_ref, inverse_ref, couple_ref, self_ref,
    *refs,
):
    if fused:
        gid_ref, label_ref, before_ref, *received = refs[:11]
        field_ref, *refs = refs[11:]
        gid, label = gid_ref[0:1, :], label_ref[0:1, :]
        field, received = fused_values(
            owned, cap, meta_ref, before_ref, received[:3], received[3:]
        )
    else:
        field_ref, gid_ref, label_ref, *after = refs[8:]
        field, received, gid, label = first_values(owned, cap, meta_ref, refs[:3], refs[3:8])
        refs = after
        gid_ref[...] = jnp.broadcast_to(gid, gid_ref.shape)
        label_ref[...] = label
        label = label[0:1, :]
    field_ref[...] = field
    own_ref, shared_ref, spread_ref, mid_ref, weight_ref, image_ref = refs
    width = spread_ref.shape[1]
    kind = element_values(field, received, meta_ref, onehot_ref, forth_ref, spread_ref)
    rows_times(couple_ref, spread_ref, mid_ref, inner, trace)
    rows_times(inverse_ref, mid_ref, weight_ref, inner, inner)
    rows_times(self_ref, spread_ref, image_ref, trace, trace)
    y = columns_times(tiles_of(image_ref, trace), couple_ref, weight_ref, trace, inner)
    z = by_kind(face_columns(y), back_ref, kind)
    sums = exact_dot(z, onehot_ref[...], 1)
    share(owned, sums, gid, label, meta_ref, own_ref, shared_ref)


def total(x):
    return jnp.sum(jnp.sum(x, axis=0, keepdims=True), axis=1, keepdims=True)


def last_kernel(
    inner, trace, owned, cap,
    meta_ref, onehot_ref, forth_ref, inverse_ref, couple_ref, self_ref,
    k0_ref, k1_ref, s0_ref, s1_ref, u0_ref, u1_ref, before_ref, *refs,
):
    received, refs = refs[:8], refs[8:]
    k2_ref, weight_ref, moment_ref, spread_ref, mid_ref, image_ref = refs
    width = spread_ref.shape[1]
    field, received = fused_values(
        owned, cap, meta_ref, before_ref, received[:3], received[3:]
    )
    k2_ref[...] = field
    element_values(field, received, meta_ref, onehot_ref, forth_ref, spread_ref)
    rows_times(couple_ref, spread_ref, mid_ref, inner, trace)
    rows_times(inverse_ref, mid_ref, weight_ref, inner, inner)
    rows_times(self_ref, spread_ref, image_ref, trace, trace)
    image, weight = image_ref[...], weight_ref[...]
    ks = (k0_ref[...], k1_ref[...], field)
    values = [total(ks[i] * ks[j]) for i in range(3) for j in range(i, 3)]
    for s_ref, u_ref in ((s0_ref, u0_ref), (s1_ref, u1_ref), (spread_ref, mid_ref)):
        values.append(total(s_ref[...] * image) + total(u_ref[...] * weight))
    lane = lax.broadcasted_iota(jnp.int32, (1, width), 1)
    row = jnp.zeros((1, width), F32)
    for number, value in enumerate(values):
        row = jnp.where(lane == number, value, row)
    moment_ref[...] = jnp.broadcast_to(row[None], moment_ref.shape)


def finish_kernel(
    moment_ref, k0_ref, k1_ref, k2_ref, w0_ref, w1_ref, w2_ref, load_ref, field_ref, interior_ref
):
    sums = jnp.sum(moment_ref[...], axis=0)
    m = [sums[:, n : n + 1] for n in range(9)]
    gram = [[m[0], m[1], m[2]], [m[1], m[3], m[4]], [m[2], m[4], m[5]]]
    energy = [[gram[i][1], gram[i][2], m[6 + i]] for i in range(3)]

    def form(x, matrix):
        return sum(x[i] * sum(matrix[i][j] * x[j] for j in range(3)) for i in range(3))

    zero, one = jnp.zeros((1, 1), F32), jnp.ones((1, 1), F32)
    x = [zero, zero, zero]
    r = [one, zero, zero]
    d = [one, zero, zero]
    current = gram[0][0]
    for iteration in range(3):
        step = current / form(d, energy)
        x = [x[i] + step * d[i] for i in range(3)]
        if iteration < 2:
            r = [r[0], r[1] - step * d[0], r[2] - step * d[1]]
            following = form(r, gram)
            d = [r[i] + following / current * d[i] for i in range(3)]
            current = following
    field_ref[...] = x[0] * k0_ref[...] + x[1] * k1_ref[...] + x[2] * k2_ref[...]
    interior_ref[...] = load_ref[...] - (
        x[0] * w0_ref[...] + x[1] * w1_ref[...] + x[2] * w2_ref[...]
    )


def call(kernel, outs, *args, scratch=(), in_hbm=0, vmem=8):
    inside = len(args) - in_hbm
    args = args[:inside] + tuple(
        pltpu.with_memory_space_constraint(x, pltpu.HBM) for x in args[inside:]
    )
    return pl.pallas_call(
        kernel,
        out_shape=[jax.ShapeDtypeStruct(shape, dtype) for shape, dtype in outs],
        in_specs=[pl.BlockSpec(memory_space=pltpu.VMEM)] * inside
        + [pl.BlockSpec(memory_space=pltpu.HBM)] * in_hbm,
        out_specs=[pl.BlockSpec(memory_space=pltpu.VMEM)] * len(outs),
        scratch_shapes=[pltpu.VMEM(shape, dtype) for shape, dtype in scratch]
        + [pltpu.SemaphoreType.DMA(())] * in_hbm,
        compiler_params=pltpu.CompilerParams(vmem_limit_bytes=vmem * 1024 * 1024),
    )(*args)


def fused_exchange(meta, shared, out, ranks, kernel, widths):
    pair = [(r, r ^ 1) for r in range(ranks)]

    def both_ways(chips):
        ahead = [(r, (r + 2 * chips + 1) % ranks) for r in range(0, ranks, 2)]
        return ahead + [(t, r) for r, t in ahead]

    skip = [(r, (r + (3 if r % 2 else ranks - 3)) % ranks) for r in range(ranks)]
    far = [(r, (r + ranks // 2) % ranks) for r in range(ranks)]
    second = lax.ppermute(out, AXES, skip)
    other = lax.ppermute(shared, AXES, pair)
    packed = call(
        kernel, [((COMP * NODES + 8, width), F32) for width in widths], meta, shared, other
    )
    got = [
        lax.ppermute(block, AXES, way)
        for block, way in zip(packed, (both_ways(1), both_ways(ranks // 4 - 1), far))
    ]
    if out is not shared:
        second, *got = lax.optimization_barrier((second, *got))
    passed = [lax.ppermute(block, AXES, pair) for block in got[:2]]
    return [shared, other, second, *got, *passed]


def local(self_block, couple, inverse, body_force, face_mortar, face_kind, *, ranks):
    trace, _, elements = self_block.shape
    inner = inverse.shape[0]
    owned = 2 * elements
    cap = max(2, elements // 4)
    width = elements
    rows = COMP * NODES
    count = RUNS * cap
    forward, backward = block_tables()
    mortar = face_mortar.reshape(FACES, width)
    kind = face_kind.reshape(FACES, width)
    self_block = self_block.reshape(trace * trace, width)
    couple = couple.reshape(inner * trace, width)
    inverse = inverse.reshape(inner * inner, width)
    force = body_force.reshape(COMP * inner, width)

    offer, out, onehot, meta, load, *matrices = call(
        functools.partial(start_kernel, ranks, inner, trace, owned, cap),
        [
            ((rows + 8, count + owned), F32),
            ((rows + 8, count), F32),
            ((owned + count, FACES * width), BF16),
            ((8, FACES * width), F32),
            ((COMP * inner, width), F32),
            (inverse.shape, F32),
            (couple.shape, F32),
            (self_block.shape, F32),
        ],
        mortar, kind, force, backward, inverse, couple, self_block,
        scratch=[
            (mortar.shape, jnp.int32), (kind.shape, jnp.int32), (force.shape, F32), (backward.shape, F32)
        ],
        in_hbm=7, vmem=16,
    )
    blocks = fused_exchange(
        meta, offer, out, ranks,
        functools.partial(first_pack_kernel, owned, cap),
        (count + 2 * owned, count, count + owned),
    )
    fields, spreads, mids, weights, ids, own = [], [], [], [], [], None
    for iteration in range(2):
        fused = iteration > 0
        first = [((rows, owned), F32)] + ([] if fused else [((8, count), F32)] * 2)
        results = call(
            functools.partial(apply_kernel, inner, trace, owned, cap, fused),
            first + [
                ((rows, owned), F32),
                ((2 * rows + 8, count), F32),
                ((COMP * trace, width), F32),
                ((COMP * inner, width), F32),
                ((COMP * inner, width), F32),
            ],
            meta, onehot, forward, backward, *matrices, *([*ids, own] if fused else []), *blocks,
            scratch=[((COMP * trace, width), F32)],
        )
        fields.append(results[0])
        ids = ids or results[1 : len(first)]
        own, shared, spread, mid, weight = results[len(first) :]
        spreads.append(spread)
        mids.append(mid)
        weights.append(weight)
        blocks = fused_exchange(
            meta, shared, shared, ranks, functools.partial(pack_kernel, cap), (count,) * 3
        )
    field, weight, moments = call(
        functools.partial(last_kernel, inner, trace, owned, cap),
        [((rows, owned), F32), ((COMP * inner, width), F32), ((ranks, 1, width), F32)],
        meta, onehot, forward, *matrices, *fields, *spreads, *mids, own, *blocks,
        scratch=[
            ((COMP * trace, width), F32),
            ((COMP * inner, width), F32),
            ((COMP * trace, width), F32),
        ],
    )
    fields.append(field)
    weights.append(weight)
    moments = lax.all_to_all(moments, AXES, split_axis=0, concat_axis=0, tiled=True)
    trace_field, interior = call(
        finish_kernel,
        [((rows, owned), F32), ((COMP * inner, width), F32)],
        moments, *fields, *weights, load,
    )
    return trace_field, interior.reshape(COMP, inner, elements)


def solution(mesh):
    placed = (
        P(None, None, AXES),
        P(None, None, AXES),
        P(None, None, AXES),
        P(None, None, AXES),
        P(AXES),
        P(AXES),
    )
    ranks = int(np.prod([mesh.shape[a] for a in AXES]))
    return jax.shard_map(
        functools.partial(local, ranks=ranks),
        mesh=mesh,
        in_specs=placed,
        out_specs=(P(None, AXES), P(None, None, AXES)),
        check_vma=False,
    )
```

```python
import functools

import jax
import jax.numpy as jnp
import numpy as np
from jax import lax
from jax.experimental import pallas as pl
from jax.experimental.pallas import tpu as pltpu
from jax.sharding import PartitionSpec as P

AXES = ("dom", "blk")
COMP = 3
NODES = 16
FACES = 6
RUNS = 4
F32 = jnp.float32
BF16 = jnp.bfloat16


def interp_tables():
    abscissae = -np.cos(np.pi * np.arange(4) / 3.0)

    def lagrange(points):
        columns = [
            np.prod(
                [
                    (points - abscissae[other_node])
                    / (abscissae[basis_node] - abscissae[other_node])
                    for other_node in range(4)
                    if other_node != basis_node
                ],
                axis=0,
            )
            for basis_node in range(4)
        ]
        return np.stack(columns, axis=1)

    lower_map = lagrange((abscissae - 1.0) / 2.0)
    upper_map = lagrange((abscissae + 1.0) / 2.0)
    return np.stack(
        [
            np.kron(lower_map, lower_map),
            np.kron(lower_map, upper_map),
            np.kron(upper_map, lower_map),
            np.kron(upper_map, upper_map),
        ]
    ).astype(np.float32)


def block_tables():
    tables = interp_tables()
    eye = np.eye(COMP, dtype=np.float32)
    forward = np.concatenate([np.kron(eye, t) for t in tables])
    backward = np.concatenate([np.kron(eye, t.T) for t in tables])
    return forward, backward


def split(x):
    hi = x.astype(BF16)
    return hi, (x - hi.astype(F32)).astype(BF16)


def dot(a, b, rhs_dim=0):
    return lax.dot_general(a, b, (((1,), (rhs_dim,)), ((), ())), preferred_element_type=F32)


def exact_dot(x, onehot, rhs_dim=0):
    hi, lo = split(x)
    both = dot(jnp.concatenate([hi, lo], axis=0), onehot, rhs_dim)
    return both[: x.shape[0]] + both[x.shape[0] :]


def by_kind(x, table_ref, kind):
    rows = x.shape[0]
    t_hi, t_lo = split(table_ref[...])
    x_hi, x_lo = split(x)
    mapped = dot(
        jnp.concatenate([t_hi, t_hi, t_lo], axis=1), jnp.concatenate([x_hi, x_lo, x_hi], axis=0)
    )
    for number in range(4):
        x = jnp.where(kind == number + 1, mapped[number * rows : (number + 1) * rows], x)
    return x


def in_a_row(x):
    return jnp.concatenate([x[r : r + 1, :] for r in range(x.shape[0])], axis=1)


def gather_rows(tiles, sublane):
    tiles = [tiles[r] for r in (0, 4, 2, 6, 1, 5, 3, 7)]
    keep = (sublane & 4) == 0
    tiles = [
        jnp.where(keep, x, y) + pltpu.roll(jnp.where(keep, y, x), 4, 0)
        for x, y in zip(tiles[::2], tiles[1::2])
    ]
    for shift in (2, 1):
        keep = (sublane & shift) == 0
        tiles = [
            jnp.where(keep, x + pltpu.roll(x, 8 - shift, 0), y + pltpu.roll(y, shift, 0))
            for x, y in zip(tiles[::2], tiles[1::2])
        ]
    return tiles[0]


def rows_times(mat_ref, vec_ref, out_ref, outs, terms):
    width = vec_ref.shape[1]
    group = outs // 2
    sublane = lax.broadcasted_iota(jnp.int32, (8, width), 0)
    vecs = [
        [vec_ref[c * terms + t : c * terms + t + 8, :] for t in range(0, terms, 8)]
        for c in range(COMP)
    ]

    def body(g, carry):
        for first in range(0, group, 8):
            sums = [[] for _ in range(COMP)]
            for r in range(first, first + 8):
                acc = [None] * COMP
                for j in range(terms // 8):
                    start = pl.multiple_of((g * group + r) * terms + 8 * j, 8)
                    tile = mat_ref[pl.ds(start, 8), :]
                    for c in range(COMP):
                        term = tile * vecs[c][j]
                        acc[c] = term if j == 0 else acc[c] + term
                for c in range(COMP):
                    sums[c].append(acc[c])
            for c in range(COMP):
                start = pl.multiple_of(c * outs + g * group + first, 8)
                out_ref[pl.ds(start, 8), :] = gather_rows(sums[c], sublane)
        return carry

    lax.fori_loop(0, outs // group, body, 0)


def columns_times(acc, mat_ref, vec_ref, outs, terms, unroll=32):
    def body(t, acc):
        acc = [list(a) for a in acc]
        vecs = [
            jnp.broadcast_to(vec_ref[pl.ds(c * terms + t, 1), :], (8, vec_ref.shape[1]))
            for c in range(COMP)
        ]
        for j in range(outs // 8):
            tile = mat_ref[pl.ds(pl.multiple_of(t * outs + j * 8, 8), 8), :]
            for c in range(COMP):
                acc[c][j] = acc[c][j] + tile * vecs[c]
        return acc

    return lax.fori_loop(0, terms, body, acc, unroll=unroll)


def tiles_of(ref, outs):
    return [[ref[c * outs + t : c * outs + t + 8, :] for t in range(0, outs, 8)] for c in range(COMP)]


def zeros(outs, width):
    return [[jnp.zeros((8, width), F32) for _ in range(outs // 8)] for _ in range(COMP)]


def face_columns(acc):
    half = NODES // 8
    return jnp.concatenate(
        [
            jnp.concatenate(
                [acc[c][f * half + h] for c in range(COMP) for h in range(half)], axis=0
            )
            for f in range(FACES)
        ],
        axis=1,
    )


def start_kernel(
    ranks, inner, trace, owned, cap,
    mortar_hbm, kind_hbm, force_hbm, back_hbm, inverse_hbm, couple_hbm, self_hbm,
    offer_ref, out_ref, onehot_ref, meta_ref, load_ref, inverse_ref, couple_ref, self_ref,
    mortar_ref, kind_ref, force_ref, back_ref, *sems,
):
    copies = [
        pltpu.make_async_copy(source, target, sem)
        for source, target, sem in zip(
            (mortar_hbm, kind_hbm, force_hbm, back_hbm, inverse_hbm, couple_hbm, self_hbm),
            (mortar_ref, kind_ref, force_ref, back_ref, inverse_ref, couple_ref, self_ref),
            sems,
        )
    ]
    for copy in copies:
        copy.start()
    width = mortar_ref.shape[1]
    slots = FACES * width
    target = lax.broadcasted_iota(jnp.int32, (1, slots), 1)
    target = lax.rem(target, width) * FACES + lax.div(target, width)
    order = jnp.where(
        lax.broadcasted_iota(jnp.int32, (slots, slots), 0) == target, 1.0, 0.0
    ).astype(BF16)
    copies[0].wait()
    copies[1].wait()
    mortar = mortar_ref[...]
    owner = lax.div(mortar, owned)
    index = lax.rem(mortar, owned)
    me = lax.rem(owner[0:1, 0:1] + 2, ranks)
    distance = lax.rem(owner - me + ranks, ranks)
    slot = lax.broadcasted_iota(jnp.int32, mortar.shape, 0) * width + lax.broadcasted_iota(
        jnp.int32, mortar.shape, 1
    )
    column = index
    begin = jnp.zeros((1, 1), jnp.int32)
    for number, away in enumerate((ranks - 2, ranks - 1, 0, 1, ranks // 2)):
        inside = distance == away
        count = jnp.sum(inside.astype(F32), keepdims=True).astype(jnp.int32)
        if away:
            run = number - (number > 2)
            column = jnp.where(inside, owned + run * cap + slot - begin, column)
        begin = begin + count
    facts = jnp.concatenate(
        [in_a_row(column), in_a_row(mortar + 1), in_a_row(kind_ref[...]), jnp.zeros((5, slots), jnp.int32)],
        axis=0,
    ).astype(F32)
    facts = exact_dot(facts, order)
    meta_ref[...] = facts
    meta_ref[3:4, :] = jnp.broadcast_to(lax.rem(me, 2).astype(F32), (1, slots))
    meta_ref[4:5, :] = jnp.broadcast_to((me * owned).astype(F32), (1, slots))
    column = facts[0:1, :].astype(jnp.int32)
    onehot_ref[...] = jnp.where(
        lax.broadcasted_iota(jnp.int32, onehot_ref.shape, 0) == column, 1.0, 0.0
    ).astype(BF16)
    copies[2].wait()
    copies[4].wait()
    rows_times(inverse_ref, force_ref, load_ref, inner, inner)
    copies[3].wait()
    copies[5].wait()
    y = columns_times(zeros(trace, width), couple_ref, load_ref, trace, inner)
    z = by_kind(face_columns(y), back_ref, facts[2:3, :])
    label = jnp.where(
        lax.broadcasted_iota(jnp.int32, (8, slots), 0) == 0, facts[1:2, :], 0.0
    )
    sums = exact_dot(jnp.concatenate([z, label], axis=0), onehot_ref[...], 1)
    count = RUNS * cap
    ids = lax.broadcasted_iota(jnp.int32, (8, owned), 1) + (me * owned + 1)
    ids = jnp.where(lax.broadcasted_iota(jnp.int32, (8, owned), 0) == 0, ids, 0)
    out_ref[...] = sums[:, owned:]
    offer_ref[:, :count] = sums[:, owned:]
    offer_ref[: COMP * NODES, count:] = sums[: COMP * NODES, :owned]
    offer_ref[COMP * NODES :, count:] = ids.astype(F32)
    copies[6].wait()


def onehot_of(condition):
    return jnp.where(condition, 1.0, 0.0).astype(BF16)


def own_ids(meta_ref, owned, count):
    base = meta_ref[4:5, :count].astype(jnp.int32)
    return lax.broadcasted_iota(jnp.int32, (owned, count), 0) + base + 1


def wanted_by(label, meta_ref, owned):
    count = label.shape[1]
    return onehot_of(own_ids(meta_ref, owned, count) == label.astype(jnp.int32))


def share(owned, sums, gid, label, meta_ref, own_ref, shared_ref):
    rows = COMP * NODES
    own = sums[:, :owned]
    own_ref[...] = own
    shared_ref[:rows, :] = sums[:, owned:]
    shared_ref[rows : 2 * rows, :] = exact_dot(own, wanted_by(label, meta_ref, owned))
    row = lax.broadcasted_iota(jnp.int32, (8, gid.shape[1]), 0)
    shared_ref[2 * rows :, :] = jnp.where(row == 0, gid, jnp.where(row == 1, label, 0.0))


def ids_down(ids, count):
    return jnp.broadcast_to(jnp.transpose(jnp.broadcast_to(ids, (8, ids.shape[1])))[:, 0:1], (ids.shape[1], count))


def laid_out(cap, *blocks):
    count = RUNS * cap
    lane = lax.broadcasted_iota(jnp.int32, (1, count), 1)
    result = jnp.zeros((COMP * NODES + 8, count), F32)
    for place, block in enumerate(blocks):
        if block is not None:
            array, run = block
            if run != place:
                array = pltpu.roll(array, ((place - run) % RUNS) * cap, 1)
            inside = (lane >= place * cap) & (lane < (place + 1) * cap)
            result = jnp.where(inside, array, result)
    return result


def first_pack_kernel(owned, cap, meta_ref, mine_ref, other_ref, one_ref, three_ref, four_ref):
    rows = COMP * NODES
    count = RUNS * cap
    laid = functools.partial(laid_out, cap)
    odd = meta_ref[3:4, :count] == 1.0
    odd_own = meta_ref[3:4, :owned] == 1.0
    outs = [mine_ref[:, :count], other_ref[:, :count]]
    fulls = []
    for source, target_ref, swap in ((outs[1], mine_ref, False), (outs[0], other_ref, True)):
        base = meta_ref[4:5, 0:1] + 1.0
        if swap:
            base = base + jnp.where(meta_ref[3:4, 0:1] == 1.0, -float(owned), float(owned))
        ids = lax.broadcasted_iota(jnp.int32, (owned, count), 0).astype(F32) + base
        match = onehot_of(ids == source[rows : rows + 1])
        full = target_ref[:rows, count:] + exact_dot(source[:rows], match, 1)
        fulls.append(jnp.concatenate([full, target_ref[rows:, count:]], axis=0))
    oe, oo = jnp.where(odd, outs[1], outs[0]), jnp.where(odd, outs[0], outs[1])
    one_ref[:, :count] = jnp.where(
        odd, laid((oe, 0), (oe, 1), None, (oo, 0)), laid(None, None, (oo, 2))
    )
    one_ref[:, count : count + owned] = jnp.where(odd_own, fulls[1], fulls[0])
    one_ref[:, count + owned :] = jnp.where(odd_own, fulls[0], fulls[1])
    three_ref[...] = jnp.where(
        odd, laid((oo, 3), None, (oo, 2), (oe, 3)), laid((oe, 0), (oe, 1), (oo, 0), (oe, 3))
    )
    four_ref[:, :count] = laid((oe, 3), (oo, 3))
    four_ref[:, count:] = fulls[0]


def pack_kernel(cap, meta_ref, mine_ref, other_ref, one_ref, three_ref, four_ref):
    rows = COMP * NODES
    count = RUNS * cap
    odd = meta_ref[3:4, :count] == 1.0
    mine, other = mine_ref[...], other_ref[...]
    even_part = jnp.where(odd, other, mine)
    odd_part = jnp.where(odd, mine, other)
    source = jnp.concatenate([even_part[:rows], odd_part[:rows]], axis=1)
    gids = jnp.concatenate([even_part[2 * rows : 2 * rows + 1], odd_part[2 * rows : 2 * rows + 1]], axis=1)
    blank = jnp.zeros((8, count), F32)
    sums = []
    for part in (even_part, odd_part):
        label = part[2 * rows + 1 : 2 * rows + 2]
        match = onehot_of((ids_down(label, 2 * count) == gids) & (gids > 0.0))
        full = part[rows : 2 * rows] + exact_dot(source, match, 1)
        sums.append(jnp.concatenate([full, blank], axis=0))
    outs = [
        jnp.concatenate([part[:rows], part[2 * rows : 2 * rows + 1], blank[1:]], axis=0)
        for part in (even_part, odd_part)
    ]
    laid = functools.partial(laid_out, cap)
    (oe, oo), (ge, go) = outs, sums
    one_ref[...] = jnp.where(
        odd, laid((oe, 0), (oe, 1), (ge, 2), (oo, 0)), laid((ge, 0), (go, 1), (oo, 2), (go, 0))
    )
    three_ref[...] = jnp.where(
        odd, laid((oo, 3), None, (oo, 2), (oe, 3)), laid((oe, 0), (oe, 1), (oo, 0), (oe, 3))
    )
    four_ref[...] = laid((oe, 3), (oo, 3), None, (jnp.where(odd, go, ge), 3))


def matched(owned, meta_ref, gid, sources, remote_sources=()):
    values = jnp.concatenate([v for v, _ in sources], axis=1)
    ids = jnp.concatenate([i for _, i in sources], axis=1)
    number = ids.shape[1]
    own = lax.broadcasted_iota(jnp.int32, (owned, number), 0).astype(F32) + (
        meta_ref[4:5, 0:1] + 1.0
    )
    gid = jnp.where(gid > 0.0, gid, -1.0)
    match = onehot_of(jnp.concatenate([own, ids_down(gid, number)], axis=0) == ids)
    sums = exact_dot(values, match, 1)
    field, remote = sums[:, :owned], sums[:, owned:]
    if remote_sources:
        values = jnp.concatenate([v for v, _ in remote_sources], axis=1)
        ids = jnp.concatenate([i for _, i in remote_sources], axis=1)
        remote = remote + exact_dot(values, onehot_of(ids_down(gid, ids.shape[1]) == ids), 1)
    return field, remote


def first_values(owned, cap, meta_ref, offers, blocks):
    rows = COMP * NODES
    count = RUNS * cap
    lane = lax.broadcasted_iota(jnp.int32, (1, count), 1)
    odd = meta_ref[3:4, :count] == 1.0
    mine_ref, other_ref, _ = offers
    one_ref, _, far_ref, passed_ref, _ = blocks
    sources = [(r[:rows, :count], r[rows : rows + 1, :count]) for r in (*offers, *blocks)]
    owners = [
        (r[:rows, count:], r[rows : rows + 1, count:])
        for r in (other_ref, one_ref, far_ref, passed_ref)
    ]
    gid = mine_ref[rows : rows + 1, :count]
    field, remote = matched(owned, meta_ref, gid, sources, owners)
    label_rows = slice(rows, rows + 8)
    other = other_ref[label_rows, :count]
    one = one_ref[label_rows, :count]
    far = far_ref[label_rows, :count]
    passed = passed_ref[label_rows, :count]
    even_form = jnp.where(
        lane < cap,
        one,
        jnp.where(
            lane < 2 * cap, other, jnp.where(lane < 3 * cap, passed, pltpu.roll(far, 3 * cap, 1))
        ),
    )
    odd_form = jnp.where(
        lane < cap,
        pltpu.roll(passed, cap, 1),
        jnp.where(
            lane < 2 * cap, passed, jnp.where(lane < 3 * cap, other, pltpu.roll(far, 2 * cap, 1))
        ),
    )
    label = jnp.where(odd, odd_form, even_form)
    return mine_ref[:rows, count:] + field, remote, gid, label


def fused_values(owned, cap, meta_ref, own_ref, offers, blocks):
    rows = COMP * NODES
    count = RUNS * cap
    lane = lax.broadcasted_iota(jnp.int32, (1, count), 1)
    odd = meta_ref[3:4, :count] == 1.0
    sources = [(r[:rows], r[2 * rows : 2 * rows + 1]) for r in offers]
    sources += [(r[:rows], r[rows : rows + 1]) for r in blocks]
    field, remote = matched(owned, meta_ref, offers[0][2 * rows : 2 * rows + 1], sources)
    near, _, far, across, _ = (r[:rows] for r in blocks)
    partner = offers[1][rows : 2 * rows]
    even_form = jnp.where(lane < 2 * cap, across, jnp.where(lane < 3 * cap, partner, far))
    odd_form = jnp.where(
        lane < cap,
        pltpu.roll(near, cap, 1),
        jnp.where(lane < 2 * cap, partner, jnp.where(lane < 3 * cap, across, far)),
    )
    return own_ref[...] + field, jnp.where(odd, odd_form, even_form) + remote


def element_values(field, received, meta_ref, onehot_ref, forth_ref, spread_ref):
    source = jnp.concatenate([field, received], axis=1)
    kind = meta_ref[2:3, :]
    faces = by_kind(exact_dot(source, onehot_ref[...]), forth_ref, kind)
    width = spread_ref.shape[1]
    for c in range(COMP):
        for f in range(FACES):
            spread_ref[(c * FACES + f) * NODES : (c * FACES + f + 1) * NODES, :] = faces[
                c * NODES : (c + 1) * NODES, f * width : (f + 1) * width
            ]
    return kind


def apply_kernel(
    inner, trace, owned, cap, fused,
    meta_ref, onehot_ref, forth_ref, back_ref, inverse_ref, couple_ref, self_ref,
    *refs,
):
    if fused:
        gid_ref, label_ref, before_ref, *received = refs[:11]
        field_ref, *refs = refs[11:]
        gid, label = gid_ref[0:1, :], label_ref[0:1, :]
        field, received = fused_values(
            owned, cap, meta_ref, before_ref, received[:3], received[3:]
        )
    else:
        field_ref, gid_ref, label_ref, *after = refs[8:]
        field, received, gid, label = first_values(owned, cap, meta_ref, refs[:3], refs[3:8])
        refs = after
        gid_ref[...] = jnp.broadcast_to(gid, gid_ref.shape)
        label_ref[...] = label
        label = label[0:1, :]
    field_ref[...] = field
    own_ref, shared_ref, spread_ref, mid_ref, weight_ref, image_ref = refs
    width = spread_ref.shape[1]
    kind = element_values(field, received, meta_ref, onehot_ref, forth_ref, spread_ref)
    rows_times(couple_ref, spread_ref, mid_ref, inner, trace)
    rows_times(inverse_ref, mid_ref, weight_ref, inner, inner)
    rows_times(self_ref, spread_ref, image_ref, trace, trace)
    y = columns_times(tiles_of(image_ref, trace), couple_ref, weight_ref, trace, inner)
    z = by_kind(face_columns(y), back_ref, kind)
    sums = exact_dot(z, onehot_ref[...], 1)
    share(owned, sums, gid, label, meta_ref, own_ref, shared_ref)


def total(x):
    return jnp.sum(jnp.sum(x, axis=0, keepdims=True), axis=1, keepdims=True)


def last_kernel(
    inner, trace, owned, cap,
    meta_ref, onehot_ref, forth_ref, inverse_ref, couple_ref, self_ref,
    k0_ref, k1_ref, s0_ref, s1_ref, u0_ref, u1_ref, before_ref, *refs,
):
    received, refs = refs[:8], refs[8:]
    k2_ref, weight_ref, moment_ref, spread_ref, mid_ref, image_ref = refs
    width = spread_ref.shape[1]
    field, received = fused_values(
        owned, cap, meta_ref, before_ref, received[:3], received[3:]
    )
    k2_ref[...] = field
    element_values(field, received, meta_ref, onehot_ref, forth_ref, spread_ref)
    rows_times(couple_ref, spread_ref, mid_ref, inner, trace)
    rows_times(inverse_ref, mid_ref, weight_ref, inner, inner)
    rows_times(self_ref, spread_ref, image_ref, trace, trace)
    image, weight = image_ref[...], weight_ref[...]
    ks = (k0_ref[...], k1_ref[...], field)
    values = [total(ks[i] * ks[j]) for i in range(3) for j in range(i, 3)]
    for s_ref, u_ref in ((s0_ref, u0_ref), (s1_ref, u1_ref), (spread_ref, mid_ref)):
        values.append(total(s_ref[...] * image) + total(u_ref[...] * weight))
    lane = lax.broadcasted_iota(jnp.int32, (1, width), 1)
    row = jnp.zeros((1, width), F32)
    for number, value in enumerate(values):
        row = jnp.where(lane == number, value, row)
    moment_ref[...] = jnp.broadcast_to(row[None], moment_ref.shape)


def finish_kernel(
    moment_ref, k0_ref, k1_ref, k2_ref, w0_ref, w1_ref, w2_ref, load_ref, field_ref, interior_ref
):
    sums = jnp.sum(moment_ref[...], axis=0)
    m = [sums[:, n : n + 1] for n in range(9)]
    gram = [[m[0], m[1], m[2]], [m[1], m[3], m[4]], [m[2], m[4], m[5]]]
    energy = [[gram[i][1], gram[i][2], m[6 + i]] for i in range(3)]

    def form(x, matrix):
        return sum(x[i] * sum(matrix[i][j] * x[j] for j in range(3)) for i in range(3))

    zero, one = jnp.zeros((1, 1), F32), jnp.ones((1, 1), F32)
    x = [zero, zero, zero]
    r = [one, zero, zero]
    d = [one, zero, zero]
    current = gram[0][0]
    for iteration in range(3):
        step = current / form(d, energy)
        x = [x[i] + step * d[i] for i in range(3)]
        if iteration < 2:
            r = [r[0], r[1] - step * d[0], r[2] - step * d[1]]
            following = form(r, gram)
            d = [r[i] + following / current * d[i] for i in range(3)]
            current = following
    field_ref[...] = x[0] * k0_ref[...] + x[1] * k1_ref[...] + x[2] * k2_ref[...]
    interior_ref[...] = load_ref[...] - (
        x[0] * w0_ref[...] + x[1] * w1_ref[...] + x[2] * w2_ref[...]
    )


def call(kernel, outs, *args, scratch=(), in_hbm=0, vmem=8):
    inside = len(args) - in_hbm
    args = args[:inside] + tuple(
        pltpu.with_memory_space_constraint(x, pltpu.HBM) for x in args[inside:]
    )
    return pl.pallas_call(
        kernel,
        out_shape=[jax.ShapeDtypeStruct(shape, dtype) for shape, dtype in outs],
        in_specs=[pl.BlockSpec(memory_space=pltpu.VMEM)] * inside
        + [pl.BlockSpec(memory_space=pltpu.HBM)] * in_hbm,
        out_specs=[pl.BlockSpec(memory_space=pltpu.VMEM)] * len(outs),
        scratch_shapes=[pltpu.VMEM(shape, dtype) for shape, dtype in scratch]
        + [pltpu.SemaphoreType.DMA(())] * in_hbm,
        compiler_params=pltpu.CompilerParams(vmem_limit_bytes=vmem * 1024 * 1024),
    )(*args)


def fused_exchange(meta, shared, out, ranks, kernel, widths):
    pair = [(r, r ^ 1) for r in range(ranks)]

    def both_ways(chips):
        ahead = [(r, (r + 2 * chips + 1) % ranks) for r in range(0, ranks, 2)]
        return ahead + [(t, r) for r, t in ahead]

    skip = [(r, (r + (3 if r % 2 else ranks - 3)) % ranks) for r in range(ranks)]
    far = [(r, (r + ranks // 2) % ranks) for r in range(ranks)]
    second = lax.ppermute(out, AXES, skip)
    other = lax.ppermute(shared, AXES, pair)
    packed = call(
        kernel, [((COMP * NODES + 8, width), F32) for width in widths], meta, shared, other
    )
    got = [
        lax.ppermute(block, AXES, way)
        for block, way in zip(packed, (both_ways(1), both_ways(ranks // 4 - 1), far))
    ]
    if out is not shared:
        second, *got = lax.optimization_barrier((second, *got))
    passed = [lax.ppermute(block, AXES, pair) for block in got[:2]]
    return [shared, other, second, *got, *passed]


def local(self_block, couple, inverse, body_force, face_mortar, face_kind, *, ranks):
    trace, _, elements = self_block.shape
    inner = inverse.shape[0]
    owned = 2 * elements
    cap = max(2, elements // 4)
    width = elements
    rows = COMP * NODES
    count = RUNS * cap
    forward, backward = block_tables()
    mortar = face_mortar.reshape(FACES, width)
    kind = face_kind.reshape(FACES, width)
    self_block = self_block.reshape(trace * trace, width)
    couple = couple.reshape(inner * trace, width)
    inverse = inverse.reshape(inner * inner, width)
    force = body_force.reshape(COMP * inner, width)

    offer, out, onehot, meta, load, *matrices = call(
        functools.partial(start_kernel, ranks, inner, trace, owned, cap),
        [
            ((rows + 8, count + owned), F32),
            ((rows + 8, count), F32),
            ((owned + count, FACES * width), BF16),
            ((8, FACES * width), F32),
            ((COMP * inner, width), F32),
            (inverse.shape, F32),
            (couple.shape, F32),
            (self_block.shape, F32),
        ],
        mortar, kind, force, backward, inverse, couple, self_block,
        scratch=[
            (mortar.shape, jnp.int32), (kind.shape, jnp.int32), (force.shape, F32), (backward.shape, F32)
        ],
        in_hbm=7, vmem=16,
    )
    blocks = fused_exchange(
        meta, offer, out, ranks,
        functools.partial(first_pack_kernel, owned, cap),
        (count + 2 * owned, count, count + owned),
    )
    fields, spreads, mids, weights, ids, own = [], [], [], [], [], None
    for iteration in range(2):
        fused = iteration > 0
        first = [((rows, owned), F32)] + ([] if fused else [((8, count), F32)] * 2)
        results = call(
            functools.partial(apply_kernel, inner, trace, owned, cap, fused),
            first + [
                ((rows, owned), F32),
                ((2 * rows + 8, count), F32),
                ((COMP * trace, width), F32),
                ((COMP * inner, width), F32),
                ((COMP * inner, width), F32),
            ],
            meta, onehot, forward, backward, *matrices, *([*ids, own] if fused else []), *blocks,
            scratch=[((COMP * trace, width), F32)],
        )
        fields.append(results[0])
        ids = ids or results[1 : len(first)]
        own, shared, spread, mid, weight = results[len(first) :]
        spreads.append(spread)
        mids.append(mid)
        weights.append(weight)
        blocks = fused_exchange(
            meta, shared, shared, ranks, functools.partial(pack_kernel, cap), (count,) * 3
        )
    field, weight, moments = call(
        functools.partial(last_kernel, inner, trace, owned, cap),
        [((rows, owned), F32), ((COMP * inner, width), F32), ((ranks, 1, width), F32)],
        meta, onehot, forward, *matrices, *fields, *spreads, *mids, own, *blocks,
        scratch=[
            ((COMP * trace, width), F32),
            ((COMP * inner, width), F32),
            ((COMP * trace, width), F32),
        ],
    )
    fields.append(field)
    weights.append(weight)
    moments = lax.all_to_all(moments, AXES, split_axis=0, concat_axis=0, tiled=True)
    trace_field, interior = call(
        finish_kernel,
        [((rows, owned), F32), ((COMP * inner, width), F32)],
        moments, *fields, *weights, load,
    )
    return trace_field, interior.reshape(COMP, inner, elements)


def solution(mesh):
    placed = (
        P(None, None, AXES),
        P(None, None, AXES),
        P(None, None, AXES),
        P(None, None, AXES),
        P(AXES),
        P(AXES),
    )
    ranks = int(np.prod([mesh.shape[a] for a in AXES]))
    return jax.shard_map(
        functools.partial(local, ranks=ranks),
        mesh=mesh,
        in_specs=placed,
        out_specs=(P(None, AXES), P(None, None, AXES)),
        check_vma=False,
    )
```

```python
import functools

import jax
import jax.numpy as jnp
import numpy as np
from jax import lax
from jax.experimental import pallas as pl
from jax.experimental.pallas import tpu as pltpu
from jax.sharding import PartitionSpec as P

AXES = ("dom", "blk")
COMP = 3
NODES = 16
FACES = 6
RUNS = 4
F32 = jnp.float32
BF16 = jnp.bfloat16


def interp_tables():
    abscissae = -np.cos(np.pi * np.arange(4) / 3.0)

    def lagrange(points):
        columns = [
            np.prod(
                [
                    (points - abscissae[other_node])
                    / (abscissae[basis_node] - abscissae[other_node])
                    for other_node in range(4)
                    if other_node != basis_node
                ],
                axis=0,
            )
            for basis_node in range(4)
        ]
        return np.stack(columns, axis=1)

    lower_map = lagrange((abscissae - 1.0) / 2.0)
    upper_map = lagrange((abscissae + 1.0) / 2.0)
    return np.stack(
        [
            np.kron(lower_map, lower_map),
            np.kron(lower_map, upper_map),
            np.kron(upper_map, lower_map),
            np.kron(upper_map, upper_map),
        ]
    ).astype(np.float32)


def block_tables():
    tables = interp_tables()
    eye = np.eye(COMP, dtype=np.float32)
    forward = np.concatenate([np.kron(eye, t) for t in tables])
    backward = np.concatenate([np.kron(eye, t.T) for t in tables])
    return forward, backward


def split(x):
    hi = x.astype(BF16)
    return hi, (x - hi.astype(F32)).astype(BF16)


def dot(a, b, rhs_dim=0):
    return lax.dot_general(a, b, (((1,), (rhs_dim,)), ((), ())), preferred_element_type=F32)


def exact_dot(x, onehot, rhs_dim=0):
    hi, lo = split(x)
    both = dot(jnp.concatenate([hi, lo], axis=0), onehot, rhs_dim)
    return both[: x.shape[0]] + both[x.shape[0] :]


def by_kind(x, table_ref, kind):
    rows = x.shape[0]
    t_hi, t_lo = split(table_ref[...])
    x_hi, x_lo = split(x)
    mapped = dot(
        jnp.concatenate([t_hi, t_hi, t_lo], axis=1), jnp.concatenate([x_hi, x_lo, x_hi], axis=0)
    )
    for number in range(4):
        x = jnp.where(kind == number + 1, mapped[number * rows : (number + 1) * rows], x)
    return x


def in_a_row(x):
    return jnp.concatenate([x[r : r + 1, :] for r in range(x.shape[0])], axis=1)


def gather_rows(tiles, sublane):
    tiles = [tiles[r] for r in (0, 4, 2, 6, 1, 5, 3, 7)]
    keep = (sublane & 4) == 0
    tiles = [
        jnp.where(keep, x, y) + pltpu.roll(jnp.where(keep, y, x), 4, 0)
        for x, y in zip(tiles[::2], tiles[1::2])
    ]
    for shift in (2, 1):
        keep = (sublane & shift) == 0
        tiles = [
            jnp.where(keep, x + pltpu.roll(x, 8 - shift, 0), y + pltpu.roll(y, shift, 0))
            for x, y in zip(tiles[::2], tiles[1::2])
        ]
    return tiles[0]


def rows_times(mat_ref, vec_ref, out_ref, outs, terms, group=32):
    width = vec_ref.shape[1]
    sublane = lax.broadcasted_iota(jnp.int32, (8, width), 0)
    vecs = [
        [vec_ref[c * terms + t : c * terms + t + 8, :] for t in range(0, terms, 8)]
        for c in range(COMP)
    ]

    def body(g, carry):
        for first in range(0, group, 8):
            sums = [[] for _ in range(COMP)]
            for r in range(first, first + 8):
                acc = [None] * COMP
                for j in range(terms // 8):
                    start = pl.multiple_of((g * group + r) * terms + 8 * j, 8)
                    tile = mat_ref[pl.ds(start, 8), :]
                    for c in range(COMP):
                        term = tile * vecs[c][j]
                        acc[c] = term if j == 0 else acc[c] + term
                for c in range(COMP):
                    sums[c].append(acc[c])
            for c in range(COMP):
                start = pl.multiple_of(c * outs + g * group + first, 8)
                out_ref[pl.ds(start, 8), :] = gather_rows(sums[c], sublane)
        return carry

    lax.fori_loop(0, outs // group, body, 0)


def columns_times(acc, mat_ref, vec_ref, outs, terms, unroll=16):
    def body(t, acc):
        acc = [list(a) for a in acc]
        vecs = [
            jnp.broadcast_to(vec_ref[pl.ds(c * terms + t, 1), :], (8, vec_ref.shape[1]))
            for c in range(COMP)
        ]
        for j in range(outs // 8):
            tile = mat_ref[pl.ds(pl.multiple_of(t * outs + j * 8, 8), 8), :]
            for c in range(COMP):
                acc[c][j] = acc[c][j] + tile * vecs[c]
        return acc

    return lax.fori_loop(0, terms, body, acc, unroll=unroll)


def tiles_of(ref, outs):
    return [[ref[c * outs + t : c * outs + t + 8, :] for t in range(0, outs, 8)] for c in range(COMP)]


def zeros(outs, width):
    return [[jnp.zeros((8, width), F32) for _ in range(outs // 8)] for _ in range(COMP)]


def face_columns(acc):
    half = NODES // 8
    return jnp.concatenate(
        [
            jnp.concatenate(
                [acc[c][f * half + h] for c in range(COMP) for h in range(half)], axis=0
            )
            for f in range(FACES)
        ],
        axis=1,
    )


def start_kernel(
    ranks, inner, trace, owned, cap,
    mortar_hbm, kind_hbm, force_hbm, back_hbm, inverse_hbm, couple_hbm, self_hbm,
    offer_ref, out_ref, onehot_ref, meta_ref, load_ref, inverse_ref, couple_ref, self_ref,
    mortar_ref, kind_ref, force_ref, back_ref, *sems,
):
    copies = [
        pltpu.make_async_copy(source, target, sem)
        for source, target, sem in zip(
            (mortar_hbm, kind_hbm, force_hbm, back_hbm, inverse_hbm, couple_hbm, self_hbm),
            (mortar_ref, kind_ref, force_ref, back_ref, inverse_ref, couple_ref, self_ref),
            sems,
        )
    ]
    for copy in copies:
        copy.start()
    width = mortar_ref.shape[1]
    slots = FACES * width
    target = lax.broadcasted_iota(jnp.int32, (1, slots), 1)
    target = lax.rem(target, width) * FACES + lax.div(target, width)
    order = jnp.where(
        lax.broadcasted_iota(jnp.int32, (slots, slots), 0) == target, 1.0, 0.0
    ).astype(BF16)
    copies[0].wait()
    copies[1].wait()
    mortar = mortar_ref[...]
    owner = lax.div(mortar, owned)
    index = lax.rem(mortar, owned)
    me = lax.rem(owner[0:1, 0:1] + 2, ranks)
    distance = lax.rem(owner - me + ranks, ranks)
    slot = lax.broadcasted_iota(jnp.int32, mortar.shape, 0) * width + lax.broadcasted_iota(
        jnp.int32, mortar.shape, 1
    )
    column = index
    begin = jnp.zeros((1, 1), jnp.int32)
    for number, away in enumerate((ranks - 2, ranks - 1, 0, 1, ranks // 2)):
        inside = distance == away
        count = jnp.sum(inside.astype(F32), keepdims=True).astype(jnp.int32)
        if away:
            run = number - (number > 2)
            column = jnp.where(inside, owned + run * cap + slot - begin, column)
        begin = begin + count
    facts = jnp.concatenate(
        [in_a_row(column), in_a_row(mortar + 1), in_a_row(kind_ref[...]), jnp.zeros((5, slots), jnp.int32)],
        axis=0,
    ).astype(F32)
    facts = exact_dot(facts, order)
    meta_ref[...] = facts
    meta_ref[3:4, :] = jnp.broadcast_to(lax.rem(me, 2).astype(F32), (1, slots))
    meta_ref[4:5, :] = jnp.broadcast_to((me * owned).astype(F32), (1, slots))
    column = facts[0:1, :].astype(jnp.int32)
    onehot_ref[...] = jnp.where(
        lax.broadcasted_iota(jnp.int32, onehot_ref.shape, 0) == column, 1.0, 0.0
    ).astype(BF16)
    copies[2].wait()
    copies[4].wait()
    rows_times(inverse_ref, force_ref, load_ref, inner, inner)
    copies[3].wait()
    copies[5].wait()
    y = columns_times(zeros(trace, width), couple_ref, load_ref, trace, inner)
    z = by_kind(face_columns(y), back_ref, facts[2:3, :])
    label = jnp.where(
        lax.broadcasted_iota(jnp.int32, (8, slots), 0) == 0, facts[1:2, :], 0.0
    )
    sums = exact_dot(jnp.concatenate([z, label], axis=0), onehot_ref[...], 1)
    count = RUNS * cap
    ids = lax.broadcasted_iota(jnp.int32, (8, owned), 1) + (me * owned + 1)
    ids = jnp.where(lax.broadcasted_iota(jnp.int32, (8, owned), 0) == 0, ids, 0)
    out_ref[...] = sums[:, owned:]
    offer_ref[:, :count] = sums[:, owned:]
    offer_ref[: COMP * NODES, count:] = sums[: COMP * NODES, :owned]
    offer_ref[COMP * NODES :, count:] = ids.astype(F32)
    copies[6].wait()


def onehot_of(condition):
    return jnp.where(condition, 1.0, 0.0).astype(BF16)


def own_ids(meta_ref, owned, count):
    base = meta_ref[4:5, :count].astype(jnp.int32)
    return lax.broadcasted_iota(jnp.int32, (owned, count), 0) + base + 1


def wanted_by(label, meta_ref, owned):
    count = label.shape[1]
    return onehot_of(own_ids(meta_ref, owned, count) == label.astype(jnp.int32))


def share(owned, sums, gid, label, meta_ref, own_ref, shared_ref):
    rows = COMP * NODES
    own = sums[:, :owned]
    own_ref[...] = own
    shared_ref[:rows, :] = sums[:, owned:]
    shared_ref[rows : 2 * rows, :] = exact_dot(own, wanted_by(label, meta_ref, owned))
    row = lax.broadcasted_iota(jnp.int32, (8, gid.shape[1]), 0)
    shared_ref[2 * rows :, :] = jnp.where(row == 0, gid, jnp.where(row == 1, label, 0.0))


def ids_down(ids, count):
    return jnp.broadcast_to(jnp.transpose(jnp.broadcast_to(ids, (8, ids.shape[1])))[:, 0:1], (ids.shape[1], count))


def laid_out(cap, *blocks):
    count = RUNS * cap
    lane = lax.broadcasted_iota(jnp.int32, (1, count), 1)
    result = jnp.zeros((COMP * NODES + 8, count), F32)
    for place, block in enumerate(blocks):
        if block is not None:
            array, run = block
            if run != place:
                array = pltpu.roll(array, ((place - run) % RUNS) * cap, 1)
            inside = (lane >= place * cap) & (lane < (place + 1) * cap)
            result = jnp.where(inside, array, result)
    return result


def first_pack_kernel(owned, cap, meta_ref, mine_ref, other_ref, one_ref, three_ref, four_ref):
    rows = COMP * NODES
    count = RUNS * cap
    laid = functools.partial(laid_out, cap)
    odd = meta_ref[3:4, :count] == 1.0
    odd_own = meta_ref[3:4, :owned] == 1.0
    outs = [mine_ref[:, :count], other_ref[:, :count]]
    fulls = []
    for source, target_ref, swap in ((outs[1], mine_ref, False), (outs[0], other_ref, True)):
        base = meta_ref[4:5, 0:1] + 1.0
        if swap:
            base = base + jnp.where(meta_ref[3:4, 0:1] == 1.0, -float(owned), float(owned))
        ids = lax.broadcasted_iota(jnp.int32, (owned, count), 0).astype(F32) + base
        match = onehot_of(ids == source[rows : rows + 1])
        full = target_ref[:rows, count:] + exact_dot(source[:rows], match, 1)
        fulls.append(jnp.concatenate([full, target_ref[rows:, count:]], axis=0))
    oe, oo = jnp.where(odd, outs[1], outs[0]), jnp.where(odd, outs[0], outs[1])
    one_ref[:, :count] = jnp.where(
        odd, laid((oe, 0), (oe, 1), None, (oo, 0)), laid(None, None, (oo, 2))
    )
    one_ref[:, count : count + owned] = jnp.where(odd_own, fulls[1], fulls[0])
    one_ref[:, count + owned :] = jnp.where(odd_own, fulls[0], fulls[1])
    three_ref[...] = jnp.where(
        odd, laid((oo, 3), None, (oo, 2), (oe, 3)), laid((oe, 0), (oe, 1), (oo, 0), (oe, 3))
    )
    four_ref[:, :count] = laid((oe, 3), (oo, 3))
    four_ref[:, count:] = fulls[0]


def pack_kernel(cap, meta_ref, mine_ref, other_ref, one_ref, three_ref, four_ref):
    rows = COMP * NODES
    count = RUNS * cap
    odd = meta_ref[3:4, :count] == 1.0
    mine, other = mine_ref[...], other_ref[...]
    even_part = jnp.where(odd, other, mine)
    odd_part = jnp.where(odd, mine, other)
    source = jnp.concatenate([even_part[:rows], odd_part[:rows]], axis=1)
    gids = jnp.concatenate([even_part[2 * rows : 2 * rows + 1], odd_part[2 * rows : 2 * rows + 1]], axis=1)
    blank = jnp.zeros((8, count), F32)
    sums = []
    for part in (even_part, odd_part):
        label = part[2 * rows + 1 : 2 * rows + 2]
        match = onehot_of((ids_down(label, 2 * count) == gids) & (gids > 0.0))
        full = part[rows : 2 * rows] + exact_dot(source, match, 1)
        sums.append(jnp.concatenate([full, blank], axis=0))
    outs = [
        jnp.concatenate([part[:rows], part[2 * rows : 2 * rows + 1], blank[1:]], axis=0)
        for part in (even_part, odd_part)
    ]
    laid = functools.partial(laid_out, cap)
    (oe, oo), (ge, go) = outs, sums
    one_ref[...] = jnp.where(
        odd, laid((oe, 0), (oe, 1), (ge, 2), (oo, 0)), laid((ge, 0), (go, 1), (oo, 2), (go, 0))
    )
    three_ref[...] = jnp.where(
        odd, laid((oo, 3), None, (oo, 2), (oe, 3)), laid((oe, 0), (oe, 1), (oo, 0), (oe, 3))
    )
    four_ref[...] = laid((oe, 3), (oo, 3), None, (jnp.where(odd, go, ge), 3))


def matched(owned, meta_ref, gid, sources, remote_sources=()):
    values = jnp.concatenate([v for v, _ in sources], axis=1)
    ids = jnp.concatenate([i for _, i in sources], axis=1)
    number = ids.shape[1]
    own = lax.broadcasted_iota(jnp.int32, (owned, number), 0).astype(F32) + (
        meta_ref[4:5, 0:1] + 1.0
    )
    gid = jnp.where(gid > 0.0, gid, -1.0)
    match = onehot_of(jnp.concatenate([own, ids_down(gid, number)], axis=0) == ids)
    sums = exact_dot(values, match, 1)
    field, remote = sums[:, :owned], sums[:, owned:]
    if remote_sources:
        values = jnp.concatenate([v for v, _ in remote_sources], axis=1)
        ids = jnp.concatenate([i for _, i in remote_sources], axis=1)
        remote = remote + exact_dot(values, onehot_of(ids_down(gid, ids.shape[1]) == ids), 1)
    return field, remote


def first_values(owned, cap, meta_ref, offers, blocks):
    rows = COMP * NODES
    count = RUNS * cap
    lane = lax.broadcasted_iota(jnp.int32, (1, count), 1)
    odd = meta_ref[3:4, :count] == 1.0
    mine_ref, other_ref, _ = offers
    one_ref, _, far_ref, passed_ref, _ = blocks
    sources = [(r[:rows, :count], r[rows : rows + 1, :count]) for r in (*offers, *blocks)]
    owners = [
        (r[:rows, count:], r[rows : rows + 1, count:])
        for r in (other_ref, one_ref, far_ref, passed_ref)
    ]
    gid = mine_ref[rows : rows + 1, :count]
    field, remote = matched(owned, meta_ref, gid, sources, owners)
    label_rows = slice(rows, rows + 8)
    other = other_ref[label_rows, :count]
    one = one_ref[label_rows, :count]
    far = far_ref[label_rows, :count]
    passed = passed_ref[label_rows, :count]
    even_form = jnp.where(
        lane < cap,
        one,
        jnp.where(
            lane < 2 * cap, other, jnp.where(lane < 3 * cap, passed, pltpu.roll(far, 3 * cap, 1))
        ),
    )
    odd_form = jnp.where(
        lane < cap,
        pltpu.roll(passed, cap, 1),
        jnp.where(
            lane < 2 * cap, passed, jnp.where(lane < 3 * cap, other, pltpu.roll(far, 2 * cap, 1))
        ),
    )
    label = jnp.where(odd, odd_form, even_form)
    return mine_ref[:rows, count:] + field, remote, gid, label


def fused_values(owned, cap, meta_ref, own_ref, offers, blocks):
    rows = COMP * NODES
    count = RUNS * cap
    lane = lax.broadcasted_iota(jnp.int32, (1, count), 1)
    odd = meta_ref[3:4, :count] == 1.0
    sources = [(r[:rows], r[2 * rows : 2 * rows + 1]) for r in offers]
    sources += [(r[:rows], r[rows : rows + 1]) for r in blocks]
    field, remote = matched(owned, meta_ref, offers[0][2 * rows : 2 * rows + 1], sources)
    near, _, far, across, _ = (r[:rows] for r in blocks)
    partner = offers[1][rows : 2 * rows]
    even_form = jnp.where(lane < 2 * cap, across, jnp.where(lane < 3 * cap, partner, far))
    odd_form = jnp.where(
        lane < cap,
        pltpu.roll(near, cap, 1),
        jnp.where(lane < 2 * cap, partner, jnp.where(lane < 3 * cap, across, far)),
    )
    return own_ref[...] + field, jnp.where(odd, odd_form, even_form) + remote


def element_values(field, received, meta_ref, onehot_ref, forth_ref, spread_ref):
    source = jnp.concatenate([field, received], axis=1)
    kind = meta_ref[2:3, :]
    faces = by_kind(exact_dot(source, onehot_ref[...]), forth_ref, kind)
    width = spread_ref.shape[1]
    for c in range(COMP):
        for f in range(FACES):
            spread_ref[(c * FACES + f) * NODES : (c * FACES + f + 1) * NODES, :] = faces[
                c * NODES : (c + 1) * NODES, f * width : (f + 1) * width
            ]
    return kind


def apply_kernel(
    inner, trace, owned, cap, fused,
    meta_ref, onehot_ref, forth_ref, back_ref, inverse_ref, couple_ref, self_ref,
    *refs,
):
    if fused:
        gid_ref, label_ref, before_ref, *received = refs[:11]
        field_ref, *refs = refs[11:]
        gid, label = gid_ref[0:1, :], label_ref[0:1, :]
        field, received = fused_values(
            owned, cap, meta_ref, before_ref, received[:3], received[3:]
        )
    else:
        field_ref, gid_ref, label_ref, *after = refs[8:]
        field, received, gid, label = first_values(owned, cap, meta_ref, refs[:3], refs[3:8])
        refs = after
        gid_ref[...] = jnp.broadcast_to(gid, gid_ref.shape)
        label_ref[...] = label
        label = label[0:1, :]
    field_ref[...] = field
    own_ref, shared_ref, spread_ref, mid_ref, weight_ref, image_ref = refs
    width = spread_ref.shape[1]
    kind = element_values(field, received, meta_ref, onehot_ref, forth_ref, spread_ref)
    rows_times(couple_ref, spread_ref, mid_ref, inner, trace)
    rows_times(inverse_ref, mid_ref, weight_ref, inner, inner)
    rows_times(self_ref, spread_ref, image_ref, trace, trace)
    y = columns_times(tiles_of(image_ref, trace), couple_ref, weight_ref, trace, inner)
    z = by_kind(face_columns(y), back_ref, kind)
    sums = exact_dot(z, onehot_ref[...], 1)
    share(owned, sums, gid, label, meta_ref, own_ref, shared_ref)


def total(x):
    return jnp.sum(jnp.sum(x, axis=0, keepdims=True), axis=1, keepdims=True)


def last_kernel(
    inner, trace, owned, cap,
    meta_ref, onehot_ref, forth_ref, inverse_ref, couple_ref, self_ref,
    k0_ref, k1_ref, s0_ref, s1_ref, u0_ref, u1_ref, before_ref, *refs,
):
    received, refs = refs[:8], refs[8:]
    k2_ref, weight_ref, moment_ref, spread_ref, mid_ref, image_ref = refs
    width = spread_ref.shape[1]
    field, received = fused_values(
        owned, cap, meta_ref, before_ref, received[:3], received[3:]
    )
    k2_ref[...] = field
    element_values(field, received, meta_ref, onehot_ref, forth_ref, spread_ref)
    rows_times(couple_ref, spread_ref, mid_ref, inner, trace)
    rows_times(inverse_ref, mid_ref, weight_ref, inner, inner)
    rows_times(self_ref, spread_ref, image_ref, trace, trace)
    image, weight = image_ref[...], weight_ref[...]
    ks = (k0_ref[...], k1_ref[...], field)
    values = [total(ks[i] * ks[j]) for i in range(3) for j in range(i, 3)]
    for s_ref, u_ref in ((s0_ref, u0_ref), (s1_ref, u1_ref), (spread_ref, mid_ref)):
        values.append(total(s_ref[...] * image) + total(u_ref[...] * weight))
    lane = lax.broadcasted_iota(jnp.int32, (1, width), 1)
    row = jnp.zeros((1, width), F32)
    for number, value in enumerate(values):
        row = jnp.where(lane == number, value, row)
    moment_ref[...] = jnp.broadcast_to(row[None], moment_ref.shape)


def finish_kernel(
    moment_ref, k0_ref, k1_ref, k2_ref, w0_ref, w1_ref, w2_ref, load_ref, field_ref, interior_ref
):
    sums = jnp.sum(moment_ref[...], axis=0)
    m = [sums[:, n : n + 1] for n in range(9)]
    gram = [[m[0], m[1], m[2]], [m[1], m[3], m[4]], [m[2], m[4], m[5]]]
    energy = [[gram[i][1], gram[i][2], m[6 + i]] for i in range(3)]

    def form(x, matrix):
        return sum(x[i] * sum(matrix[i][j] * x[j] for j in range(3)) for i in range(3))

    zero, one = jnp.zeros((1, 1), F32), jnp.ones((1, 1), F32)
    x = [zero, zero, zero]
    r = [one, zero, zero]
    d = [one, zero, zero]
    current = gram[0][0]
    for iteration in range(3):
        step = current / form(d, energy)
        x = [x[i] + step * d[i] for i in range(3)]
        if iteration < 2:
            r = [r[0], r[1] - step * d[0], r[2] - step * d[1]]
            following = form(r, gram)
            d = [r[i] + following / current * d[i] for i in range(3)]
            current = following
    field_ref[...] = x[0] * k0_ref[...] + x[1] * k1_ref[...] + x[2] * k2_ref[...]
    interior_ref[...] = load_ref[...] - (
        x[0] * w0_ref[...] + x[1] * w1_ref[...] + x[2] * w2_ref[...]
    )


def call(kernel, outs, *args, scratch=(), in_hbm=0, vmem=8):
    inside = len(args) - in_hbm
    args = args[:inside] + tuple(
        pltpu.with_memory_space_constraint(x, pltpu.HBM) for x in args[inside:]
    )
    return pl.pallas_call(
        kernel,
        out_shape=[jax.ShapeDtypeStruct(shape, dtype) for shape, dtype in outs],
        in_specs=[pl.BlockSpec(memory_space=pltpu.VMEM)] * inside
        + [pl.BlockSpec(memory_space=pltpu.HBM)] * in_hbm,
        out_specs=[pl.BlockSpec(memory_space=pltpu.VMEM)] * len(outs),
        scratch_shapes=[pltpu.VMEM(shape, dtype) for shape, dtype in scratch]
        + [pltpu.SemaphoreType.DMA(())] * in_hbm,
        compiler_params=pltpu.CompilerParams(vmem_limit_bytes=vmem * 1024 * 1024),
    )(*args)


def fused_exchange(meta, shared, out, ranks, kernel, widths):
    pair = [(r, r ^ 1) for r in range(ranks)]

    def both_ways(chips):
        ahead = [(r, (r + 2 * chips + 1) % ranks) for r in range(0, ranks, 2)]
        return ahead + [(t, r) for r, t in ahead]

    skip = [(r, (r + (3 if r % 2 else ranks - 3)) % ranks) for r in range(ranks)]
    far = [(r, (r + ranks // 2) % ranks) for r in range(ranks)]
    second = lax.ppermute(out, AXES, skip)
    other = lax.ppermute(shared, AXES, pair)
    packed = call(
        kernel, [((COMP * NODES + 8, width), F32) for width in widths], meta, shared, other
    )
    got = [
        lax.ppermute(block, AXES, way)
        for block, way in zip(packed, (both_ways(1), both_ways(ranks // 4 - 1), far))
    ]
    if out is not shared:
        got = [*lax.optimization_barrier(tuple(got[:2])), got[2]]
    passed = [lax.ppermute(block, AXES, pair) for block in got[:2]]
    return [shared, other, second, *got, *passed]


def local(self_block, couple, inverse, body_force, face_mortar, face_kind, *, ranks):
    trace, _, elements = self_block.shape
    inner = inverse.shape[0]
    owned = 2 * elements
    cap = max(2, elements // 4)
    width = elements
    rows = COMP * NODES
    count = RUNS * cap
    forward, backward = block_tables()
    mortar = face_mortar.reshape(FACES, width)
    kind = face_kind.reshape(FACES, width)
    self_block = self_block.reshape(trace * trace, width)
    couple = couple.reshape(inner * trace, width)
    inverse = inverse.reshape(inner * inner, width)
    force = body_force.reshape(COMP * inner, width)

    offer, out, onehot, meta, load, *matrices = call(
        functools.partial(start_kernel, ranks, inner, trace, owned, cap),
        [
            ((rows + 8, count + owned), F32),
            ((rows + 8, count), F32),
            ((owned + count, FACES * width), BF16),
            ((8, FACES * width), F32),
            ((COMP * inner, width), F32),
            (inverse.shape, F32),
            (couple.shape, F32),
            (self_block.shape, F32),
        ],
        mortar, kind, force, backward, inverse, couple, self_block,
        scratch=[
            (mortar.shape, jnp.int32), (kind.shape, jnp.int32), (force.shape, F32), (backward.shape, F32)
        ],
        in_hbm=7, vmem=16,
    )
    blocks = fused_exchange(
        meta, offer, out, ranks,
        functools.partial(first_pack_kernel, owned, cap),
        (count + 2 * owned, count, count + owned),
    )
    fields, spreads, mids, weights, ids, own = [], [], [], [], [], None
    for iteration in range(2):
        fused = iteration > 0
        first = [((rows, owned), F32)] + ([] if fused else [((8, count), F32)] * 2)
        results = call(
            functools.partial(apply_kernel, inner, trace, owned, cap, fused),
            first + [
                ((rows, owned), F32),
                ((2 * rows + 8, count), F32),
                ((COMP * trace, width), F32),
                ((COMP * inner, width), F32),
                ((COMP * inner, width), F32),
            ],
            meta, onehot, forward, backward, *matrices, *([*ids, own] if fused else []), *blocks,
            scratch=[((COMP * trace, width), F32)],
        )
        fields.append(results[0])
        ids = ids or results[1 : len(first)]
        own, shared, spread, mid, weight = results[len(first) :]
        spreads.append(spread)
        mids.append(mid)
        weights.append(weight)
        blocks = fused_exchange(
            meta, shared, shared, ranks, functools.partial(pack_kernel, cap), (count,) * 3
        )
    field, weight, moments = call(
        functools.partial(last_kernel, inner, trace, owned, cap),
        [((rows, owned), F32), ((COMP * inner, width), F32), ((ranks, 1, width), F32)],
        meta, onehot, forward, *matrices, *fields, *spreads, *mids, own, *blocks,
        scratch=[
            ((COMP * trace, width), F32),
            ((COMP * inner, width), F32),
            ((COMP * trace, width), F32),
        ],
    )
    fields.append(field)
    weights.append(weight)
    moments = lax.all_to_all(moments, AXES, split_axis=0, concat_axis=0, tiled=True)
    trace_field, interior = call(
        finish_kernel,
        [((rows, owned), F32), ((COMP * inner, width), F32)],
        moments, *fields, *weights, load,
    )
    return trace_field, interior.reshape(COMP, inner, elements)


def solution(mesh):
    placed = (
        P(None, None, AXES),
        P(None, None, AXES),
        P(None, None, AXES),
        P(None, None, AXES),
        P(AXES),
        P(AXES),
    )
    ranks = int(np.prod([mesh.shape[a] for a in AXES]))
    return jax.shard_map(
        functools.partial(local, ranks=ranks),
        mesh=mesh,
        in_specs=placed,
        out_specs=(P(None, AXES), P(None, None, AXES)),
        check_vma=False,
    )
```
